32 devices in a mesh: dp: 4 (over y, core), fsdp: 8 (over z, x).
Axes of the slice: x: 2, y: 2, z: 4, core: 2. Of those that a mesh axis runs over, the one named last changes fastest.
Arguments:
- hidden_in: bfloat16 [2, 32, 128, 1024], P(None, ('dp', 'fsdp')), may hold values from -6 to 6
- memory: bfloat16 [2, 32, 588, 1024], P(None, ('dp', 'fsdp')), may hold values from -6 to 6
- cotangent: bfloat16 [2, 32, 128, 1024], P(None, ('dp', 'fsdp')), may hold values from -6 to 6
- lengths: int32 [2, 32], P(None, ('dp', 'fsdp')), may hold values from 32 to 128, as said below
- memory_count: int32 [2, 32], P(None, ('dp', 'fsdp')), may hold values from 147 to 588, as said below
- causal_gain: bfloat16 [1024], P(('dp', 'fsdp')), may hold values from 0.5 to 1.5
- causal_query: bfloat16 [1024, 1024], P(('dp', 'fsdp')), may hold values from -0.1875 to 0.1875
- causal_key: bfloat16 [1024, 1024], P(('dp', 'fsdp')), may hold values from -0.1875 to 0.1875
- causal_value: bfloat16 [1024, 1024], P(('dp', 'fsdp')), may hold values from -0.1875 to 0.1875
- causal_output: bfloat16 [1024, 1024], P(('dp', 'fsdp')), may hold values from -1.5 to 1.5
- source_gain: bfloat16 [1024], P(('dp', 'fsdp')), may hold values from 0.5 to 1.5
- source_query: bfloat16 [1024, 1024], P(('dp', 'fsdp')), may hold values from -0.1875 to 0.1875
- source_key: bfloat16 [1024, 1024], P(('dp', 'fsdp')), may hold values from -0.1875 to 0.1875
- source_value: bfloat16 [1024, 1024], P(('dp', 'fsdp')), may hold values from -0.1875 to 0.1875
- source_output: bfloat16 [1024, 1024], P(('dp', 'fsdp')), may hold values from -1.5 to 1.5
- dense_gain: bfloat16 [1024], P(('dp', 'fsdp')), may hold values from 0.5 to 1.5
- dense_expand: bfloat16 [1024, 4096], P(('dp', 'fsdp')), may hold values from -0.1875 to 0.1875
- dense_reduce: bfloat16 [4096, 1024], P(('dp', 'fsdp')), may hold values from -0.09375 to 0.09375
Outputs:
- hidden_out: bfloat16 [2, 32, 128, 1024], P(None, ('dp', 'fsdp'))
- input_gradient: float32 [2, 32, 128, 1024], P(None, ('dp', 'fsdp'))
- memory_gradient: float32 [2, 32, 588, 1024], P(None, ('dp', 'fsdp'))
- causal_gain_gradient: float32 [1024], P(('dp', 'fsdp'))
- causal_query_gradient: float32 [1024, 1024], P(('dp', 'fsdp'))
- causal_key_gradient: float32 [1024, 1024], P(('dp', 'fsdp'))
- causal_value_gradient: float32 [1024, 1024], P(('dp', 'fsdp'))
- causal_output_gradient: float32 [1024, 1024], P(('dp', 'fsdp'))
- source_gain_gradient: float32 [1024], P(('dp', 'fsdp'))
- source_query_gradient: float32 [1024, 1024], P(('dp', 'fsdp'))
- source_key_gradient: float32 [1024, 1024], P(('dp', 'fsdp'))
- source_value_gradient: float32 [1024, 1024], P(('dp', 'fsdp'))
- source_output_gradient: float32 [1024, 1024], P(('dp', 'fsdp'))
- dense_gain_gradient: float32 [1024], P(('dp', 'fsdp'))
- dense_expand_gradient: float32 [1024, 4096], P(('dp', 'fsdp'))
- dense_reduce_gradient: float32 [4096, 1024], P(('dp', 'fsdp'))
The draws below stay inside these ranges and needn't reach their ends.
Inputs may be any that keep to these rules, and one draw needn't show every extreme that they name: `lengths`: each micro-batch has a page of exactly 128 tokens. `memory_count`: each value is 147 or 588; both occur in every draw.
All inputs are finite; a program needn't handle non-finite values.
Results may differ from the reference program's by a relative error of at most 0.019.
Values may be sent and summed in bfloat16 or wider, within the bound.
A program may use at most 384 MiB of HBM per device.

```python
import jax
import jax.numpy as jnp
from jax import lax

D = 1024
FF = 4096
HD = 64
LEN = 128
MB = 2
MEM = 588
MEM_SMALL = 147
PAGES = 32


def draw_lengths(key, part):
    values = jax.random.randint(key, (MB, PAGES), LEN // 4, LEN + 1)
    places = jax.random.randint(jax.random.fold_in(key, 7), (MB,), 0, PAGES)
    full = jnp.arange(PAGES)[None, :] == places[:, None]
    return jnp.where(full, LEN, values).astype(jnp.int32)


def draw_memory_count(key, part):
    coins = jax.random.randint(key, (MB, PAGES), 0, 2)
    values = MEM_SMALL + coins * (MEM - MEM_SMALL)
    place = jax.random.randint(jax.random.fold_in(key, 11), (), 0, PAGES)
    columns = jnp.arange(PAGES)[None, :]
    first_row = jnp.arange(MB)[:, None] == 0
    values = jnp.where(first_row & (columns == place), MEM_SMALL, values)
    values = jnp.where(first_row & (columns == (place + 1) % PAGES), MEM, values)
    return values.astype(jnp.int32)


def spiked(entries, own_key, source, target, parts, factor):
    def block_of(position):
        return (jnp.arange(entries.shape[position]) // (entries.shape[position] // parts)).reshape((-1,) + (1,) * (entries.ndim - 1 - position))

    near = jax.random.permutation(own_key, parts)[block_of(target)]
    other_side = (block_of(target) + parts // 2) % parts
    return jnp.where((block_of(source) == near) | (block_of(source) == other_side), factor * entries, entries)


def shard_levels(stream_key, shape, split, smallest, high):
    def one(axis_at, parts):
        draws = jax.random.uniform(jax.random.fold_in(jax.random.fold_in(stream_key, 6), axis_at), (parts,), jnp.float32, smallest / len(split), high / len(split))
        return jnp.repeat(jnp.exp(draws), shape[axis_at] // parts).reshape((-1,) + (1,) * (len(shape) - axis_at - 1))

    factor_of = one(*split[0])
    for cut in split[1:]:
        factor_of = factor_of * one(*cut)
    return factor_of


def bell_draw(own_key, dims, scale, bound, shards=(), held_as=jnp.bfloat16):
    entries = scale * jax.random.normal(own_key, dims, jnp.float32)
    if shards:
        entries = entries * shard_levels(own_key, dims, shards, -0.22, 0.18)
    return jnp.clip(entries, -bound, bound).astype(held_as)


def bell_draw_with(rng, extent, scale, most, shards, heavy, kind=jnp.bfloat16):
    array = scale * jax.random.normal(rng, extent, jnp.float32)
    if shards:
        array = array * shard_levels(rng, extent, shards, -0.22, 0.18)
    return jnp.clip(spiked(array, jax.random.fold_in(rng, 3), *heavy), -most, most).astype(kind)


def setup_inputs(seed: int = 0) -> dict:
    key_of = jax.random.split(jax.random.key(seed), 19)
    return {
        "hidden_in": bell_draw_with(key_of[0], (MB, PAGES, LEN, D), 1.0, 6.0, ((1, 32),), (1, 3, 32, 2.75)),
        "memory": bell_draw(key_of[1], (MB, PAGES, MEM, D), 1.0, 6.0, ((1, 32),)),
        "cotangent": bell_draw_with(key_of[2], (MB, PAGES, LEN, D), 1.0, 6.0, ((1, 32),), (1, 3, 32, 2.75)),
        "lengths": draw_lengths(jax.random.fold_in(key_of[18], 71), 0),
        "memory_count": draw_memory_count(jax.random.fold_in(key_of[18], 71), 0),
        "causal_gain": jnp.clip(1.0 + 0.1 * jax.random.normal(key_of[5], (D,), jnp.float32), 0.5, 1.5).astype(jnp.bfloat16),
        "causal_query": bell_draw(key_of[6], (D, D), D ** -0.5, 0.1875, ((0, 32),)),
        "causal_key": bell_draw(key_of[7], (D, D), D ** -0.5, 0.1875, ((0, 32),)),
        "causal_value": bell_draw(key_of[8], (D, D), D ** -0.5, 0.1875, ((0, 32),)),
        "causal_output": bell_draw(key_of[9], (D, D), (D // 64) ** -0.5, 1.5, ((0, 32),)),
        "source_gain": jnp.clip(1.0 + 0.1 * jax.random.normal(key_of[10], (D,), jnp.float32), 0.5, 1.5).astype(jnp.bfloat16),
        "source_query": bell_draw(key_of[11], (D, D), D ** -0.5, 0.1875, ((0, 32),)),
        "source_key": bell_draw(key_of[12], (D, D), D ** -0.5, 0.1875, ((0, 32),)),
        "source_value": bell_draw(key_of[13], (D, D), D ** -0.5, 0.1875, ((0, 32),)),
        "source_output": bell_draw(key_of[14], (D, D), (D // 64) ** -0.5, 1.5, ((0, 32),)),
        "dense_gain": jnp.clip(1.0 + 0.1 * jax.random.normal(key_of[15], (D,), jnp.float32), 0.5, 1.5).astype(jnp.bfloat16),
        "dense_expand": bell_draw(key_of[16], (D, FF), D ** -0.5, 0.1875, ((0, 32),)),
        "dense_reduce": bell_draw(key_of[17], (FF, D), FF ** -0.5, 0.09375, ((0, 32),)),
    }


@jax.custom_vjp
def low(v):
    return lax.optimization_barrier(v.astype(jnp.bfloat16)).astype(jnp.float32)

@jax.custom_vjp
def low_back(v):
    return v

def low_keep(v):
    return (low(v), None)

def low_pass(kept, grad):
    return (grad,)

def back_keep(v):
    return (v, None)

def back_low(kept, grad):
    return (low(grad),)
low.defvjp(low_keep, low_pass)
low_back.defvjp(back_keep, back_low)
EPS = 1e-05
HIGHEST = lax.Precision.HIGHEST

def product(left, right):
    return jnp.dot(left, right, precision=HIGHEST)

def normalize(value, gain):
    centred = value - lax.optimization_barrier(jnp.mean(value, axis=-1, keepdims=True))
    spread = lax.optimization_barrier(jnp.mean(centred * centred, axis=-1, keepdims=True))
    return centred * lax.rsqrt(spread + EPS) * gain

def split_heads(value):
    return value.reshape(value.shape[0], D // HD, HD)

def attend(queries, keys, values, allowed):
    scores = jnp.einsum('qhd,khd->hqk', split_heads(queries), split_heads(keys), precision=HIGHEST) * HD ** (-0.5)
    scores = low_back(scores)
    scores = jnp.where(allowed[None], scores, -1000000000.0)
    probs = low(jax.nn.softmax(scores, axis=-1))
    context = jnp.einsum('hqk,khd->qhd', probs, split_heads(values), precision=HIGHEST)
    return context.reshape(queries.shape[0], D)

def page_layer(inputs, source, weights, length, count):
    causal_gain, causal_query, causal_key, causal_value, causal_output, source_gain, source_query, source_key, source_value, source_output, dense_gain, dense_expand, dense_reduce = weights
    places = jnp.arange(LEN)
    causal_mask = (places[None, :] <= places[:, None]) & (places[None, :] < length)
    source_mask = (jnp.arange(MEM) < count)[None, :]
    first = low(normalize(inputs, causal_gain))
    queries = low_back(low(product(first, causal_query)))
    keys = low_back(low(product(first, causal_key)))
    values = low_back(low(product(first, causal_value)))
    context = low_back(low(attend(queries, keys, values, causal_mask)))
    after_self = inputs + low_back(product(context, causal_output))
    second = low(normalize(after_self, source_gain))
    cross_queries = low_back(low(product(second, source_query)))
    memory_keys = low_back(low(product(source, source_key)))
    memory_values = low_back(low(product(source, source_value)))
    cross_context = low_back(low(attend(cross_queries, memory_keys, memory_values, source_mask)))
    after_cross = after_self + low_back(product(cross_context, source_output))
    third = low(normalize(after_cross, dense_gain))
    hidden_pre = low_back(product(third, dense_expand))
    hidden = low(jax.nn.gelu(hidden_pre, approximate=False))
    return after_cross + low_back(product(hidden, dense_reduce))

def reference(hidden_in, memory, cotangent, lengths, memory_count, causal_gain, causal_query, causal_key, causal_value, causal_output, source_gain, source_query, source_key, source_value, source_output, dense_gain, dense_expand, dense_reduce):
    weights = tuple((w.astype(jnp.float32) for w in (causal_gain, causal_query, causal_key, causal_value, causal_output, source_gain, source_query, source_key, source_value, source_output, dense_gain, dense_expand, dense_reduce)))
    inputs_all = hidden_in.reshape(MB * PAGES, LEN, D)
    source_all = memory.reshape(MB * PAGES, MEM, D)
    grads_all = cotangent.reshape(MB * PAGES, LEN, D)
    length_all = lengths.reshape(MB * PAGES).astype(jnp.int32)
    count_all = memory_count.reshape(MB * PAGES).astype(jnp.int32)

    def one_page(totals, items):
        inputs, source, grad_out, length, count = items

        def layer(x_value, m_value, w_value):
            return page_layer(x_value, m_value, w_value, length, count)
        result, pullback = jax.vjp(layer, inputs.astype(jnp.float32), source.astype(jnp.float32), weights)
        grad_x, grad_m, grad_w = pullback(grad_out.astype(jnp.float32))
        totals = jax.tree.map(lambda a, b: a + b, totals, grad_w)
        return (totals, (result.astype(jnp.bfloat16), grad_x, grad_m))
    zeros = tuple((jnp.zeros(w.shape, jnp.float32) for w in weights))
    totals, (results, grad_inputs, grad_sources) = lax.scan(one_page, zeros, (inputs_all, source_all, grads_all, length_all, count_all))
    return (results.reshape(MB, PAGES, LEN, D), grad_inputs.reshape(MB, PAGES, LEN, D), grad_sources.reshape(MB, PAGES, MEM, D), totals[0], totals[1], totals[2], totals[3], totals[4], totals[5], totals[6], totals[7], totals[8], totals[9], totals[10], totals[11], totals[12])
```

```python
import jax
import jax.numpy as jnp
from jax import lax
from jax.sharding import PartitionSpec as P

HD = 64
EPS = 1e-05
AXES = ("dp", "fsdp")
CORES = 2


class Grid:
    def __init__(self, dp, fsdp):
        self.y = dp // CORES
        self.x = self.y
        self.z = fsdp // self.x
        self.fsdp = fsdp
        self.devices = dp * fsdp
        d, f = lax.axis_index("dp"), lax.axis_index("fsdp")
        self.at = (d // CORES, d % CORES, f // self.x, f % self.x)

    def index(self, y, c, z, x):
        return (y * CORES + c) * self.fsdp + z * self.x + x

    def send(self, value, move):
        pairs = []
        for y in range(self.y):
            for c in range(CORES):
                for z in range(self.z):
                    for x in range(self.x):
                        pairs.append((self.index(y, c, z, x), self.index(*move(y, c, z, x))))
        return lax.ppermute(value, AXES, pairs)

    def send_core(self, value):
        return self.send(value, lambda y, c, z, x: (y, 1 - c, z, x))

    def send_z(self, value, k):
        return self.send(value, lambda y, c, z, x: (y, c, (z + k) % self.z, x))

    def send_plane(self, value, k, swap):
        def move(y, c, z, x):
            if (c + swap) % 2 == 0:
                return (y, c, z, (x + k) % self.x)
            return ((y + k) % self.y, c, z, x)

        return self.send(value, move)

    def place(self, a, b, core):
        y, _, _, x = self.at
        x_first = core == 0
        ky = jnp.where(x_first, b, a)
        kx = jnp.where(x_first, a, b)
        return (y + ky) % self.y, (x + kx) % self.x


def gather(grid, shard):
    r, cols = shard.shape
    z, n = grid.z, grid.x
    core = grid.at[1]
    line = [shard] + [grid.send_z(shard, k) for k in range(1, z)]
    order = [line[k] for k in range(z - 1, -1, -1)] + [line[k] for k in range(z - 1, 0, -1)]
    column = lax.dynamic_slice_in_dim(jnp.stack(order), z - 1 - grid.at[2], z, axis=0)
    pieces = {(0, 0): column}
    for a in range(1, n):
        pieces[(a, 0)] = grid.send_plane(column, a, 0)
    for a in range(n):
        for b in range(1, n):
            pieces[(a, b)] = grid.send_plane(pieces[(a, 0)], b, 1)
    out = jnp.zeros((grid.y, CORES, z, n, r, cols), shard.dtype)
    for (a, b), piece in pieces.items():
        other = grid.send_core(piece)
        for part, c in ((piece, core), (other, 1 - core)):
            yy, xx = grid.place((n - a) % n, (n - b) % n, c)
            out = lax.dynamic_update_slice(out, part[None, None, :, None], (yy, c, 0, xx, 0, 0))
    return out.reshape(grid.devices * r, cols)


def outer(left, grad):
    return lax.dot_general(left, grad, (((0,), (0,)), ((), ())), preferred_element_type=jnp.float32)


def core_columns(grid, left, c):
    width = left.shape[1] // (grid.y * CORES)
    return jnp.concatenate(
        [
            lax.dynamic_slice_in_dim(left, (y * CORES + c) * width, width, axis=1)
            for y in range(grid.y)
        ],
        axis=1,
    )


def reduce_outer(grid, left, grad):
    z, n = grid.z, grid.x
    _, core, at_z, _ = grid.at
    rows, cols = left.shape[1], grad.shape[1]
    r = rows // grid.devices
    sent = outer(core_columns(grid, left, 1 - core), grad).astype(jnp.bfloat16)
    got = grid.send_core(sent)
    mine = (outer(core_columns(grid, left, core), grad) + got.astype(jnp.float32)).astype(jnp.bfloat16)
    mine = mine.reshape(grid.y, z, n, r, cols)

    def piece(a, b):
        yy, xx = grid.place(a, b, core)
        return lax.dynamic_slice(mine, (yy, 0, xx, 0, 0), (1, z, 1, r, cols)).reshape(z, r, cols)

    kept = []
    for b in range(n):
        total = piece(0, b).astype(jnp.float32)
        for a in range(1, n):
            total = total + grid.send_plane(piece(a, b), a, 0).astype(jnp.float32)
        kept.append(total.astype(jnp.bfloat16))
    total = kept[0].astype(jnp.float32)
    for b in range(1, n):
        total = total + grid.send_plane(kept[b], b, 1).astype(jnp.float32)
    column = total.astype(jnp.bfloat16)

    def block(k):
        return lax.dynamic_index_in_dim(column, (at_z + k) % z, axis=0, keepdims=False)

    total = block(0).astype(jnp.float32)
    for k in range(1, z):
        total = total + grid.send_z(block(k), k).astype(jnp.float32)
    return total


def reduce_gains(grid, gains):
    z, n = grid.z, grid.x
    total = gains + grid.send_core(gains)
    for swap in (0, 1):
        total = sum((grid.send_plane(total, a, swap) for a in range(1, n)), total)
    total = sum((grid.send_z(total, k) for k in range(1, z)), total)
    width = gains.shape[1] // grid.devices
    y, c, zz, x = grid.at
    return lax.dynamic_slice_in_dim(total, grid.index(y, c, zz, x) * width, width, axis=1)


def split_heads(value):
    return value.reshape(value.shape[0], value.shape[1], -1, HD)


def project(left, weight):
    return jnp.einsum("bld,de->ble", left, weight, preferred_element_type=jnp.float32)


def project_back(grad, weight):
    return jnp.einsum("ble,de->bld", grad, weight, preferred_element_type=jnp.float32)


def normalize(value, gain):
    centred = value - jnp.mean(value, axis=-1, keepdims=True)
    spread = jnp.mean(centred * centred, axis=-1, keepdims=True)
    scale_row = lax.rsqrt(spread + EPS)
    unit = centred * scale_row
    return (unit * gain, unit, scale_row)


def normalize_back(grad, unit, scale_row, gain):
    grad_unit = grad * gain
    grad_gain = jnp.sum(grad * unit, axis=(0, 1))
    centred = grad_unit - jnp.mean(grad_unit, axis=-1, keepdims=True)
    grad_input = scale_row * (centred - unit * jnp.mean(grad_unit * unit, axis=-1, keepdims=True))
    return (grad_input, grad_gain)


def masked_scores(queries, keys, allowed):
    scores = jnp.einsum(
        "bqhd,bkhd->bhqk",
        split_heads(queries),
        split_heads(keys),
        preferred_element_type=jnp.float32,
    ) * HD ** (-0.5)
    return jnp.where(allowed[:, None], scores, -1000000000.0)


def attend(queries, keys, values, allowed):
    scores = masked_scores(queries, keys, allowed)
    top = jnp.max(scores, axis=-1, keepdims=True)
    expos = jnp.exp(scores - top)
    total = jnp.sum(expos, axis=-1, keepdims=True)
    probs = (expos / total).astype(jnp.bfloat16)
    context = jnp.einsum(
        "bhqk,bkhd->bqhd", probs, split_heads(values), preferred_element_type=jnp.float32
    )
    return (context.reshape(queries.shape).astype(jnp.bfloat16), top + jnp.log(total))


def attend_back(queries, keys, values, allowed, logsum, grad_context):
    probs = jnp.exp(masked_scores(queries, keys, allowed) - logsum)
    grad_heads = split_heads(grad_context)
    grad_values = jnp.einsum(
        "bhqk,bqhd->bkhd",
        probs.astype(jnp.bfloat16),
        grad_heads,
        preferred_element_type=jnp.float32,
    )
    grad_probs = jnp.einsum(
        "bqhd,bkhd->bhqk", grad_heads, split_heads(values), preferred_element_type=jnp.float32
    )
    inner = jnp.sum(probs * grad_probs, axis=-1, keepdims=True)
    grad_scores = (probs * (grad_probs - inner)).astype(jnp.bfloat16)
    scale = HD ** (-0.5)
    grad_queries = (
        jnp.einsum(
            "bhqk,bkhd->bqhd", grad_scores, split_heads(keys), preferred_element_type=jnp.float32
        )
        * scale
    )
    grad_keys = (
        jnp.einsum(
            "bhqk,bqhd->bkhd", grad_scores, split_heads(queries), preferred_element_type=jnp.float32
        )
        * scale
    )
    return (
        grad_queries.reshape(queries.shape).astype(jnp.bfloat16),
        grad_keys.reshape(keys.shape).astype(jnp.bfloat16),
        grad_values.reshape(values.shape).astype(jnp.bfloat16),
    )


def per_device(
    hidden_in,
    memory,
    cotangent,
    lengths,
    memory_count,
    causal_gain,
    causal_query,
    causal_key,
    causal_value,
    causal_output,
    source_gain,
    source_query,
    source_key,
    source_value,
    source_output,
    dense_gain,
    dense_expand,
    dense_reduce,
):
    grid = Grid(lax.axis_size("dp"), lax.axis_size("fsdp"))
    inputs = hidden_in[:, 0].astype(jnp.float32)
    source = memory[:, 0]
    page_length = lengths[:, 0]
    page_count = memory_count[:, 0]
    pages, rows, width = inputs.shape
    slots = source.shape[1]
    places = jnp.arange(rows)
    causal_mask = (places[None, None, :] <= places[None, :, None]) & (
        places[None, None, :] < page_length[:, None, None]
    )
    source_mask = jnp.arange(slots)[None, None, :] < page_count[:, None, None]

    def flat(value):
        return value.reshape(pages * value.shape[1], value.shape[2])

    gains = jnp.stack([causal_gain, source_gain, dense_gain], axis=1)
    gains = jnp.pad(gains, ((0, 0), (0, 125)))
    kv_weight = gather(grid, jnp.concatenate([source_key, source_value], axis=1))
    self_weight = gather(
        grid,
        jnp.concatenate([causal_query, causal_key, causal_value, causal_output, gains], axis=1),
    )
    qo_weight = gather(grid, jnp.concatenate([source_query, source_output], axis=1))
    expand_weight = gather(grid, dense_expand)
    reduce_weight = gather(grid, dense_reduce)
    gain_rows = self_weight[:, 4 * width : 4 * width + 3].T.astype(jnp.float32)
    gain_one, gain_two, gain_three = gain_rows[0], gain_rows[1], gain_rows[2]
    qkv_weight = self_weight[:, : 3 * width]
    out_weight = self_weight[:, 3 * width : 4 * width]
    source_query_weight, source_out_weight = qo_weight[:, :width], qo_weight[:, width:]

    memory_both = project(source, kv_weight).astype(jnp.bfloat16)
    memory_keys, memory_values = memory_both[..., :width], memory_both[..., width:]
    normed, unit_one, scale_one = normalize(inputs, gain_one)
    first = normed.astype(jnp.bfloat16)
    qkv = project(first, qkv_weight).astype(jnp.bfloat16)
    queries, keys, values = (qkv[..., i * width : (i + 1) * width] for i in range(3))
    context, logsum_self = attend(queries, keys, values, causal_mask)
    after_self = inputs + project(context, out_weight)
    normed, unit_two, scale_two = normalize(after_self, gain_two)
    second = normed.astype(jnp.bfloat16)
    cross_queries = project(second, source_query_weight).astype(jnp.bfloat16)
    cross_context, logsum_cross = attend(cross_queries, memory_keys, memory_values, source_mask)
    after_cross = after_self + project(cross_context, source_out_weight)
    normed, unit_three, scale_three = normalize(after_cross, gain_three)
    third = normed.astype(jnp.bfloat16)
    hidden_pre = project(third, expand_weight)
    hidden = jax.nn.gelu(hidden_pre, approximate=False).astype(jnp.bfloat16)
    result = after_cross + project(hidden, reduce_weight)

    grad_out = cotangent[:, 0].astype(jnp.float32)
    grad_branch = grad_out.astype(jnp.bfloat16)
    grad_reduce = reduce_outer(grid, flat(hidden), flat(grad_branch))
    grad_hidden = project_back(grad_branch, reduce_weight)
    _, gelu_pull = jax.vjp(lambda v: jax.nn.gelu(v, approximate=False), hidden_pre)
    grad_pre = gelu_pull(grad_hidden)[0].astype(jnp.bfloat16)
    grad_expand = reduce_outer(grid, flat(third), flat(grad_pre))
    grad_norm, grad_gain_three = normalize_back(
        project_back(grad_pre, expand_weight), unit_three, scale_three, gain_three
    )
    grad_cross = grad_out + grad_norm

    grad_branch = grad_cross.astype(jnp.bfloat16)
    grad_source_output = reduce_outer(grid, flat(cross_context), flat(grad_branch))
    grad_context = project_back(grad_branch, source_out_weight).astype(jnp.bfloat16)
    grad_cq, grad_mk, grad_mv = attend_back(
        cross_queries, memory_keys, memory_values, source_mask, logsum_cross, grad_context
    )
    grad_both = jnp.concatenate([grad_mk, grad_mv], axis=-1)
    grad_source_query = reduce_outer(grid, flat(second), flat(grad_cq))
    grad_source_both = reduce_outer(grid, flat(source), flat(grad_both))
    grad_memory = project_back(grad_both, kv_weight)
    grad_norm, grad_gain_two = normalize_back(
        project_back(grad_cq, source_query_weight), unit_two, scale_two, gain_two
    )
    grad_self = grad_cross + grad_norm

    grad_branch = grad_self.astype(jnp.bfloat16)
    grad_causal_output = reduce_outer(grid, flat(context), flat(grad_branch))
    grad_context = project_back(grad_branch, out_weight).astype(jnp.bfloat16)
    grad_q, grad_k, grad_v = attend_back(
        queries, keys, values, causal_mask, logsum_self, grad_context
    )
    grad_qkv = jnp.concatenate([grad_q, grad_k, grad_v], axis=-1)
    grad_causal = reduce_outer(grid, flat(first), flat(grad_qkv))
    grad_norm, grad_gain_one = normalize_back(
        project_back(grad_qkv, qkv_weight), unit_one, scale_one, gain_one
    )
    grad_inputs = grad_self + grad_norm
    grad_gains = reduce_gains(grid, jnp.stack([grad_gain_one, grad_gain_two, grad_gain_three]))
    return (
        result.astype(jnp.bfloat16)[:, None],
        grad_inputs[:, None],
        grad_memory[:, None],
        grad_gains[0],
        grad_causal[:, :width],
        grad_causal[:, width : 2 * width],
        grad_causal[:, 2 * width :],
        grad_causal_output,
        grad_gains[1],
        grad_source_query,
        grad_source_both[:, :width],
        grad_source_both[:, width:],
        grad_source_output,
        grad_gains[2],
        grad_expand,
        grad_reduce,
    )


def solution(mesh):
    pages = P(None, AXES, None, None)
    counts = P(None, AXES)
    gain = P(AXES)
    weight = P(AXES, None)
    return jax.shard_map(
        per_device,
        mesh=mesh,
        in_specs=(pages, pages, pages, counts, counts)
        + (gain, weight, weight, weight, weight)
        + (gain, weight, weight, weight, weight)
        + (gain, weight, weight),
        out_specs=(pages, pages, pages)
        + (gain, weight, weight, weight, weight)
        + (gain, weight, weight, weight, weight)
        + (gain, weight, weight),
        check_vma=False,
    )
```

```python
import functools

import jax
import jax.numpy as jnp
from jax import lax
from jax.experimental import pallas as pl
from jax.experimental.pallas import tpu as pltpu
from jax.sharding import PartitionSpec as P

HD = 64
EPS = 1e-05
AXES = ("dp", "fsdp")
CORES = 2
WIDTH = 1024
MESH = pl.DeviceIdType.MESH


class Grid:
    def __init__(self):
        dp, fsdp = lax.axis_size("dp"), lax.axis_size("fsdp")
        self.n = dp // CORES
        self.depth = fsdp // self.n
        self.devices = dp * fsdp
        d, f = lax.axis_index("dp"), lax.axis_index("fsdp")
        self.at = (d // CORES, d % CORES, f // self.n, f % self.n)

    def device(self, y, c, z, x):
        return (y * CORES + c, z * self.n + x)

    def step_z(self, k):
        y, c, z, x = self.at
        return self.device(y, c, lax.rem(z + k, self.depth), x)

    def step_plane(self, k, swap):
        y, c, z, x = self.at
        odd = lax.rem(c + swap, 2)
        return self.device(
            lax.rem(y + k * odd, self.n), c, z, lax.rem(x + k * (1 - odd), self.n)
        )

    def partner(self):
        y, c, z, x = self.at
        return self.device(y, 1 - c, z, x)

    def place(self, a, b):
        y, c, z, x = self.at
        ky = a * c + b * (1 - c)
        kx = a * (1 - c) + b * c
        return lax.rem(y + ky, self.n), lax.rem(x + kx, self.n)

    def peers(self):
        line = [self.step_z(k) for k in range(1, self.depth)]
        plane = [self.step_plane(k, s) for s in (0, 1) for k in range(1, self.n)]
        return line + plane + [self.partner()]

    def meet(self):
        barrier = pltpu.get_barrier_semaphore()
        peers = self.peers()
        for peer in peers:
            pl.semaphore_signal(barrier, inc=1, device_id=peer, device_id_type=MESH)
        pl.semaphore_wait(barrier, len(peers))


def remote(src, dst, send_sem, recv_sem, device):
    return pltpu.make_async_remote_copy(
        src_ref=src,
        dst_ref=dst,
        send_sem=send_sem,
        recv_sem=recv_sem,
        device_id=device,
        device_id_type=MESH,
    )


def started(*copy):
    made = remote(*copy)
    made.start()
    return made


class Plan:
    def __init__(self):
        self.calls = {}

    def add(self, tick, rank, call, *args):
        self.calls.setdefault((tick, rank), []).append((call, args))

    def run(self):
        for key in sorted(self.calls):
            for call, args in self.calls[key]:
                call(*args)


def gather_kernel(chunks, count, *refs):
    grid = Grid()
    n, depth = grid.n, grid.depth
    shards, outs = refs[:count], refs[count : 2 * count]
    local, zs, zr, ps, pr, qs, qr, cs, cr, us, ur, ds, dr = refs[2 * count :]
    y, c, z, x = grid.at
    grid.meet()
    pending = []

    def send(*copy):
        made = started(*copy)
        pending.append(made)
        return made

    def window(i):
        _, r0, nr, c0, nc, _ = chunks[i]
        return pl.ds(r0, nr), pl.ds(c0, nc)

    def shard(i):
        return shards[chunks[i][0]].at[window(i)]

    def block(i, yy, zz, xx):
        return outs[chunks[i][0]].at[(yy, c, zz, xx) + window(i)]

    def back(a, b):
        return grid.place((n - a) % n, (n - b) % n)

    def column(i, a, b):
        yy, xx = back(a, b)
        return outs[chunks[i][0]].at[(yy, c, slice(None), xx) + window(i)]

    def share(i, a, b):
        piece = column(i, a, b)
        slot = a * n + b
        return send(piece, piece, cs.at[i, slot], cr.at[i, slot], grid.partner())

    zc, pc, qc, cc, lc = {}, {}, {}, {}, {}

    def keep_own(i):
        lc[i] = pltpu.make_async_copy(shard(i), block(i, y, z, x), local.at[i])
        lc[i].start()

    def stage_z(i):
        zc[i] = [
            send(shard(i), block(i, y, z, x), zs.at[i, k - 1], zr.at[i, k - 1], grid.step_z(k))
            for k in range(1, depth)
        ]
        keep_own(i)

    def stage_p(i):
        for copy in zc[i]:
            copy.wait_recv()
        lc[i].wait()
        piece = column(i, 0, 0)
        pc[i] = [
            send(piece, piece, ps.at[i, a - 1], pr.at[i, a - 1], grid.step_plane(a, 0))
            for a in range(1, n)
        ]
        qc[i] = [
            send(piece, piece, qs.at[i, b - 1], qr.at[i, b - 1], grid.step_plane(b, 1))
            for b in range(1, n)
        ]
        cc[i] = [share(i, 0, 0)]

    def stage_q(i):
        for a in range(1, n):
            pc[i][a - 1].wait_recv()
            piece = column(i, a, 0)
            for b in range(1, n):
                j = a * (n - 1) + b - 1
                qc[i].append(
                    send(piece, piece, qs.at[i, j], qr.at[i, j], grid.step_plane(b, 1))
                )
            cc[i].append(share(i, a, 0))

    def stage_c(i):
        j = 0
        for a in range(n):
            for b in range(1, n):
                qc[i][j].wait_recv()
                j += 1
                cc[i].append(share(i, a, b))

    def tall_p(i):
        keep_own(i)
        pc[i] = [
            send(shard(i), block(i, y, z, x), ps.at[i, a - 1], pr.at[i, a - 1], grid.step_plane(a, 0))
            for a in range(1, n)
        ]

    def tall_q(i):
        lc[i].wait()
        qc[i] = []
        for a in range(n):
            if a:
                pc[i][a - 1].wait_recv()
            yy, xx = back(a, 0)
            piece = block(i, yy, z, xx)
            for b in range(1, n):
                j = a * (n - 1) + b - 1
                qc[i].append(
                    send(piece, piece, qs.at[i, j], qr.at[i, j], grid.step_plane(b, 1))
                )

    def layer(i, k, j):
        zz = lax.rem(z + (depth - j if k == 0 else j), depth)
        return outs[chunks[i][0]].at[(slice(None), c, zz, slice(None)) + window(i)]

    def hop(i, k, j):
        piece = layer(i, k, j)
        send_sem, recv_sem = ((us, ur), (ds, dr))[k]
        to = grid.device(y, c, lax.rem(z + (1 if k == 0 else depth - 1), depth), x)
        return remote(piece, piece, send_sem.at[i, j], recv_sem.at[i, j], to)

    def share_layer(i, k, j):
        piece = layer(i, k, j)
        slot = k * (depth - 1) + j
        return remote(piece, piece, cs.at[i, slot], cr.at[i, slot], grid.partner())

    def level(k):
        return z if k == 0 else depth - 1 - z

    def climb(i, j):
        if j == 0:
            for copy in qc[i]:
                copy.wait_recv()
            share_layer(i, 0, 0).start()
        for k in (0, 1):
            if j:

                @pl.when(level(k) >= j)
                def _():
                    hop(i, k, j - 1).wait_recv()
                    share_layer(i, k, j).start()

            if j < depth - 1:

                @pl.when((level(k) >= j) & (level(k) < depth - 1))
                def _():
                    hop(i, k, j).start()

    def finish_tall(i):
        share_layer(i, 0, 0).wait()
        for k in (0, 1):
            for j in range(depth - 1):

                @pl.when((level(k) >= j) & (level(k) < depth - 1))
                def _():
                    hop(i, k, j).wait_send()

                @pl.when(level(k) >= j + 1)
                def _():
                    share_layer(i, k, j + 1).wait()

    plan = Plan()
    flat = [i for i, chunk in enumerate(chunks) if not chunk[5]]
    tall = [i for i, chunk in enumerate(chunks) if chunk[5]]
    for t, i in enumerate(flat):
        plan.add(t - 2, 0, stage_z, i)
        plan.add(t, 2, stage_p, i)
        plan.add(t + 1, 4, stage_q, i)
        plan.add(t + 2, 6, stage_c, i)
    for t, i in enumerate(tall):
        t = 3 * t - 1
        plan.add(t, 1, tall_p, i)
        plan.add(t + 2, 3, tall_q, i)
        for h in range(depth):
            plan.add(t + 4 + 2 * h, 5, climb, i, h)
    plan.run()
    for i in flat:
        for copy in cc[i]:
            copy.wait_recv()
    for i in tall:
        finish_tall(i)
    for copy in pending:
        copy.wait_send()


def gather_all(shards, tall):
    dp, fsdp = lax.axis_size("dp"), lax.axis_size("fsdp")
    n = dp // CORES
    depth = fsdp // n
    rows = shards[0].shape[0]
    chunks = []
    for m, shard in enumerate(shards):
        r, cols = shard.shape
        for r0 in range(0, r, rows):
            for c0 in range(0, cols // WIDTH * WIDTH, WIDTH):
                nc = WIDTH if c0 + 2 * WIDTH <= cols else cols - c0
                chunks.append((m, r0, rows, c0, nc, len(chunks) in tall))
    t = len(chunks)
    slots = max(n * n, 2 * depth - 1)
    shapes = (1, depth - 1, depth - 1, n - 1, n - 1, n * (n - 1), n * (n - 1), slots, slots)
    shapes += (depth - 1,) * 4
    dma = pltpu.SemaphoreType.DMA
    outs = pl.pallas_call(
        functools.partial(gather_kernel, chunks, len(shards)),
        out_shape=[
            jax.ShapeDtypeStruct((n, CORES, depth, n) + s.shape, s.dtype) for s in shards
        ],
        in_specs=[pl.BlockSpec(memory_space=pltpu.VMEM)] * len(shards),
        out_specs=[pl.BlockSpec(memory_space=pltpu.HBM)] * len(shards),
        scratch_shapes=[dma((t,))] + [dma((t, k)) for k in shapes[1:]],
        compiler_params=pltpu.CompilerParams(collective_id=0, has_side_effects=True),
    )(*shards)
    return [o.reshape(dp * fsdp * s.shape[0], s.shape[1]) for o, s in zip(outs, shards)]


RING = 4


def reduce_kernel(chunks, count, *refs):
    grid = Grid()
    n, depth = grid.n, grid.depth
    y, c, z, x = grid.at
    parts, gain_in = refs[:count], refs[count]
    outs, gain_out = refs[count + 1 : 2 * count + 1], refs[2 * count + 1]
    (own, got0, send1, got1, keep1, send2, got2, keep2, line, got3, gain_sum, gain_got) = refs[
        2 * count + 2 : 2 * count + 14
    ]
    local, s0, r0, s1, r1, s2, r2, s3, r3, gs, gr = refs[2 * count + 14 :]
    rows, width = own.shape[-2:]
    total = len(chunks)
    f32, bf16 = jnp.float32, jnp.bfloat16
    grid.meet()
    copies = {}

    def half(i, core):
        m, row, col = chunks[i]
        return parts[m].at[:, core, :, :, pl.ds(row, rows), pl.ds(col, width)]

    def reuse(i, stage):
        if i >= RING:
            for copy in copies[i - RING, stage]:
                copy.wait_send()

    def load(i):
        copies[i, "own"] = pltpu.make_async_copy(half(i, c), own.at[i % RING], local.at[i % RING])
        copies[i, "own"].start()

    def stage0(i):
        copies[i, 0] = [
            started(half(i, 1 - c), got0.at[i], s0.at[i], r0.at[i], grid.partner())
        ]

    def stage1(i):
        s = i % RING
        reuse(i, 1)
        copies[i, "own"].wait()
        copies[i, 0][0].wait_recv()

        def add(dst, a, b):
            yy, xx = grid.place(a, b)

            def body(zz, carry):
                total_ = own[s, yy, zz, xx].astype(f32) + got0[i, yy, zz, xx].astype(f32)
                dst[zz] = total_.astype(bf16)
                return carry

            lax.fori_loop(0, depth, body, 0)

        copies[i, 1] = []
        for a in range(1, n):
            for b in range(n):
                add(send1.at[s, a - 1, b], a, b)
            copies[i, 1].append(
                started(
                    send1.at[s, a - 1],
                    got1.at[i, a - 1],
                    s1.at[s, a - 1],
                    r1.at[i, a - 1],
                    grid.step_plane(a, 0),
                )
            )
        for b in range(n):
            add(keep1.at[s, b], 0, b)
        if i + RING < total:
            load(i + RING)

    def stage2(i):
        s = i % RING
        reuse(i, 2)
        for copy in copies[i, 1]:
            copy.wait_recv()
        copies[i, 2] = []
        for b in list(range(1, n)) + [0]:
            dst = send2.at[s, b - 1] if b else keep2.at[s]

            def body(zz, carry):
                total_ = keep1[s, b, zz].astype(f32)
                for a in range(1, n):
                    total_ = total_ + got1[i, a - 1, b, zz].astype(f32)
                dst[zz] = total_.astype(bf16)
                return carry

            lax.fori_loop(0, depth, body, 0)
            if b:
                copies[i, 2].append(
                    started(
                        send2.at[s, b - 1],
                        got2.at[i, b - 1],
                        s2.at[s, b - 1],
                        r2.at[i, b - 1],
                        grid.step_plane(b, 1),
                    )
                )

    def stage3(i):
        s = i % RING
        reuse(i, 3)
        for copy in copies[i, 2]:
            copy.wait_recv()

        def body(zz, carry):
            total_ = keep2[s, zz].astype(f32)
            for b in range(1, n):
                total_ = total_ + got2[i, b - 1, zz].astype(f32)
            line[s, zz] = total_.astype(bf16)
            return carry

        lax.fori_loop(0, depth, body, 0)
        copies[i, 3] = [
            started(
                line.at[s, lax.rem(z + k, depth)],
                got3.at[i, k - 1],
                s3.at[s, k - 1],
                r3.at[i, k - 1],
                grid.step_z(k),
            )
            for k in range(1, depth)
        ]

    def stage4(i):
        m, row, col = chunks[i]
        for copy in copies[i, 3]:
            copy.wait_recv()
        total_ = line[i % RING, z].astype(f32)
        for k in range(1, depth):
            total_ = total_ + got3[i, k - 1].astype(f32)
        outs[m][pl.ds(row, rows), pl.ds(col, width)] = total_

    moves = [
        [grid.partner()],
        [grid.step_plane(a, 0) for a in range(1, n)],
        [grid.step_plane(a, 1) for a in range(1, n)],
        [grid.step_z(k) for k in range(1, depth)],
        [],
    ]
    first = [0, 1, n, 2 * n - 1, 2 * n + depth - 2]

    def gain_step(h):
        total_ = gain_in[...]
        if h:
            total_ = gain_sum[h - 1]
            for j, copy in enumerate(copies["gain", h - 1]):
                copy.wait_recv()
                total_ = total_ + gain_got[first[h - 1] + j]
        if h == len(moves) - 1:
            gain_out[...] = total_
        else:
            gain_sum[h] = total_
        copies["gain", h] = [
            started(
                gain_sum.at[h],
                gain_got.at[first[h] + j],
                gs.at[first[h] + j],
                gr.at[first[h] + j],
                device,
            )
            for j, device in enumerate(moves[h])
        ]

    plan = Plan()
    for i in range(total):
        plan.add(i - 2, 0, stage0, i)
        plan.add(i, 1, stage1, i)
        plan.add(i + 1, 2, stage2, i)
        plan.add(i + 2, 3, stage3, i)
        plan.add(i + 3, 4, stage4, i)
    for h in range(len(moves)):
        plan.add(total - 4 + h, 5, gain_step, h)
    for i in range(min(RING, total)):
        load(i)
    plan.run()
    for i in range(total):
        copies[i, 0][0].wait_send()
        if i >= total - RING:
            for stage in (1, 2, 3):
                for copy in copies[i, stage]:
                    copy.wait_send()
    for h in range(len(moves)):
        for copy in copies["gain", h]:
            copy.wait_send()


def reduce_all(parts, gains):
    dp, fsdp = lax.axis_size("dp"), lax.axis_size("fsdp")
    n = dp // CORES
    depth = fsdp // n
    devices = dp * fsdp
    rows = WIDTH // devices
    chunks = []
    for m, part in enumerate(parts):
        for row in range(0, part.shape[0] // devices, rows):
            for col in range(0, part.shape[1], WIDTH):
                chunks.append((m, row, col))
    t = len(chunks)
    dma = pltpu.SemaphoreType.DMA
    hops = 2 * n + depth - 2

    def scratch(*lead):
        return pltpu.VMEM(lead + (rows, WIDTH), jnp.bfloat16)

    views = [p.reshape(n, CORES, depth, n, p.shape[0] // devices, p.shape[1]) for p in parts]
    return pl.pallas_call(
        functools.partial(reduce_kernel, chunks, len(parts)),
        out_shape=[
            jax.ShapeDtypeStruct((p.shape[0] // devices, p.shape[1]), jnp.float32) for p in parts
        ]
        + [jax.ShapeDtypeStruct(gains.shape, jnp.float32)],
        in_specs=[pl.BlockSpec(memory_space=pltpu.HBM)] * len(parts)
        + [pl.BlockSpec(memory_space=pltpu.VMEM)],
        out_specs=[pl.BlockSpec(memory_space=pltpu.VMEM)] * (len(parts) + 1),
        scratch_shapes=[
            scratch(RING, n, depth, n),
            scratch(t, n, depth, n),
            scratch(RING, n - 1, n, depth),
            scratch(t, n - 1, n, depth),
            scratch(RING, n, depth),
            scratch(RING, n - 1, depth),
            scratch(t, n - 1, depth),
            scratch(RING, depth),
            scratch(RING, depth),
            scratch(t, depth - 1),
            pltpu.VMEM((4,) + gains.shape, jnp.float32),
            pltpu.VMEM((hops,) + gains.shape, jnp.float32),
            dma((RING,)),
            dma((t,)),
            dma((t,)),
            dma((RING, n - 1)),
            dma((t, n - 1)),
            dma((RING, n - 1)),
            dma((t, n - 1)),
            dma((RING, depth - 1)),
            dma((t, depth - 1)),
            dma((hops,)),
            dma((hops,)),
        ],
        compiler_params=pltpu.CompilerParams(
            collective_id=1, has_side_effects=True, vmem_limit_bytes=60 << 20
        ),
    )(*views, gains)


def outer(left, grad):
    total = lax.dot_general(left, grad, (((0,), (0,)), ((), ())), preferred_element_type=jnp.float32)
    return total.astype(jnp.bfloat16)


def split_heads(value):
    return value.reshape(value.shape[0], value.shape[1], -1, HD)


def project(left, weight):
    return jnp.einsum("bld,de->ble", left, weight, preferred_element_type=jnp.float32)


def project_back(grad, weight):
    return jnp.einsum("ble,de->bld", grad, weight, preferred_element_type=jnp.float32)


def normalize(value, gain):
    centred = value - jnp.mean(value, axis=-1, keepdims=True)
    spread = jnp.mean(centred * centred, axis=-1, keepdims=True)
    scale_row = lax.rsqrt(spread + EPS)
    unit = centred * scale_row
    return (unit * gain, unit, scale_row)


def normalize_back(grad, unit, scale_row, gain):
    grad_unit = grad * gain
    grad_gain = jnp.sum(grad * unit, axis=(0, 1))
    centred = grad_unit - jnp.mean(grad_unit, axis=-1, keepdims=True)
    grad_input = scale_row * (centred - unit * jnp.mean(grad_unit * unit, axis=-1, keepdims=True))
    return (grad_input, grad_gain)


def masked_scores(queries, keys, allowed):
    scores = jnp.einsum(
        "bqhd,bkhd->bhqk",
        split_heads(queries),
        split_heads(keys),
        preferred_element_type=jnp.float32,
    ) * HD ** (-0.5)
    return jnp.where(allowed[:, None], scores, -1000000000.0)


def attend(queries, keys, values, allowed):
    scores = masked_scores(queries, keys, allowed)
    top = jnp.max(scores, axis=-1, keepdims=True)
    expos = jnp.exp(scores - top)
    total = jnp.sum(expos, axis=-1, keepdims=True)
    probs = (expos / total).astype(jnp.bfloat16)
    context = jnp.einsum(
        "bhqk,bkhd->bqhd", probs, split_heads(values), preferred_element_type=jnp.float32
    )
    return (context.reshape(queries.shape).astype(jnp.bfloat16), top + jnp.log(total))


def attend_back(queries, keys, values, allowed, logsum, grad_context):
    probs = jnp.exp(masked_scores(queries, keys, allowed) - logsum)
    grad_heads = split_heads(grad_context)
    grad_values = jnp.einsum(
        "bhqk,bqhd->bkhd",
        probs.astype(jnp.bfloat16),
        grad_heads,
        preferred_element_type=jnp.float32,
    )
    grad_probs = jnp.einsum(
        "bqhd,bkhd->bhqk", grad_heads, split_heads(values), preferred_element_type=jnp.float32
    )
    inner = jnp.sum(probs * grad_probs, axis=-1, keepdims=True)
    grad_scores = (probs * (grad_probs - inner)).astype(jnp.bfloat16)
    scale = HD ** (-0.5)
    grad_queries = (
        jnp.einsum(
            "bhqk,bkhd->bqhd", grad_scores, split_heads(keys), preferred_element_type=jnp.float32
        )
        * scale
    )
    grad_keys = (
        jnp.einsum(
            "bhqk,bqhd->bkhd", grad_scores, split_heads(queries), preferred_element_type=jnp.float32
        )
        * scale
    )
    return (
        grad_queries.reshape(queries.shape).astype(jnp.bfloat16),
        grad_keys.reshape(keys.shape).astype(jnp.bfloat16),
        grad_values.reshape(values.shape).astype(jnp.bfloat16),
    )


def per_device(
    hidden_in,
    memory,
    cotangent,
    lengths,
    memory_count,
    causal_gain,
    causal_query,
    causal_key,
    causal_value,
    causal_output,
    source_gain,
    source_query,
    source_key,
    source_value,
    source_output,
    dense_gain,
    dense_expand,
    dense_reduce,
):
    inputs = hidden_in[:, 0].astype(jnp.float32)
    source = memory[:, 0]
    page_length = lengths[:, 0]
    page_count = memory_count[:, 0]
    pages, rows, width = inputs.shape
    slots = source.shape[1]
    places = jnp.arange(rows)
    causal_mask = (places[None, None, :] <= places[None, :, None]) & (
        places[None, None, :] < page_length[:, None, None]
    )
    source_mask = jnp.arange(slots)[None, None, :] < page_count[:, None, None]

    def flat(value):
        return value.reshape(pages * value.shape[1], value.shape[2])

    gains = jnp.stack([causal_gain, source_gain, dense_gain], axis=1)
    gains = jnp.pad(gains, ((0, 0), (0, 125)))
    kv_weight, self_weight, qo_weight, expand_weight, reduce_weight = gather_all(
        [
            jnp.concatenate([source_key, source_value], axis=1),
            jnp.concatenate([causal_query, causal_key, causal_value, causal_output, gains], axis=1),
            jnp.concatenate([source_query, source_output], axis=1),
            dense_expand,
            dense_reduce,
        ],
        (1, 5, 9),
    )
    gain_rows = self_weight[:, 4 * width : 4 * width + 3].T.astype(jnp.float32)
    gain_one, gain_two, gain_three = gain_rows[0], gain_rows[1], gain_rows[2]
    qkv_weight = self_weight[:, : 3 * width]
    out_weight = self_weight[:, 3 * width : 4 * width]
    source_query_weight, source_out_weight = qo_weight[:, :width], qo_weight[:, width:]

    memory_both = project(source, kv_weight).astype(jnp.bfloat16)
    memory_keys, memory_values = memory_both[..., :width], memory_both[..., width:]
    normed, unit_one, scale_one = normalize(inputs, gain_one)
    first = normed.astype(jnp.bfloat16)
    qkv = project(first, qkv_weight).astype(jnp.bfloat16)
    queries, keys, values = (qkv[..., i * width : (i + 1) * width] for i in range(3))
    context, logsum_self = attend(queries, keys, values, causal_mask)
    after_self = inputs + project(context, out_weight)
    normed, unit_two, scale_two = normalize(after_self, gain_two)
    second = normed.astype(jnp.bfloat16)
    cross_queries = project(second, source_query_weight).astype(jnp.bfloat16)
    cross_context, logsum_cross = attend(cross_queries, memory_keys, memory_values, source_mask)
    after_cross = after_self + project(cross_context, source_out_weight)
    normed, unit_three, scale_three = normalize(after_cross, gain_three)
    third = normed.astype(jnp.bfloat16)
    hidden_pre = project(third, expand_weight)
    hidden = jax.nn.gelu(hidden_pre, approximate=False).astype(jnp.bfloat16)
    result = after_cross + project(hidden, reduce_weight)

    grad_out = cotangent[:, 0].astype(jnp.float32)
    grad_branch = grad_out.astype(jnp.bfloat16)
    grad_reduce = outer(flat(hidden), flat(grad_branch))
    grad_hidden = project_back(grad_branch, reduce_weight)
    _, gelu_pull = jax.vjp(lambda v: jax.nn.gelu(v, approximate=False), hidden_pre)
    grad_pre = gelu_pull(grad_hidden)[0].astype(jnp.bfloat16)
    grad_expand = outer(flat(third), flat(grad_pre))
    grad_norm, grad_gain_three = normalize_back(
        project_back(grad_pre, expand_weight), unit_three, scale_three, gain_three
    )
    grad_cross = grad_out + grad_norm

    grad_branch = grad_cross.astype(jnp.bfloat16)
    grad_source_output = outer(flat(cross_context), flat(grad_branch))
    grad_context = project_back(grad_branch, source_out_weight).astype(jnp.bfloat16)
    grad_cq, grad_mk, grad_mv = attend_back(
        cross_queries, memory_keys, memory_values, source_mask, logsum_cross, grad_context
    )
    grad_both = jnp.concatenate([grad_mk, grad_mv], axis=-1)
    grad_source_query = outer(flat(second), flat(grad_cq))
    grad_source_both = outer(flat(source), flat(grad_both))
    grad_memory = project_back(grad_both, kv_weight)
    grad_norm, grad_gain_two = normalize_back(
        project_back(grad_cq, source_query_weight), unit_two, scale_two, gain_two
    )
    grad_self = grad_cross + grad_norm

    grad_branch = grad_self.astype(jnp.bfloat16)
    grad_causal_output = outer(flat(context), flat(grad_branch))
    grad_context = project_back(grad_branch, out_weight).astype(jnp.bfloat16)
    grad_q, grad_k, grad_v = attend_back(
        queries, keys, values, causal_mask, logsum_self, grad_context
    )
    grad_qkv = jnp.concatenate([grad_q, grad_k, grad_v], axis=-1)
    grad_causal = outer(flat(first), flat(grad_qkv))
    grad_norm, grad_gain_one = normalize_back(
        project_back(grad_qkv, qkv_weight), unit_one, scale_one, gain_one
    )
    grad_inputs = grad_self + grad_norm
    gain_sums = jnp.stack([grad_gain_one, grad_gain_two, grad_gain_three])
    gain_sums = jnp.pad(gain_sums, ((0, 5), (0, 0)))
    (
        grad_reduce,
        grad_expand,
        grad_source_output,
        grad_source_query,
        grad_source_both,
        grad_causal_output,
        grad_causal,
        grad_gains,
    ) = reduce_all(
        [
            grad_reduce,
            grad_expand,
            grad_source_output,
            grad_source_query,
            grad_source_both,
            grad_causal_output,
            grad_causal,
        ],
        gain_sums,
    )
    entries = causal_gain.shape[0]
    me = lax.axis_index("dp") * lax.axis_size("fsdp") + lax.axis_index("fsdp")
    grad_gains = lax.dynamic_slice_in_dim(grad_gains, me * entries, entries, axis=1)
    return (
        result.astype(jnp.bfloat16)[:, None],
        grad_inputs[:, None],
        grad_memory[:, None],
        grad_gains[0],
        grad_causal[:, :width],
        grad_causal[:, width : 2 * width],
        grad_causal[:, 2 * width :],
        grad_causal_output,
        grad_gains[1],
        grad_source_query,
        grad_source_both[:, :width],
        grad_source_both[:, width:],
        grad_source_output,
        grad_gains[2],
        grad_expand,
        grad_reduce,
    )


def solution(mesh):
    pages = P(None, AXES, None, None)
    counts = P(None, AXES)
    gain = P(AXES)
    weight = P(AXES, None)
    return jax.shard_map(
        per_device,
        mesh=mesh,
        in_specs=(pages, pages, pages, counts, counts)
        + (gain, weight, weight, weight, weight)
        + (gain, weight, weight, weight, weight)
        + (gain, weight, weight),
        out_specs=(pages, pages, pages)
        + (gain, weight, weight, weight, weight)
        + (gain, weight, weight, weight, weight)
        + (gain, weight, weight),
        check_vma=False,
    )
```

```python
import functools

import jax
import jax.numpy as jnp
from jax import lax
from jax.experimental import pallas as pl
from jax.experimental.pallas import tpu as pltpu
from jax.sharding import PartitionSpec as P

HD = 64
EPS = 1e-05
AXES = ("dp", "fsdp")
CORES = 2
WIDTH = 1024
MESH = pl.DeviceIdType.MESH


class Grid:
    def __init__(self):
        dp, fsdp = lax.axis_size("dp"), lax.axis_size("fsdp")
        self.n = dp // CORES
        self.depth = fsdp // self.n
        self.devices = dp * fsdp
        d, f = lax.axis_index("dp"), lax.axis_index("fsdp")
        self.at = (d // CORES, d % CORES, f // self.n, f % self.n)

    def device(self, y, c, z, x):
        return (y * CORES + c, z * self.n + x)

    def step_z(self, k):
        y, c, z, x = self.at
        return self.device(y, c, lax.rem(z + k, self.depth), x)

    def step_plane(self, k, swap):
        y, c, z, x = self.at
        odd = lax.rem(c + swap, 2)
        return self.device(
            lax.rem(y + k * odd, self.n), c, z, lax.rem(x + k * (1 - odd), self.n)
        )

    def partner(self):
        y, c, z, x = self.at
        return self.device(y, 1 - c, z, x)

    def place(self, a, b):
        y, c, z, x = self.at
        ky = a * c + b * (1 - c)
        kx = a * (1 - c) + b * c
        return lax.rem(y + ky, self.n), lax.rem(x + kx, self.n)

    def peers(self):
        line = [self.step_z(k) for k in range(1, self.depth)]
        plane = [self.step_plane(k, s) for s in (0, 1) for k in range(1, self.n)]
        return line + plane + [self.partner()]

    def meet(self):
        barrier = pltpu.get_barrier_semaphore()
        peers = self.peers()
        for peer in peers:
            pl.semaphore_signal(barrier, inc=1, device_id=peer, device_id_type=MESH)
        pl.semaphore_wait(barrier, len(peers))


def remote(src, dst, send_sem, recv_sem, device):
    return pltpu.make_async_remote_copy(
        src_ref=src,
        dst_ref=dst,
        send_sem=send_sem,
        recv_sem=recv_sem,
        device_id=device,
        device_id_type=MESH,
    )


def started(*copy):
    made = remote(*copy)
    made.start()
    return made


class Plan:
    def __init__(self):
        self.calls = {}

    def add(self, tick, rank, call, *args):
        self.calls.setdefault((tick, rank), []).append((call, args))

    def run(self):
        for key in sorted(self.calls):
            for call, args in self.calls[key]:
                call(*args)


def gather_kernel(chunks, count, *refs):
    grid = Grid()
    n, depth = grid.n, grid.depth
    shards, outs = refs[:count], refs[count : 2 * count]
    local, zs, zr, ps, pr, qs, qr, cs, cr, us, ur, ds, dr = refs[2 * count :]
    y, c, z, x = grid.at
    grid.meet()
    pending = []

    def send(*copy):
        made = started(*copy)
        pending.append(made)
        return made

    def window(i):
        _, r0, nr, c0, nc, _ = chunks[i]
        return pl.ds(r0, nr), pl.ds(c0, nc)

    def shard(i):
        return shards[chunks[i][0]].at[window(i)]

    def block(i, yy, zz, xx):
        return outs[chunks[i][0]].at[(yy, c, zz, xx) + window(i)]

    def back(a, b):
        return grid.place((n - a) % n, (n - b) % n)

    def column(i, a, b):
        yy, xx = back(a, b)
        return outs[chunks[i][0]].at[(yy, c, slice(None), xx) + window(i)]

    def share(i, a, b):
        piece = column(i, a, b)
        slot = a * n + b
        return send(piece, piece, cs.at[i, slot], cr.at[i, slot], grid.partner())

    zc, pc, qc, cc, lc = {}, {}, {}, {}, {}

    def keep_own(i):
        lc[i] = pltpu.make_async_copy(shard(i), block(i, y, z, x), local.at[i])
        lc[i].start()

    def stage_z(i):
        zc[i] = [
            send(shard(i), block(i, y, z, x), zs.at[i, k - 1], zr.at[i, k - 1], grid.step_z(k))
            for k in range(1, depth)
        ]
        keep_own(i)

    def stage_p(i):
        for copy in zc[i]:
            copy.wait_recv()
        lc[i].wait()
        piece = column(i, 0, 0)
        pc[i] = [
            send(piece, piece, ps.at[i, a - 1], pr.at[i, a - 1], grid.step_plane(a, 0))
            for a in range(1, n)
        ]
        qc[i] = [
            send(piece, piece, qs.at[i, b - 1], qr.at[i, b - 1], grid.step_plane(b, 1))
            for b in range(1, n)
        ]
        cc[i] = [share(i, 0, 0)]

    def stage_q(i):
        for a in range(1, n):
            pc[i][a - 1].wait_recv()
            piece = column(i, a, 0)
            for b in range(1, n):
                j = a * (n - 1) + b - 1
                qc[i].append(
                    send(piece, piece, qs.at[i, j], qr.at[i, j], grid.step_plane(b, 1))
                )
            cc[i].append(share(i, a, 0))

    def stage_c(i):
        j = 0
        for a in range(n):
            for b in range(1, n):
                qc[i][j].wait_recv()
                j += 1
                cc[i].append(share(i, a, b))

    def tall_p(i):
        keep_own(i)
        pc[i] = [
            send(shard(i), block(i, y, z, x), ps.at[i, a - 1], pr.at[i, a - 1], grid.step_plane(a, 0))
            for a in range(1, n)
        ]

    def tall_q(i):
        lc[i].wait()
        qc[i] = []
        for a in range(n):
            if a:
                pc[i][a - 1].wait_recv()
            yy, xx = back(a, 0)
            piece = block(i, yy, z, xx)
            for b in range(1, n):
                j = a * (n - 1) + b - 1
                qc[i].append(
                    send(piece, piece, qs.at[i, j], qr.at[i, j], grid.step_plane(b, 1))
                )

    def layer(i, k, j):
        zz = lax.rem(z + (depth - j if k == 0 else j), depth)
        return outs[chunks[i][0]].at[(slice(None), c, zz, slice(None)) + window(i)]

    def hop(i, k, j):
        piece = layer(i, k, j)
        send_sem, recv_sem = ((us, ur), (ds, dr))[k]
        to = grid.device(y, c, lax.rem(z + (1 if k == 0 else depth - 1), depth), x)
        return remote(piece, piece, send_sem.at[i, j], recv_sem.at[i, j], to)

    def share_layer(i, k, j):
        piece = layer(i, k, j)
        slot = k * (depth - 1) + j
        return remote(piece, piece, cs.at[i, slot], cr.at[i, slot], grid.partner())

    def level(k):
        return z if k == 0 else depth - 1 - z

    def climb(i, j):
        if j == 0:
            for copy in qc[i]:
                copy.wait_recv()
            share_layer(i, 0, 0).start()
        for k in (0, 1):
            if j:

                @pl.when(level(k) >= j)
                def _():
                    hop(i, k, j - 1).wait_recv()
                    share_layer(i, k, j).start()

            if j < depth - 1:

                @pl.when((level(k) >= j) & (level(k) < depth - 1))
                def _():
                    hop(i, k, j).start()

    def finish_tall(i):
        share_layer(i, 0, 0).wait()
        for k in (0, 1):
            for j in range(depth - 1):

                @pl.when((level(k) >= j) & (level(k) < depth - 1))
                def _():
                    hop(i, k, j).wait_send()

                @pl.when(level(k) >= j + 1)
                def _():
                    share_layer(i, k, j + 1).wait()

    plan = Plan()
    flat = [i for i, chunk in enumerate(chunks) if not chunk[5]]
    tall = [i for i, chunk in enumerate(chunks) if chunk[5]]
    for t, i in enumerate(flat):
        plan.add(t - 2, 0, stage_z, i)
        plan.add(t, 2, stage_p, i)
        plan.add(t + 1, 4, stage_q, i)
        plan.add(t + 2, 6, stage_c, i)
    for t, i in enumerate(tall):
        t = 3 * t - 1
        plan.add(t, 1, tall_p, i)
        plan.add(t + 2, 3, tall_q, i)
        for h in range(depth):
            plan.add(t + 4 + 2 * h, 5, climb, i, h)
    plan.run()
    for i in flat:
        for copy in cc[i]:
            copy.wait_recv()
    for i in tall:
        finish_tall(i)
    for copy in pending:
        copy.wait_send()


def gather_all(shards, tall):
    dp, fsdp = lax.axis_size("dp"), lax.axis_size("fsdp")
    n = dp // CORES
    depth = fsdp // n
    rows = shards[0].shape[0]
    chunks = []
    for m, shard in enumerate(shards):
        r, cols = shard.shape
        for r0 in range(0, r, rows):
            for c0 in range(0, cols // WIDTH * WIDTH, WIDTH):
                nc = WIDTH if c0 + 2 * WIDTH <= cols else cols - c0
                chunks.append((m, r0, rows, c0, nc, len(chunks) in tall))
    t = len(chunks)
    slots = max(n * n, 2 * depth - 1)
    shapes = (1, depth - 1, depth - 1, n - 1, n - 1, n * (n - 1), n * (n - 1), slots, slots)
    shapes += (depth - 1,) * 4
    dma = pltpu.SemaphoreType.DMA
    outs = pl.pallas_call(
        functools.partial(gather_kernel, chunks, len(shards)),
        out_shape=[
            jax.ShapeDtypeStruct((n, CORES, depth, n) + s.shape, s.dtype) for s in shards
        ],
        in_specs=[pl.BlockSpec(memory_space=pltpu.VMEM)] * len(shards),
        out_specs=[pl.BlockSpec(memory_space=pltpu.HBM)] * len(shards),
        scratch_shapes=[dma((t,))] + [dma((t, k)) for k in shapes[1:]],
        compiler_params=pltpu.CompilerParams(collective_id=0, has_side_effects=True),
    )(*shards)
    return [o.reshape(dp * fsdp * s.shape[0], s.shape[1]) for o, s in zip(outs, shards)]


RING = 4
BLOCK = 256
SPARE = 3


def back_kernel(dims, *refs):
    pages, length, slots = dims
    it = iter(refs)

    def take(k):
        return [next(it) for _ in range(k)]

    (hidden_in, pre_in, third_in, out_in, cross_in, cctx_in, second_in, cq_in, kv_in, memory_in,
     self_in, ctx_in, first_in, qkv_in, x_in, wqo_in, wkv_in, wself_in) = take(18)
    counts, lengths, gains, gain_three, lse_cross, lse_self = take(6)
    grad_outs = take(7)
    gain_out, input_out, memory_out = take(3)
    (hidden, pre, third, out_grad, cross, cctx, second, cq, kv, memory, after_self, ctx, first, qkv, x_bf,
     w_a, w_b, branch, g_ctx, stage) = take(20)
    send0, got0, parts, got1, halves, got2, line, got3, gain_sum, gain_got = take(10)
    local, s0, r0, s1, r1, s2, r2, s3, r3, gs, gr, free = take(12)

    grid = Grid()
    n, depth = grid.n, grid.depth
    y, c, z, x = grid.at
    rows, width = send0.shape[-2:]
    f32, bf16 = jnp.float32, jnp.bfloat16
    copies, loads = {}, {}

    def fetch(name, src, dst, slot):
        loads[name] = pltpu.make_async_copy(src, dst, local.at[slot])
        loads[name].start()

    def need(*names):
        for name in names:
            copy = loads.pop(name, None)
            if copy is not None:
                copy.wait()

    D = x_bf.shape[1]
    fetch("hidden", hidden_in, hidden, 0)
    fetch("out", out_in, out_grad, 1)
    fetch("pre", pre_in, pre, 2)
    fetch("third", third_in, third, 3)
    fetch("cross", cross_in, cross, 4)
    fetch("wqo", wqo_in, w_a, 15)
    grid.meet()
    fetch("cctx", cctx_in, cctx, 5)
    fetch("cq", cq_in, cq, 7)
    fetch("kv", kv_in, kv, 8)
    fetch("second", second_in, second, 6)
    fetch("memory", memory_in, memory, 9)
    fetch("self", self_in, after_self, 10)
    fetch("ctx", ctx_in, ctx, 11)
    fetch("first", first_in, first, 12)
    fetch("qkv", qkv_in, qkv, 13)
    fetch("x", x_in, x_bf, 14)
    fetch("wo", wself_in.at[:, pl.ds(3 * D, D)], w_b.at[:, pl.ds(0, D)], 16)
    fetch("wq", wself_in.at[:, pl.ds(0, D)], w_b.at[:, pl.ds(D, D)], 17)

    chunks = []
    wide = hidden.shape[1] // grid.devices
    for col in range(0, D, width * rows // wide):
        chunks.append((0, hidden, out_grad, col, ("hidden", "out")))
    for col in range(0, pre.shape[1], width):
        chunks.append((1, third, pre, col, ("third", "pre")))
    chunks.append((2, cctx, branch, 0, ("cctx",)))
    chunks.append((3, second, cq, 0, ("second",)))
    chunks.append((4, memory, kv, 0, ("memory",)))
    chunks.append((4, memory, kv, D, ()))
    chunks.append((5, ctx, branch, 0, ("ctx",)))
    for col in range(0, 3 * D, width):
        chunks.append((6, first, qkv, col, ("first",)))
    total = len(chunks)

    def products(i, core, emit):
        _, left, right, col, names = chunks[i]
        need(*names)
        own = left.shape[1] // grid.devices
        span = left.shape[1] // (n * CORES)
        lanes = width * rows // own

        def body(yy, carry):
            at = pl.multiple_of((yy * CORES + core) * span, min(span, BLOCK))
            value = lax.dot_general(
                left[:, pl.ds(at, span)],
                right[:, pl.ds(col, lanes)],
                (((0,), (0,)), ((), ())),
                preferred_element_type=f32,
            )
            for k in range(depth * n):
                for part in range(own // rows):
                    top = k * own + part * rows
                    emit(yy, k // n, k % n, part * lanes, lanes, value[top : top + rows])
            return carry

        lax.fori_loop(0, n, body, 0)

    def reuse(i, stage, ring):
        if i >= ring:
            for copy in copies[i - ring, stage]:
                copy.wait_send()

    def stage0(i):
        s = i % SPARE
        reuse(i, 0, SPARE)

        def emit(yy, zz, xx, lane, lanes, value):
            send0[s, yy, zz, xx, :, pl.ds(lane, lanes)] = value.astype(bf16)

        products(i, 1 - c, emit)
        if i >= RING:
            pl.semaphore_wait(free, 1)
        copies[i, 0] = [started(send0.at[s], got0.at[i % RING], s0.at[s], r0.at[i % RING], grid.partner())]

    def stage1(i):
        s = i % RING
        reuse(i, 1, RING)
        copies[i, 0][0].wait_recv()

        def emit(yy, zz, xx, lane, lanes, value):
            value = value + got0[s, yy, zz, xx, :, pl.ds(lane, lanes)].astype(f32)
            to_y = lax.rem(yy - y + n, n)
            to_x = lax.rem(xx - x + n, n)
            a = to_x * (1 - c) + to_y * c
            b = to_y * (1 - c) + to_x * c
            parts[s, a, b, zz, :, pl.ds(lane, lanes)] = value.astype(bf16)

        products(i, c, emit)
        if i + RING < total:
            pl.semaphore_signal(free, inc=1, device_id=grid.partner(), device_id_type=MESH)
        copies[i, 1] = [
            started(
                parts.at[s, a],
                got1.at[i, a - 1],
                s1.at[s, a - 1],
                r1.at[i, a - 1],
                grid.step_plane(a, 0),
            )
            for a in range(1, n)
        ]

    def stage2(i):
        s = i % RING
        reuse(i, 2, RING)
        for copy in copies[i, 1]:
            copy.wait_recv()
        copies[i, 2] = []
        for b in list(range(1, n)) + [0]:

            def body(zz, carry):
                value = parts[s, 0, b, zz].astype(f32)
                for a in range(1, n):
                    value = value + got1[i, a - 1, b, zz].astype(f32)
                halves[s, b, zz] = value.astype(bf16)
                return carry

            lax.fori_loop(0, depth, body, 0)
            if b:
                copies[i, 2].append(
                    started(
                        halves.at[s, b],
                        got2.at[i, b - 1],
                        s2.at[s, b - 1],
                        r2.at[i, b - 1],
                        grid.step_plane(b, 1),
                    )
                )

    def stage3(i):
        s = i % RING
        reuse(i, 3, RING)
        for copy in copies[i, 2]:
            copy.wait_recv()

        def body(zz, carry):
            value = halves[s, 0, zz].astype(f32)
            for b in range(1, n):
                value = value + got2[i, b - 1, zz].astype(f32)
            line[s, zz] = value.astype(bf16)
            return carry

        lax.fori_loop(0, depth, body, 0)
        copies[i, 3] = [
            started(
                line.at[s, lax.rem(z + k, depth)],
                got3.at[i, k - 1],
                s3.at[s, k - 1],
                r3.at[i, k - 1],
                grid.step_z(k),
            )
            for k in range(1, depth)
        ]

    def stage4(i):
        m, left, _, col, _ = chunks[i]
        for copy in copies[i, 3]:
            copy.wait_recv()
        value = line[i % RING, z].astype(f32)
        for k in range(1, depth):
            value = value + got3[i, k - 1].astype(f32)
        own = left.shape[1] // grid.devices
        if own == rows:
            grad_outs[m][:, pl.ds(col, width)] = value
        else:
            for part in range(own // rows):
                grad_outs[m][pl.ds(part * rows, rows), pl.ds(col, BLOCK)] = value[
                    :, part * BLOCK : (part + 1) * BLOCK
                ]

    moves = [
        [grid.partner()],
        [grid.step_plane(a, 0) for a in range(1, n)],
        [grid.step_plane(a, 1) for a in range(1, n)],
        [grid.step_z(k) for k in range(1, depth)],
        [],
    ]
    start = [0, 1, n, 2 * n - 1, 2 * n + depth - 2]

    def gain_step(h):
        value = gain_sum[min(h, 3)]
        if h:
            for j, copy in enumerate(copies["gain", h - 1]):
                copy.wait_recv()
                value = value + gain_got[start[h - 1] + j]
        if h == len(moves) - 1:
            gain_out[...] = value
        elif h:
            gain_sum[h] = value
        if h < len(moves) - 2:
            gain_sum[h + 1] = value
        copies["gain", h] = [
            started(
                gain_sum.at[h],
                gain_got.at[start[h] + j],
                gs.at[start[h] + j],
                gr.at[start[h] + j],
                device,
            )
            for j, device in enumerate(moves[h])
        ]

    def times_transposed(left, right):
        return lax.dot_general(left, right, (((1,), (1,)), ((), ())), preferred_element_type=f32)

    def round_branch():
        need("cross")

        def body(k, carry):
            at = pl.ds(k * 32, 32)
            branch[at] = cross[at].astype(bf16)
            return carry

        lax.fori_loop(0, cross.shape[0] // 32, body, 0)

    def context_grad(weight, col):
        def body(k, carry):
            at = pl.multiple_of(k * BLOCK, BLOCK)
            g_ctx[:, pl.ds(at, BLOCK)] = times_transposed(
                branch[...], weight[pl.ds(at, BLOCK), pl.ds(col, D)]
            ).astype(bf16)
            return carry

        lax.fori_loop(0, D // BLOCK, body, 0)

    lane = lax.broadcasted_iota(jnp.int32, (length, 2 * HD), 1)
    scale = HD ** (-0.5)

    def attention(page, pair, q_ref, q_col, k_ref, k_row, k_rows, k_col, v_col, lse, allowed):
        def lanes(col):
            return pl.ds(pl.multiple_of(col + pair * 2 * HD, 2 * HD), 2 * HD)

        q_at = pl.ds(page * length, length)
        k_at = pl.ds(k_row, k_rows)
        queries, grads = q_ref[q_at, lanes(q_col)], g_ctx[q_at, lanes(0)]
        keys, values = k_ref[k_at, lanes(k_col)], k_ref[k_at, lanes(v_col)]
        g_keys = g_values = None
        g_queries = []
        for h in range(2):
            mine = (lane // HD) == h
            q = jnp.where(mine, queries, jnp.zeros_like(queries))
            g = jnp.where(mine, grads, jnp.zeros_like(grads))
            scores = times_transposed(keys, q) * scale
            scores = jnp.where(allowed, scores, -1000000000.0)
            row = page * (D // HD) + pair * 2 + h
            probs = jnp.exp(scores - lse[pl.ds(row, 1), :])
            g_probs = times_transposed(values, g)
            inner = jnp.sum(probs * g_probs, axis=0, keepdims=True)
            g_scores = (probs * (g_probs - inner)).astype(bf16)
            g_v = jnp.dot(probs.astype(bf16), g, preferred_element_type=f32)
            g_k = jnp.dot(g_scores, q, preferred_element_type=f32)
            g_queries.append(
                lax.dot_general(
                    g_scores, keys, (((0,), (0,)), ((), ())), preferred_element_type=f32
                )
            )
            g_keys = g_k if g_keys is None else g_keys + g_k
            g_values = g_v if g_values is None else g_values + g_v
        g_q = jnp.where(lane < HD, g_queries[0], g_queries[1]) * scale
        q_ref[q_at, lanes(q_col)] = g_q.astype(bf16)
        k_ref[k_at, lanes(k_col)] = (g_keys * scale).astype(bf16)
        k_ref[k_at, lanes(v_col)] = g_values.astype(bf16)

    def cross_attention(page):
        need("cq", "kv")
        place = lax.broadcasted_iota(jnp.int32, (slots, length), 0)
        allowed = place < counts[page]

        def body(pair, carry):
            attention(page, pair, cq, 0, kv, page * slots, slots, 0, D, lse_cross, allowed)
            return carry

        lax.fori_loop(0, D // (2 * HD), body, 0)

    def self_attention(page):
        need("qkv")
        key = lax.broadcasted_iota(jnp.int32, (length, length), 0)
        query = lax.broadcasted_iota(jnp.int32, (length, length), 1)
        allowed = (key <= query) & (key < lengths[page])

        def body(pair, carry):
            attention(page, pair, qkv, 0, qkv, page * length, length, D, 2 * D, lse_self, allowed)
            return carry

        lax.fori_loop(0, D // (2 * HD), body, 0)

    def norm_back(value_ref, gain_row, grad_of, put):
        gain = gains[pl.ds(gain_row, 1), :]

        def body(k, total_):
            at = pl.ds(k * 32, 32)
            value = value_ref[at].astype(f32)
            centred = value - jnp.mean(value, axis=-1, keepdims=True)
            spread = jnp.mean(centred * centred, axis=-1, keepdims=True)
            row_scale = lax.rsqrt(spread + EPS)
            unit = centred * row_scale
            grad = grad_of(at)
            grad_unit = grad * gain
            inner = jnp.mean(grad_unit * unit, axis=-1, keepdims=True)
            put(at, row_scale * (grad_unit - jnp.mean(grad_unit, axis=-1, keepdims=True) - unit * inner))
            return total_ + jnp.sum(grad * unit, axis=0, keepdims=True)

        summed = lax.fori_loop(0, value_ref.shape[0] // 32, body, jnp.zeros((1, D), f32))
        gain_sum[0, pl.ds(gain_row, 1), :] = summed

    def second_norm():
        need("self")

        def grad_of(at):
            return times_transposed(cq[at], w_a[:, pl.ds(0, D)])

        def put(at, value):
            value = cross[at] + value
            cross[at] = value
            branch[at] = value.astype(bf16)

        norm_back(after_self, 1, grad_of, put)
        fetch("wkv2", wself_in.at[:, pl.ds(D, 2 * D)], w_a, 15)

    def first_norm():
        need("x", "wkv2")

        def grad_of(at):
            value = times_transposed(qkv[at, pl.ds(0, D)], w_b[:, pl.ds(D, D)])
            return value + times_transposed(qkv[at, pl.ds(D, 2 * D)], w_a_cat(at))

        def w_a_cat(at):
            return w_a[...]

        def grad_of(at):
            value = times_transposed(qkv[at, pl.ds(0, D)], w_b[:, pl.ds(D, D)])
            value = value + times_transposed(qkv[at, pl.ds(D, D)], w_a[:, pl.ds(0, D)])
            return value + times_transposed(qkv[at, pl.ds(2 * D, D)], w_a[:, pl.ds(D, D)])

        def put(at, value):
            input_out[at] = cross[at] + value

        norm_back(x_bf, 0, grad_of, put)
        fetch("wkv", wkv_in, w_b, 16)

    def memory_grad(page, part):
        need("wkv")
        slot = part % 2
        need(("stage", slot))
        top = part * span
        height = min(slots - top, span)
        live = min(memory_rows - top, height)
        at = pl.ds(page * slots + top, height)

        def body(k, carry):
            col = pl.multiple_of(k * BLOCK, BLOCK)
            value = times_transposed(kv[at, :], w_b[pl.ds(col, BLOCK), :])
            for j in range(BLOCK // 128):
                stage[slot, pl.ds(k * (BLOCK // 128) + j, live, 8), :] = value[:live, j * 128 : j * 128 + 128]
            return carry

        lax.fori_loop(0, D // BLOCK, body, 0)
        fetch(
            ("stage", slot),
            stage.at[slot, pl.ds(0, live * 8)],
            memory_out.at[pl.ds((page * memory_rows + top) * 8, live * 8)],
            18 + slot,
        )

    span = -(-slots // 32) * 16
    memory_rows = memory_out.shape[0] // 8 // pages
    gain_sum[0] = gain_three[...]
    plan = Plan()
    for i in range(total):
        plan.add(i - 2, 0, stage0, i)
        plan.add(i, 1, stage1, i)
        plan.add(i + 1, 2, stage2, i)
        plan.add(i + 2, 3, stage3, i)
        plan.add(i + 3, 4, stage4, i)

    def cross_in_grad():
        need("wqo")
        context_grad(w_a, D)

    def self_in_grad():
        need("wo", "wq")
        context_grad(w_b, 0)

    plan.add(0, 9, round_branch)
    plan.add(0, 9, cross_in_grad)
    for page in range(pages):
        plan.add(1 + page, 9, cross_attention, page)
        plan.add(8 + page, 11, self_attention, page)
    plan.add(8, 9, second_norm)
    plan.add(8, 9, self_in_grad)
    plan.add(9 + pages, 9, first_norm)
    for page in range(pages):
        for part in range(2):
            plan.add(12 + 2 * part, 9, memory_grad, page, part)
    for h in range(len(moves)):
        plan.add(total - 4 + h, 5, gain_step, h)
    plan.run()
    for i in range(total):
        if i >= total - SPARE:
            copies[i, 0][0].wait_send()
        if i >= total - RING:
            for stage in (1, 2, 3):
                for copy in copies[i, stage]:
                    copy.wait_send()
    for h in range(len(moves)):
        for copy in copies["gain", h]:
            copy.wait_send()
    need(*list(loads))


def backward(big, small, shapes):
    dp, fsdp = lax.axis_size("dp"), lax.axis_size("fsdp")
    n = dp // CORES
    depth = fsdp // n
    devices = dp * fsdp
    rows = WIDTH // devices
    pages, length, slots, live = shapes
    tokens = pages * length
    D = WIDTH
    t = sum(k * m for k, m in ((big[0].shape[1], D), (D, big[1].shape[1]), (D, 8 * D))) // (D * D)
    dma = pltpu.SemaphoreType.DMA
    hops = 2 * n + depth - 2
    outs = [(big[0].shape[1], D), (D, big[1].shape[1]), (D, D), (D, D), (D, 2 * D), (D, D), (D, 3 * D)]
    f32 = jnp.float32

    def scratch(*lead):
        return pltpu.VMEM(lead + (rows, WIDTH), jnp.bfloat16)

    def like(value):
        return pltpu.VMEM(value.shape, value.dtype)

    hbm = pl.BlockSpec(memory_space=pltpu.HBM)
    vmem = pl.BlockSpec(memory_space=pltpu.VMEM)
    smem = pl.BlockSpec(memory_space=pltpu.SMEM)
    return pl.pallas_call(
        functools.partial(back_kernel, (pages, length, slots)),
        out_shape=[jax.ShapeDtypeStruct((k // devices, m), f32) for k, m in outs]
        + [
            jax.ShapeDtypeStruct((8, D), f32),
            jax.ShapeDtypeStruct((tokens, D), f32),
            jax.ShapeDtypeStruct((pages * live * D // 128, 128), f32),
        ],
        in_specs=[hbm] * len(big) + [smem, smem] + [vmem] * 4,
        out_specs=[vmem] * (len(outs) + 2) + [hbm],
        scratch_shapes=[like(v) for v in big[:15]]
        + [pltpu.VMEM((D, 2 * D), jnp.bfloat16)] * 2
        + [pltpu.VMEM((tokens, D), jnp.bfloat16)] * 2
        + [
            pltpu.VMEM((2, -(-slots // 32) * 16 * 8, 128), f32),
            scratch(SPARE, n, depth, n),
            scratch(RING, n, depth, n),
            scratch(RING, n, n, depth),
            scratch(t, n - 1, n, depth),
            scratch(RING, n, depth),
            scratch(t, n - 1, depth),
            scratch(RING, depth),
            scratch(t, depth - 1),
            pltpu.VMEM((4, 8, D), f32),
            pltpu.VMEM((hops, 8, D), f32),
            dma((20,)),
            dma((SPARE,)),
            dma((RING,)),
            dma((RING, n - 1)),
            dma((t, n - 1)),
            dma((RING, n - 1)),
            dma((t, n - 1)),
            dma((RING, depth - 1)),
            dma((t, depth - 1)),
            dma((hops,)),
            dma((hops,)),
            pltpu.SemaphoreType.REGULAR,
        ],
        compiler_params=pltpu.CompilerParams(
            collective_id=1, has_side_effects=True, vmem_limit_bytes=67043328
        ),
    )(*big, *small)


def split_heads(value):
    return value.reshape(value.shape[0], value.shape[1], -1, HD)


def project(left, weight):
    return jnp.einsum("bld,de->ble", left, weight, preferred_element_type=jnp.float32)


def project_back(grad, weight):
    return jnp.einsum("ble,de->bld", grad, weight, preferred_element_type=jnp.float32)


def normalize(value, gain):
    centred = value - jnp.mean(value, axis=-1, keepdims=True)
    spread = jnp.mean(centred * centred, axis=-1, keepdims=True)
    scale_row = lax.rsqrt(spread + EPS)
    unit = centred * scale_row
    return (unit * gain, unit, scale_row)


def normalize_back(grad, unit, scale_row, gain):
    grad_unit = grad * gain
    grad_gain = jnp.sum(grad * unit, axis=(0, 1))
    centred = grad_unit - jnp.mean(grad_unit, axis=-1, keepdims=True)
    grad_input = scale_row * (centred - unit * jnp.mean(grad_unit * unit, axis=-1, keepdims=True))
    return (grad_input, grad_gain)


def masked_scores(queries, keys, allowed):
    scores = jnp.einsum(
        "bqhd,bkhd->bhqk",
        split_heads(queries),
        split_heads(keys),
        preferred_element_type=jnp.float32,
    ) * HD ** (-0.5)
    return jnp.where(allowed[:, None], scores, -1000000000.0)


def attend(queries, keys, values, allowed):
    scores = masked_scores(queries, keys, allowed)
    top = jnp.max(scores, axis=-1, keepdims=True)
    expos = jnp.exp(scores - top)
    total = jnp.sum(expos, axis=-1, keepdims=True)
    probs = (expos / total).astype(jnp.bfloat16)
    context = jnp.einsum(
        "bhqk,bkhd->bqhd", probs, split_heads(values), preferred_element_type=jnp.float32
    )
    return (context.reshape(queries.shape).astype(jnp.bfloat16), top + jnp.log(total))


def per_device(
    hidden_in,
    memory,
    cotangent,
    lengths,
    memory_count,
    causal_gain,
    causal_query,
    causal_key,
    causal_value,
    causal_output,
    source_gain,
    source_query,
    source_key,
    source_value,
    source_output,
    dense_gain,
    dense_expand,
    dense_reduce,
):
    inputs = hidden_in[:, 0].astype(jnp.float32)
    source = memory[:, 0]
    page_length = lengths[:, 0]
    page_count = memory_count[:, 0]
    pages, rows, width = inputs.shape
    slots = source.shape[1]
    places = jnp.arange(rows)
    causal_mask = (places[None, None, :] <= places[None, :, None]) & (
        places[None, None, :] < page_length[:, None, None]
    )
    source_mask = jnp.arange(slots)[None, None, :] < page_count[:, None, None]

    def flat(value):
        return value.reshape(pages * value.shape[1], value.shape[2])

    gains = jnp.stack([causal_gain, source_gain, dense_gain], axis=1)
    gains = jnp.pad(gains, ((0, 0), (0, 125)))
    kv_weight, self_weight, qo_weight, expand_weight, reduce_weight = gather_all(
        [
            jnp.concatenate([source_key, source_value], axis=1),
            jnp.concatenate([causal_query, causal_key, causal_value, causal_output, gains], axis=1),
            jnp.concatenate([source_query, source_output], axis=1),
            dense_expand,
            dense_reduce,
        ],
        (1, 5, 9),
    )
    gain_rows = self_weight[:, 4 * width : 4 * width + 3].T.astype(jnp.float32)
    gain_one, gain_two, gain_three = gain_rows[0], gain_rows[1], gain_rows[2]
    qkv_weight = self_weight[:, : 3 * width]
    out_weight = self_weight[:, 3 * width : 4 * width]
    source_query_weight, source_out_weight = qo_weight[:, :width], qo_weight[:, width:]

    memory_both = project(source, kv_weight).astype(jnp.bfloat16)
    memory_keys, memory_values = memory_both[..., :width], memory_both[..., width:]
    normed, unit_one, scale_one = normalize(inputs, gain_one)
    first = normed.astype(jnp.bfloat16)
    qkv = project(first, qkv_weight).astype(jnp.bfloat16)
    queries, keys, values = (qkv[..., i * width : (i + 1) * width] for i in range(3))
    context, logsum_self = attend(queries, keys, values, causal_mask)
    after_self = inputs + project(context, out_weight)
    normed, unit_two, scale_two = normalize(after_self, gain_two)
    second = normed.astype(jnp.bfloat16)
    cross_queries = project(second, source_query_weight).astype(jnp.bfloat16)
    cross_context, logsum_cross = attend(cross_queries, memory_keys, memory_values, source_mask)
    after_cross = after_self + project(cross_context, source_out_weight)
    normed, unit_three, scale_three = normalize(after_cross, gain_three)
    third = normed.astype(jnp.bfloat16)
    hidden_pre = project(third, expand_weight)
    hidden = jax.nn.gelu(hidden_pre, approximate=False).astype(jnp.bfloat16)
    result = after_cross + project(hidden, reduce_weight)

    grad_out = cotangent[:, 0].astype(jnp.float32)
    grad_branch = grad_out.astype(jnp.bfloat16)
    grad_hidden = project_back(grad_branch, reduce_weight)
    _, gelu_pull = jax.vjp(lambda v: jax.nn.gelu(v, approximate=False), hidden_pre)
    grad_pre = gelu_pull(grad_hidden)[0].astype(jnp.bfloat16)
    grad_norm, grad_gain_three = normalize_back(
        project_back(grad_pre, expand_weight), unit_three, scale_three, gain_three
    )
    grad_cross = grad_out + grad_norm

    pad = -slots % 16
    both = jnp.pad(memory_both, ((0, 0), (0, pad), (0, 0)))
    big = [
        flat(hidden),
        flat(grad_pre),
        flat(third),
        flat(grad_branch),
        flat(grad_cross),
        flat(cross_context),
        flat(second),
        flat(cross_queries),
        flat(both),
        flat(jnp.pad(source, ((0, 0), (0, pad), (0, 0)))),
        flat(after_self),
        flat(context),
        flat(first),
        flat(qkv),
        flat(hidden_in[:, 0]),
        qo_weight,
        kv_weight,
        self_weight,
    ]
    small = [
        page_count,
        page_length,
        jnp.pad(gain_rows, ((0, 5), (0, 0))),
        jnp.pad(grad_gain_three[None], ((2, 5), (0, 0))),
        logsum_cross.reshape(-1, rows),
        logsum_self.reshape(-1, rows),
    ]
    (
        grad_reduce,
        grad_expand,
        grad_source_output,
        grad_source_query,
        grad_source_both,
        grad_causal_output,
        grad_causal,
        grad_gains,
        grad_inputs,
        grad_memory,
    ) = backward(big, small, (pages, rows, slots + pad, slots))
    entries = causal_gain.shape[0]
    me = lax.axis_index("dp") * lax.axis_size("fsdp") + lax.axis_index("fsdp")
    grad_gains = lax.dynamic_slice_in_dim(grad_gains, me * entries, entries, axis=1)
    return (
        result.astype(jnp.bfloat16)[:, None],
        grad_inputs.reshape(pages, 1, rows, width),
        grad_memory.reshape(memory.shape),
        grad_gains[0],
        grad_causal[:, :width],
        grad_causal[:, width : 2 * width],
        grad_causal[:, 2 * width :],
        grad_causal_output,
        grad_gains[1],
        grad_source_query,
        grad_source_both[:, :width],
        grad_source_both[:, width:],
        grad_source_output,
        grad_gains[2],
        grad_expand,
        grad_reduce,
    )


def solution(mesh):
    pages = P(None, AXES, None, None)
    counts = P(None, AXES)
    gain = P(AXES)
    weight = P(AXES, None)
    return jax.shard_map(
        per_device,
        mesh=mesh,
        in_specs=(pages, pages, pages, counts, counts)
        + (gain, weight, weight, weight, weight)
        + (gain, weight, weight, weight, weight)
        + (gain, weight, weight),
        out_specs=(pages, pages, pages)
        + (gain, weight, weight, weight, weight)
        + (gain, weight, weight, weight, weight)
        + (gain, weight, weight),
        check_vma=False,
    )
```

```python
import functools

import jax
import jax.numpy as jnp
from jax import lax
from jax.experimental import pallas as pl
from jax.experimental.pallas import tpu as pltpu
from jax.sharding import PartitionSpec as P

HD = 64
EPS = 1e-05
AXES = ("dp", "fsdp")
CORES = 2
WIDTH = 1024
BLOCK = 256
MESH = pl.DeviceIdType.MESH


class Grid:
    def __init__(self):
        dp, fsdp = lax.axis_size("dp"), lax.axis_size("fsdp")
        self.n = dp // CORES
        self.depth = fsdp // self.n
        self.devices = dp * fsdp
        d, f = lax.axis_index("dp"), lax.axis_index("fsdp")
        self.at = (d // CORES, d % CORES, f // self.n, f % self.n)

    def device(self, y, c, z, x):
        return (y * CORES + c, z * self.n + x)

    def step_z(self, k):
        y, c, z, x = self.at
        return self.device(y, c, lax.rem(z + k, self.depth), x)

    def step_plane(self, k, swap):
        y, c, z, x = self.at
        odd = lax.rem(c + swap, 2)
        return self.device(
            lax.rem(y + k * odd, self.n), c, z, lax.rem(x + k * (1 - odd), self.n)
        )

    def partner(self):
        y, c, z, x = self.at
        return self.device(y, 1 - c, z, x)

    def place(self, a, b):
        y, c, z, x = self.at
        ky = a * c + b * (1 - c)
        kx = a * (1 - c) + b * c
        return lax.rem(y + ky, self.n), lax.rem(x + kx, self.n)

    def peers(self):
        line = [self.step_z(k) for k in range(1, self.depth)]
        plane = [self.step_plane(k, s) for s in (0, 1) for k in range(1, self.n)]
        return line + plane + [self.partner()]

    def meet(self):
        barrier = pltpu.get_barrier_semaphore()
        peers = self.peers()
        for peer in peers:
            pl.semaphore_signal(barrier, inc=1, device_id=peer, device_id_type=MESH)
        pl.semaphore_wait(barrier, len(peers))


def remote(src, dst, send_sem, recv_sem, device):
    return pltpu.make_async_remote_copy(
        src_ref=src,
        dst_ref=dst,
        send_sem=send_sem,
        recv_sem=recv_sem,
        device_id=device,
        device_id_type=MESH,
    )


def started(*copy):
    made = remote(*copy)
    made.start()
    return made


class Plan:
    def __init__(self):
        self.calls = {}

    def add(self, tick, rank, call, *args):
        self.calls.setdefault((tick, rank), []).append((call, args))

    def run(self):
        for key in sorted(self.calls):
            for call, args in self.calls[key]:
                call(*args)


def times(left, right):
    return jnp.dot(left, right, preferred_element_type=jnp.float32)


def times_transposed(left, right):
    return lax.dot_general(left, right, (((1,), (1,)), ((), ())), preferred_element_type=jnp.float32)


def transposed_times(left, right):
    return lax.dot_general(left, right, (((0,), (0,)), ((), ())), preferred_element_type=jnp.float32)


def standardize(value):
    centred = value - jnp.mean(value, axis=-1, keepdims=True)
    spread = jnp.mean(centred * centred, axis=-1, keepdims=True)
    row_scale = lax.rsqrt(spread + EPS)
    return centred * row_scale, row_scale


def standardize_back(grad, unit, row_scale, gain):
    grad_unit = grad * gain
    inner = jnp.mean(grad_unit * unit, axis=-1, keepdims=True)
    return row_scale * (grad_unit - jnp.mean(grad_unit, axis=-1, keepdims=True) - unit * inner)


def lane_window(col, pair):
    return pl.ds(pl.multiple_of(col + pair * 2 * HD, 2 * HD), 2 * HD)


STRIP = 32


def strips(count, body, carry=None):
    def one(k, carry):
        return body(pl.ds(pl.multiple_of(k * STRIP, STRIP), STRIP), carry)

    return lax.fori_loop(0, count // STRIP, one, carry)


FLAT_AHEAD = 2
TALL_GAP = 2
ARRIVED = 5


def front_kernel(dims, chunks, counts_, *refs):
    pages, length, slots = dims
    n_src, n_out = counts_
    it = iter(refs)

    def take(k):
        return [next(it) for _ in range(k)]

    shards = take(n_src)
    x_in, cot_in, memory_in, counts, lengths = take(5)
    outs = take(n_out)
    saved_out = take(13)
    gains, gain_three, lse_cross, lse_self = take(4)
    saved = take(13)
    (result, hidden, pre, third, cross_grad, cctx, second, cq, kv, after_self, ctx, first, qkv) = saved
    x_bf, cot, memory, w_a, w_b, w_d, w_gain, after_cross, slope, g_hidden = take(10)
    local, zs, zr, ps, pr, qs, qr, cs, cr, us, ur, ds, dr, loads_sem, stores_sem = take(15)
    f32, bf16 = jnp.float32, jnp.bfloat16
    grid = Grid()
    n, depth = grid.n, grid.depth
    y, c, z, x = grid.at
    tokens, D = x_bf.shape
    loads = {}

    def fetch(name, src, dst, slot):
        loads[name] = pltpu.make_async_copy(src, dst, loads_sem.at[slot])
        loads[name].start()

    def need(*names):
        for name in names:
            copy = loads.pop(name, None)
            if copy is not None:
                copy.wait()

    fetch("x", x_in, x_bf, 0)
    fetch("cot", cot_in, cot, 1)
    fetch("memory", memory_in, memory, 2)
    grid.meet()
    pending = []

    def send(*copy):
        made = started(*copy)
        pending.append(made)
        return made

    def window(i):
        _, r0, nr, c0, nc, _, o0, _ = chunks[i]
        return pl.ds(r0, nr), pl.ds(o0, nc)

    def out(i):
        return outs[chunks[i][5]]

    def shard(i):
        m, r0, nr, c0, nc, _, _, _ = chunks[i]
        return shards[m].at[pl.ds(r0, nr), pl.ds(c0, nc)]

    def block(i, yy, zz, xx):
        return out(i).at[(yy, c, zz, xx) + window(i)]

    def back(a, b):
        return grid.place((n - a) % n, (n - b) % n)

    def column(i, a, b):
        yy, xx = back(a, b)
        return out(i).at[(yy, c, slice(None), xx) + window(i)]

    def share(i, a, b):
        piece = column(i, a, b)
        slot = a * n + b
        return send(piece, piece, cs.at[i, slot], cr.at[i, slot], grid.partner())

    zc, pc, qc, cc, lc = {}, {}, {}, {}, {}

    def keep_own(i):
        lc[i] = pltpu.make_async_copy(shard(i), block(i, y, z, x), local.at[i])
        lc[i].start()

    def stage_z(i):
        zc[i] = [
            send(shard(i), block(i, y, z, x), zs.at[i, k - 1], zr.at[i, k - 1], grid.step_z(k))
            for k in range(1, depth)
        ]
        keep_own(i)

    def stage_p(i):
        for copy in zc[i]:
            copy.wait_recv()
        lc[i].wait()
        piece = column(i, 0, 0)
        pc[i] = [
            send(piece, piece, ps.at[i, a - 1], pr.at[i, a - 1], grid.step_plane(a, 0))
            for a in range(1, n)
        ]
        qc[i] = [
            send(piece, piece, qs.at[i, b - 1], qr.at[i, b - 1], grid.step_plane(b, 1))
            for b in range(1, n)
        ]
        cc[i] = [share(i, 0, 0)]

    def stage_q(i):
        for a in range(1, n):
            pc[i][a - 1].wait_recv()
            piece = column(i, a, 0)
            for b in range(1, n):
                j = a * (n - 1) + b - 1
                qc[i].append(
                    send(piece, piece, qs.at[i, j], qr.at[i, j], grid.step_plane(b, 1))
                )
            cc[i].append(share(i, a, 0))

    def stage_c(i):
        j = 0
        for a in range(n):
            for b in range(1, n):
                qc[i][j].wait_recv()
                j += 1
                cc[i].append(share(i, a, b))

    def tall_p(i):
        keep_own(i)
        pc[i] = [
            send(shard(i), block(i, y, z, x), ps.at[i, a - 1], pr.at[i, a - 1], grid.step_plane(a, 0))
            for a in range(1, n)
        ]

    def tall_q(i):
        lc[i].wait()
        qc[i] = []
        for a in range(n):
            if a:
                pc[i][a - 1].wait_recv()
            yy, xx = back(a, 0)
            piece = block(i, yy, z, xx)
            for b in range(1, n):
                j = a * (n - 1) + b - 1
                qc[i].append(
                    send(piece, piece, qs.at[i, j], qr.at[i, j], grid.step_plane(b, 1))
                )

    def layer(i, k, j):
        zz = lax.rem(z + (depth - j if k == 0 else j), depth)
        return out(i).at[(slice(None), c, zz, slice(None)) + window(i)]

    def hop(i, k, j):
        piece = layer(i, k, j)
        send_sem, recv_sem = ((us, ur), (ds, dr))[k]
        to = grid.device(y, c, lax.rem(z + (1 if k == 0 else depth - 1), depth), x)
        return remote(piece, piece, send_sem.at[i, j], recv_sem.at[i, j], to)

    def share_layer(i, k, j):
        piece = layer(i, k, j)
        slot = k * (depth - 1) + j
        return remote(piece, piece, cs.at[i, slot], cr.at[i, slot], grid.partner())

    def level(k):
        return z if k == 0 else depth - 1 - z

    def climb(i, j):
        if j == 0:
            for copy in qc[i]:
                copy.wait_recv()
            share_layer(i, 0, 0).start()
        for k in (0, 1):
            if j:

                @pl.when(level(k) >= j)
                def _():
                    hop(i, k, j - 1).wait_recv()
                    share_layer(i, k, j).start()

            if j < depth - 1:

                @pl.when((level(k) >= j) & (level(k) < depth - 1))
                def _():
                    hop(i, k, j).start()

    def each_layer(i, call, hops):
        call(share_layer(i, 0, 0))
        for k in (0, 1):
            for j in range(depth - 1):
                if hops:

                    @pl.when((level(k) >= j) & (level(k) < depth - 1))
                    def _():
                        call(hop(i, k, j))

                @pl.when(level(k) >= j + 1)
                def _():
                    call(share_layer(i, k, j + 1))

    there = set()

    def arrive(*ids):
        for i in ids:
            if i in there:
                continue
            there.add(i)
            if chunks[i][7]:
                each_layer(i, lambda copy: copy.wait_recv(), False)
            else:
                for copy in cc[i]:
                    copy.wait_recv()

    def pull(i, dst, dst_row, slot):
        _, _, nr, _, nc, o, o0, _ = chunks[i]
        arrive(i)
        loads[i] = pltpu.make_async_copy(
            out(i).at[:, :, :, :, :, pl.ds(o0, nc)], dst, loads_sem.at[slot]
        )
        loads[i].start()

    def store(name, slot):
        src = saved[name]
        made = pltpu.make_async_copy(src, saved_out[name], stores_sem.at[slot])
        made.start()
        stores.append(made)

    stores = []
    lane = lax.broadcasted_iota(jnp.int32, (length, 2 * HD), 1)

    def attention(page, pair, q_ref, k_ref, k_row, k_rows, k_col, v_col, allowed, to, lse):
        q_at, k_at = pl.ds(page * length, length), pl.ds(k_row, k_rows)
        queries = q_ref[q_at, lane_window(0, pair)]
        keys = k_ref[k_at, lane_window(k_col, pair)]
        values = k_ref[k_at, lane_window(v_col, pair)]
        found = []
        for h in range(2):
            q = jnp.where((lane // HD) == h, queries, jnp.zeros_like(queries))
            scores = times_transposed(keys, q) * HD ** (-0.5)
            scores = jnp.where(allowed, scores, -1000000000.0)
            top = jnp.max(scores, axis=0, keepdims=True)
            expos = jnp.exp(scores - top)
            sum_ = jnp.sum(expos, axis=0, keepdims=True)
            probs = (expos * (1.0 / sum_)).astype(bf16)
            lse[pl.ds(page * (D // HD) + pair * 2 + h, 1), :] = top + jnp.log(sum_)
            found.append(transposed_times(probs, values))
        to[q_at, lane_window(0, pair)] = jnp.where(lane < HD, found[0], found[1]).astype(bf16)

    def read_gains():
        arrive(GAIN)
        piece = outs[GAIN_OUT]
        copy = pltpu.make_async_copy(piece, w_gain, loads_sem.at[3])
        copy.start()
        copy.wait()
        columns = w_gain.reshape(D, 128)[...].astype(f32)
        gains[...] = columns.T[:8]

    def project(left, weight, col, count, to, to_col):
        def body(k, carry):
            at = pl.multiple_of(k * BLOCK, BLOCK)
            to[:, pl.ds(to_col + at, BLOCK)] = times(
                left[...], weight[:, pl.ds(col + at, BLOCK)]
            ).astype(to.dtype)
            return carry

        lax.fori_loop(0, count // BLOCK, body, 0)

    def first_norm():
        need("x")
        gain = gains[pl.ds(0, 1), :]

        def body(at, carry):
            unit, _ = standardize(x_bf[at].astype(f32))
            first[at] = (unit * gain).astype(bf16)
            return carry

        strips(tokens, body, 0)

    def self_project(k):
        need(SELF[k])
        project(first, flat_b, k * D, D, qkv, k * D)

    def self_attention(page):
        key = lax.broadcasted_iota(jnp.int32, (length, length), 0)
        query = lax.broadcasted_iota(jnp.int32, (length, length), 1)
        allowed = (key <= query) & (key < lengths[page])

        def body(pair, carry):
            attention(page, pair, qkv, qkv, page * length, length, D, 2 * D, allowed, ctx, lse_self)
            return carry

        lax.fori_loop(0, D // (2 * HD), body, 0)

    def residual(left, weight, col, base, to):
        def body(k, carry):
            at = pl.ds(pl.multiple_of(k * BLOCK, BLOCK), BLOCK)
            w_at = pl.ds(pl.multiple_of(col + k * BLOCK, BLOCK), BLOCK)
            to[:, at] = base[:, at].astype(f32) + times(left[...], weight[:, w_at])
            return carry

        lax.fori_loop(0, D // BLOCK, body, 0)

    def self_out():
        need(SELF[3])
        residual(ctx, flat_b, 3 * D, x_bf, after_self)
        gain = gains[pl.ds(1, 1), :]

        def body(at, carry):
            unit, _ = standardize(after_self[at])
            second[at] = (unit * gain).astype(bf16)
            return carry

        strips(tokens, body, 0)

    def memory_project(page, part):
        need("memory", KV[0], KV[1])
        span = -(-slots // 32) * 16
        at = pl.ds(page * slots + part * span, min(span, slots - part * span))

        def body(k, carry):
            col = pl.ds(pl.multiple_of(k * 2 * BLOCK, BLOCK), 2 * BLOCK)
            kv[at, col] = times(memory[at, :], flat_a[:, col]).astype(bf16)
            return carry

        lax.fori_loop(0, D // BLOCK, body, 0)

    def cross_query():
        need(QO[0])
        project(second, flat_a, 0, D, cq, 0)

    def cross_attention(page):
        allowed = lax.broadcasted_iota(jnp.int32, (slots, length), 0) < counts[page]

        def body(pair, carry):
            attention(page, pair, cq, kv, page * slots, slots, 0, D, allowed, cctx, lse_cross)
            return carry

        lax.fori_loop(0, D // (2 * HD), body, 0)

    def cross_out():
        need(QO[1])
        residual(cctx, flat_a, D, after_self, after_cross)
        gain = gains[pl.ds(2, 1), :]

        def body(at, carry):
            unit, _ = standardize(after_cross[at])
            third[at] = (unit * gain).astype(bf16)
            return carry

        strips(tokens, body, 0)

    def expand(k):
        need(EXPAND[k])

        def body(j, carry):
            at = pl.ds(pl.multiple_of(k * D + j * BLOCK, BLOCK), BLOCK)
            value = times(third[...], flat_b[:, at])
            below = 0.5 + 0.5 * lax.erf(value * 0.5**0.5)
            hidden[:, at] = (value * below).astype(bf16)
            density = jnp.exp(-0.5 * value * value) * 0.3989422804014327
            slope[:, at] = below + value * density
            return carry

        lax.fori_loop(0, D // BLOCK, body, 0)

    def hidden_grad(k):
        need("cot", REDUCE[k])
        col = pl.ds(k * BLOCK, BLOCK)

        def body(j, carry):
            at = pl.ds(pl.multiple_of(j * 2 * BLOCK, BLOCK), 2 * BLOCK)
            value = times_transposed(cot[:, col], flat_d[at, col])
            g_hidden[:, at] = value if k == 0 else g_hidden[:, at] + value
            return carry

        lax.fori_loop(0, hidden.shape[1] // (2 * BLOCK), body, 0)

    def reduce_out(k):
        col = pl.ds(k * BLOCK, BLOCK)
        result[:, col] = (after_cross[:, col] + times(hidden[...], flat_d[:, col])).astype(bf16)

    def last_part():
        def body(j, carry):
            at = pl.ds(pl.multiple_of(j * BLOCK, BLOCK), BLOCK)
            pre[:, at] = (g_hidden[:, at] * slope[:, at]).astype(bf16)
            return carry

        lax.fori_loop(0, hidden.shape[1] // BLOCK, body, 0)
        store(2, 2)

        def dot_body(j, carry):
            at = pl.ds(pl.multiple_of(j * BLOCK, BLOCK), BLOCK)
            g_hidden[:, at] = times_transposed(pre[...], flat_b[at, :])
            return carry

        lax.fori_loop(0, D // BLOCK, dot_body, 0)
        gain = gains[pl.ds(2, 1), :]

        def body(at, total_):
            unit, row_scale = standardize(after_cross[at])
            grad = g_hidden[at, pl.ds(0, D)]
            cross_grad[at] = cot[at].astype(f32) + standardize_back(grad, unit, row_scale, gain)
            return total_ + jnp.sum(grad * unit, axis=0, keepdims=True)

        summed = strips(tokens, body, jnp.zeros((1, D), f32))
        gain_three[...] = jnp.zeros_like(gain_three)
        gain_three[pl.ds(2, 1), :] = summed

    flat_a, flat_b, flat_d = w_a.reshape(D, 2 * D), w_b.reshape(D, 4 * D), w_d.reshape(4 * D, D)

    ids = {}
    for i, chunk in enumerate(chunks):
        ids.setdefault(chunk[5], []).append(i)
    SELF, KV, QO, EXPAND, REDUCE = (sorted(ids[o], key=lambda i: chunks[i][6]) for o in range(5))
    GAIN, GAIN_OUT = ids[5][0], 5

    plan = Plan()
    flat = [i for i, chunk in enumerate(chunks) if not chunk[7]]
    tall = [i for i, chunk in enumerate(chunks) if chunk[7]]
    tick = {}
    for t, i in enumerate(flat):
        plan.add(t - FLAT_AHEAD, 0, stage_z, i)
        plan.add(t, 2, stage_p, i)
        plan.add(t + 1, 4, stage_q, i)
        plan.add(t + 2, 6, stage_c, i)
        tick[i] = t + 3
    for t, i in enumerate(tall):
        t = TALL_GAP * t - 1
        plan.add(t, 1, tall_p, i)
        plan.add(t + 2, 3, tall_q, i)
        for h in range(depth):
            plan.add(t + 4 + 2 * h, 5, climb, i, h)
        tick[i] = t + 4 + 2 * (depth - 1) + 1

    def part(buffer, k, width):
        return buffer.at[:, :, :, :, :, pl.ds(k * width, width)]

    now = max(tick[GAIN], tick[SELF[0]])
    plan.add(tick[GAIN], 8, read_gains)
    plan.add(tick[GAIN], 9, first_norm)
    for k in range(4):
        plan.add(tick[SELF[k]], 8, pull, SELF[k], part(w_b, k, D), 0, 4 + k)
        now = max(now, tick[SELF[k]])
        if k < 3:
            plan.add(tick[SELF[k]] + 1, 9, self_project, k)
    t = tick[SELF[2]] + 1
    for page in range(pages):
        plan.add(t + page, 10, self_attention, page)
    t = max(t + pages, tick[SELF[3]] + 1)
    plan.add(t, 11, self_out)
    done_self = t
    for k in range(2):
        plan.add(tick[KV[k]], 8, pull, KV[k], part(w_a, k, D), 0, 8 + k)
    t = max(tick[KV[1]] + 1, done_self)
    for page in range(pages):
        for half in range(2):
            plan.add(t, 12, memory_project, page, half)
    t = max(t + 1, tick[QO[1]])
    for k in range(2):
        plan.add(t, 8, pull, QO[k], part(w_a, k, D), 0, 10 + k)
    plan.add(t, 13, cross_query)
    for page in range(pages):
        plan.add(t + page, 14, cross_attention, page)
    t = t + pages - 1
    plan.add(t, 15, cross_out)
    done_cross = t
    for k in range(4):
        t = max(tick[EXPAND[k]], done_self + 1)
        plan.add(t, 8, pull, EXPAND[k], part(w_b, k, D), 0, 12 + k)
        plan.add(max(t, done_cross), 16, expand, k)
    last = 0
    for k in range(4):
        t = tick[REDUCE[k]]
        plan.add(t, 8, pull, REDUCE[k], part(w_d, k, BLOCK), 0, 16 + k)
        plan.add(t + 1, 17, hidden_grad, k)
        last = max(last, t + 1)
    last = max([last, done_cross] + [tick[i] for i in EXPAND])

    def finish():
        for name, slot in ((1, 1), (3, 3), (5, 5), (6, 6), (7, 7), (8, 8), (9, 9), (10, 10), (11, 11), (12, 12)):
            store(name, slot)
        for k in range(4):
            reduce_out(k)
        store(0, 0)
        last_part()
        store(4, 4)

    plan.add(last + 1, 20, finish)
    plan.run()
    for i in flat:
        arrive(i)
    for i in tall:
        arrive(i)
        each_layer(i, lambda copy: copy.wait_send(), True)
    for copy in pending:
        copy.wait_send()
    for copy in stores:
        copy.wait()


def front(sources, pieces, tokens_in, shapes):
    dp, fsdp = lax.axis_size("dp"), lax.axis_size("fsdp")
    n = dp // CORES
    depth = fsdp // n
    rows = sources[0].shape[0]
    pages, length, slots = shapes
    tokens, D = pages * length, WIDTH
    chunks = [
        (m, 0, sources[m].shape[0], c0, nc, group, o0, tall) for m, c0, nc, group, o0, tall in pieces
    ]
    groups = [(rows, 4 * D), (rows, 2 * D), (rows, 2 * D), (rows, 4 * D), (4 * rows, D), (rows, 128)]
    t = len(chunks)
    slot_count = max(n * n, 2 * depth - 1)
    shapes_ = (depth - 1, depth - 1, n - 1, n - 1, n * (n - 1), n * (n - 1), slot_count, slot_count)
    shapes_ += (depth - 1,) * 4
    dma = pltpu.SemaphoreType.DMA
    f32, bf16 = jnp.float32, jnp.bfloat16
    lead = (n, CORES, depth, n)
    saved = [
        ((tokens, D), bf16),
        ((tokens, 4 * D), bf16),
        ((tokens, 4 * D), bf16),
        ((tokens, D), bf16),
        ((tokens, D), f32),
        ((tokens, D), bf16),
        ((tokens, D), bf16),
        ((tokens, D), bf16),
        ((pages * slots, 2 * D), bf16),
        ((tokens, D), f32),
        ((tokens, D), bf16),
        ((tokens, D), bf16),
        ((tokens, 3 * D), bf16),
    ]
    small = [((8, D), f32), ((8, D), f32), ((pages * D // HD, length), f32), ((pages * D // HD, length), f32)]
    hbm = pl.BlockSpec(memory_space=pltpu.HBM)
    vmem = pl.BlockSpec(memory_space=pltpu.VMEM)
    smem = pl.BlockSpec(memory_space=pltpu.SMEM)
    found = pl.pallas_call(
        functools.partial(front_kernel, shapes, chunks, (len(sources), len(groups))),
        out_shape=[jax.ShapeDtypeStruct(lead + g, bf16) for g in groups]
        + [jax.ShapeDtypeStruct(*s) for s in saved + small],
        in_specs=[vmem] * len(sources) + [hbm] * 3 + [smem] * 2,
        out_specs=[hbm] * (len(groups) + len(saved)) + [vmem] * 4,
        scratch_shapes=[pltpu.VMEM(*s) for s in saved]
        + [
            pltpu.VMEM((tokens, D), bf16),
            pltpu.VMEM((tokens, D), bf16),
            pltpu.VMEM((pages * slots, D), bf16),
            pltpu.VMEM(lead + groups[1], bf16),
            pltpu.VMEM(lead + groups[0], bf16),
            pltpu.VMEM(lead + groups[4], bf16),
            pltpu.VMEM(lead + groups[5], bf16),
            pltpu.VMEM((tokens, D), f32),
            pltpu.VMEM((tokens, 4 * D), f32),
            pltpu.VMEM((tokens, 4 * D), f32),
            dma((t,)),
        ]
        + [dma((t, k)) for k in shapes_]
        + [dma((20,)), dma((13,))],
        compiler_params=pltpu.CompilerParams(
            collective_id=0, has_side_effects=True, vmem_limit_bytes=67043328
        ),
    )(*sources, *tokens_in)
    weights = [
        w.reshape(dp * fsdp * g[0], g[1]) for w, g in zip(found[: len(groups)], groups)
    ]
    return weights, found[len(groups) : len(groups) + len(saved)], found[len(groups) + len(saved) :]


RING = 4
SPARE = 2


def back_kernel(dims, *refs):
    pages, length, slots = dims
    it = iter(refs)

    def take(k):
        return [next(it) for _ in range(k)]

    (hidden_in, pre_in, third_in, out_in, cross_in, cctx_in, second_in, cq_in, kv_in, memory_in,
     self_in, ctx_in, first_in, qkv_in, x_in, wqo_in, wkv_in, wself_in) = take(18)
    counts, lengths, gains, gain_three, lse_cross, lse_self = take(6)
    grad_outs = take(7)
    gain_out, input_out, memory_out = take(3)
    (hidden, pre, third, out_grad, cross, cctx, second, cq, kv, memory, after_self, ctx, first, qkv, x_bf,
     w_a, w_b, branch, g_ctx, stage, g_norm) = take(21)
    send0, got0, parts, got1, halves, got2, line, got3, gain_sum, gain_got = take(10)
    local, s0, r0, s1, r1, s2, r2, s3, r3, gs, gr, free = take(12)

    grid = Grid()
    n, depth = grid.n, grid.depth
    y, c, z, x = grid.at
    rows, width = send0.shape[-2:]
    f32, bf16 = jnp.float32, jnp.bfloat16
    copies, loads = {}, {}

    def fetch(name, src, dst, slot):
        loads[name] = pltpu.make_async_copy(src, dst, local.at[slot])
        loads[name].start()

    def need(*names):
        for name in names:
            copy = loads.pop(name, None)
            if copy is not None:
                copy.wait()

    D = x_bf.shape[1]
    fetch("hidden", hidden_in, hidden, 0)
    fetch("out", out_in, out_grad, 1)
    fetch("pre", pre_in, pre, 2)
    fetch("third", third_in, third, 3)
    fetch("cross", cross_in, cross, 4)
    fetch("wqo", wqo_in, w_a, 15)
    grid.meet()
    fetch("cctx", cctx_in, cctx, 5)
    fetch("cq", cq_in, cq, 7)
    fetch("kv", kv_in, kv, 8)
    fetch("second", second_in, second, 6)
    fetch("memory", memory_in, memory, 9)
    fetch("self", self_in, after_self, 10)
    fetch("ctx", ctx_in, ctx, 11)
    fetch("first", first_in, first, 12)
    fetch("qkv", qkv_in, qkv, 13)
    fetch("x", x_in, x_bf, 14)
    fetch("wo", wself_in.at[:, pl.ds(3 * D, D)], w_b.at[:, pl.ds(0, D)], 16)
    fetch("wq", wself_in.at[:, pl.ds(0, D)], w_b.at[:, pl.ds(D, D)], 17)

    chunks = []
    wide = hidden.shape[1] // grid.devices
    for col in range(0, D, width * rows // wide):
        chunks.append((0, hidden, out_grad, col, ("hidden", "out")))
    for col in range(0, pre.shape[1], width):
        chunks.append((1, third, pre, col, ("third", "pre")))
    chunks.append((2, cctx, branch, 0, ("cctx",)))
    chunks.append((3, second, cq, 0, ("second",)))
    chunks.append((4, memory, kv, 0, ("memory",)))
    chunks.append((4, memory, kv, D, ()))
    chunks.append((5, ctx, branch, 0, ("ctx",)))
    for col in range(0, 3 * D, width):
        chunks.append((6, first, qkv, col, ("first",)))
    total = len(chunks)

    def products(i, core, emit):
        _, left, right, col, names = chunks[i]
        need(*names)
        own = left.shape[1] // grid.devices
        span = left.shape[1] // (n * CORES)
        lanes = width * rows // own

        def body(yy, carry):
            at = pl.multiple_of((yy * CORES + core) * span, min(span, BLOCK))
            value = lax.dot_general(
                left[:, pl.ds(at, span)],
                right[:, pl.ds(col, lanes)],
                (((0,), (0,)), ((), ())),
                preferred_element_type=f32,
            )
            for k in range(depth * n):
                for part in range(own // rows):
                    top = k * own + part * rows
                    emit(yy, k // n, k % n, part * lanes, lanes, value[top : top + rows])
            return carry

        lax.fori_loop(0, n, body, 0)

    def reuse(i, stage, ring):
        if i >= ring:
            for copy in copies[i - ring, stage]:
                copy.wait_send()

    def stage0(i):
        s = i % SPARE
        reuse(i, 0, SPARE)

        def emit(yy, zz, xx, lane, lanes, value):
            send0[s, yy, zz, xx, :, pl.ds(lane, lanes)] = value.astype(bf16)

        products(i, 1 - c, emit)
        if i >= RING:
            pl.semaphore_wait(free, 1)
        copies[i, 0] = [started(send0.at[s], got0.at[i % RING], s0.at[s], r0.at[i % RING], grid.partner())]

    def stage1(i):
        s = i % RING
        reuse(i, 1, RING)
        copies[i, 0][0].wait_recv()

        def emit(yy, zz, xx, lane, lanes, value):
            value = value + got0[s, yy, zz, xx, :, pl.ds(lane, lanes)].astype(f32)
            to_y = lax.rem(yy - y + n, n)
            to_x = lax.rem(xx - x + n, n)
            a = to_x * (1 - c) + to_y * c
            b = to_y * (1 - c) + to_x * c
            parts[s, a, b, zz, :, pl.ds(lane, lanes)] = value.astype(bf16)

        products(i, c, emit)
        if i + RING < total:
            pl.semaphore_signal(free, inc=1, device_id=grid.partner(), device_id_type=MESH)
        copies[i, 1] = [
            started(
                parts.at[s, a],
                got1.at[i, a - 1],
                s1.at[s, a - 1],
                r1.at[i, a - 1],
                grid.step_plane(a, 0),
            )
            for a in range(1, n)
        ]

    def stage2(i):
        s = i % RING
        reuse(i, 2, RING)
        for copy in copies[i, 1]:
            copy.wait_recv()
        copies[i, 2] = []
        for b in list(range(1, n)) + [0]:

            def body(zz, carry):
                value = parts[s, 0, b, zz].astype(f32)
                for a in range(1, n):
                    value = value + got1[i, a - 1, b, zz].astype(f32)
                halves[s, b, zz] = value.astype(bf16)
                return carry

            lax.fori_loop(0, depth, body, 0)
            if b:
                copies[i, 2].append(
                    started(
                        halves.at[s, b],
                        got2.at[i, b - 1],
                        s2.at[s, b - 1],
                        r2.at[i, b - 1],
                        grid.step_plane(b, 1),
                    )
                )

    def stage3(i):
        s = i % RING
        reuse(i, 3, RING)
        for copy in copies[i, 2]:
            copy.wait_recv()

        def body(zz, carry):
            value = halves[s, 0, zz].astype(f32)
            for b in range(1, n):
                value = value + got2[i, b - 1, zz].astype(f32)
            line[s, zz] = value.astype(bf16)
            return carry

        lax.fori_loop(0, depth, body, 0)
        copies[i, 3] = [
            started(
                line.at[s, lax.rem(z + k, depth)],
                got3.at[i, k - 1],
                s3.at[s, k - 1],
                r3.at[i, k - 1],
                grid.step_z(k),
            )
            for k in range(1, depth)
        ]

    def stage4(i):
        m, left, _, col, _ = chunks[i]
        for copy in copies[i, 3]:
            copy.wait_recv()
        value = line[i % RING, z].astype(f32)
        for k in range(1, depth):
            value = value + got3[i, k - 1].astype(f32)
        own = left.shape[1] // grid.devices
        if own == rows:
            grad_outs[m][:, pl.ds(col, width)] = value
        else:
            for part in range(own // rows):
                grad_outs[m][pl.ds(part * rows, rows), pl.ds(col, BLOCK)] = value[
                    :, part * BLOCK : (part + 1) * BLOCK
                ]

    moves = [
        [grid.partner()],
        [grid.step_plane(a, 0) for a in range(1, n)],
        [grid.step_plane(a, 1) for a in range(1, n)],
        [grid.step_z(k) for k in range(1, depth)],
        [],
    ]
    start = [0, 1, n, 2 * n - 1, 2 * n + depth - 2]

    def gain_step(h):
        value = gain_sum[min(h, 3)]
        if h:
            for j, copy in enumerate(copies["gain", h - 1]):
                copy.wait_recv()
                value = value + gain_got[start[h - 1] + j]
        if h == len(moves) - 1:
            gain_out[...] = value
        elif h:
            gain_sum[h] = value
        if h < len(moves) - 2:
            gain_sum[h + 1] = value
        copies["gain", h] = [
            started(
                gain_sum.at[h],
                gain_got.at[start[h] + j],
                gs.at[start[h] + j],
                gr.at[start[h] + j],
                device,
            )
            for j, device in enumerate(moves[h])
        ]

    def times_transposed(left, right):
        return lax.dot_general(left, right, (((1,), (1,)), ((), ())), preferred_element_type=f32)

    def round_branch():
        need("cross")

        def body(k, carry):
            at = pl.ds(k * 32, 32)
            branch[at] = cross[at].astype(bf16)
            return carry

        lax.fori_loop(0, cross.shape[0] // 32, body, 0)

    def context_grad(weight, col):
        def body(k, carry):
            at = pl.multiple_of(k * BLOCK, BLOCK)
            g_ctx[:, pl.ds(at, BLOCK)] = times_transposed(
                branch[...], weight[pl.ds(at, BLOCK), pl.ds(col, D)]
            ).astype(bf16)
            return carry

        lax.fori_loop(0, D // BLOCK, body, 0)

    lane = lax.broadcasted_iota(jnp.int32, (length, 2 * HD), 1)
    scale = HD ** (-0.5)

    def attention(page, pair, q_ref, q_col, k_ref, k_row, k_rows, k_col, v_col, lse, allowed):
        def lanes(col):
            return pl.ds(pl.multiple_of(col + pair * 2 * HD, 2 * HD), 2 * HD)

        q_at = pl.ds(page * length, length)
        k_at = pl.ds(k_row, k_rows)
        queries, grads = q_ref[q_at, lanes(q_col)], g_ctx[q_at, lanes(0)]
        keys, values = k_ref[k_at, lanes(k_col)], k_ref[k_at, lanes(v_col)]
        g_keys = g_values = None
        g_queries = []
        for h in range(2):
            mine = (lane // HD) == h
            q = jnp.where(mine, queries, jnp.zeros_like(queries))
            g = jnp.where(mine, grads, jnp.zeros_like(grads))
            scores = times_transposed(keys, q) * scale
            scores = jnp.where(allowed, scores, -1000000000.0)
            row = page * (D // HD) + pair * 2 + h
            probs = jnp.exp(scores - lse[pl.ds(row, 1), :])
            g_probs = times_transposed(values, g)
            inner = jnp.sum(probs * g_probs, axis=0, keepdims=True)
            g_scores = (probs * (g_probs - inner)).astype(bf16)
            g_v = jnp.dot(probs.astype(bf16), g, preferred_element_type=f32)
            g_k = jnp.dot(g_scores, q, preferred_element_type=f32)
            g_queries.append(
                lax.dot_general(
                    g_scores, keys, (((0,), (0,)), ((), ())), preferred_element_type=f32
                )
            )
            g_keys = g_k if g_keys is None else g_keys + g_k
            g_values = g_v if g_values is None else g_values + g_v
        g_q = jnp.where(lane < HD, g_queries[0], g_queries[1]) * scale
        q_ref[q_at, lanes(q_col)] = g_q.astype(bf16)
        k_ref[k_at, lanes(k_col)] = (g_keys * scale).astype(bf16)
        k_ref[k_at, lanes(v_col)] = g_values.astype(bf16)

    def cross_attention(page):
        need("cq", "kv")
        place = lax.broadcasted_iota(jnp.int32, (slots, length), 0)
        allowed = place < counts[page]

        def body(pair, carry):
            attention(page, pair, cq, 0, kv, page * slots, slots, 0, D, lse_cross, allowed)
            return carry

        lax.fori_loop(0, D // (2 * HD), body, 0)

    def self_attention(page):
        need("qkv")
        key = lax.broadcasted_iota(jnp.int32, (length, length), 0)
        query = lax.broadcasted_iota(jnp.int32, (length, length), 1)
        allowed = (key <= query) & (key < lengths[page])

        def body(pair, carry):
            attention(page, pair, qkv, 0, qkv, page * length, length, D, 2 * D, lse_self, allowed)
            return carry

        lax.fori_loop(0, D // (2 * HD), body, 0)

    def norm_back(value_ref, gain_row, put):
        gain = gains[pl.ds(gain_row, 1), :]

        def body(k, total_):
            at = pl.ds(k * 32, 32)
            value = value_ref[at].astype(f32)
            centred = value - jnp.mean(value, axis=-1, keepdims=True)
            spread = jnp.mean(centred * centred, axis=-1, keepdims=True)
            row_scale = lax.rsqrt(spread + EPS)
            unit = centred * row_scale
            grad = g_norm[at]
            grad_unit = grad * gain
            inner = jnp.mean(grad_unit * unit, axis=-1, keepdims=True)
            put(at, row_scale * (grad_unit - jnp.mean(grad_unit, axis=-1, keepdims=True) - unit * inner))
            return total_ + jnp.sum(grad * unit, axis=0, keepdims=True)

        summed = lax.fori_loop(0, value_ref.shape[0] // 32, body, jnp.zeros((1, D), f32))
        gain_sum[0, pl.ds(gain_row, 1), :] = summed

    def spread(terms):
        def body(k, carry):
            at = pl.ds(pl.multiple_of(k * BLOCK, BLOCK), BLOCK)
            value = None
            for left, left_col, right, right_col in terms:
                term = times_transposed(
                    left[:, pl.ds(left_col, D)], right[at, pl.ds(right_col, D)]
                )
                value = term if value is None else value + term
            g_norm[:, at] = value
            return carry

        lax.fori_loop(0, D // BLOCK, body, 0)

    def second_norm():
        need("self")
        spread([(cq, 0, w_a, 0)])

        def put(at, value):
            value = cross[at] + value
            cross[at] = value
            branch[at] = value.astype(bf16)

        norm_back(after_self, 1, put)
        fetch("wkv2", wself_in.at[:, pl.ds(D, 2 * D)], w_a, 15)

    def first_norm():
        need("x", "wkv2")
        spread([(qkv, 0, w_b, D), (qkv, D, w_a, 0), (qkv, 2 * D, w_a, D)])

        def put(at, value):
            input_out[at] = cross[at] + value

        norm_back(x_bf, 0, put)
        fetch("wkv", wkv_in, w_b, 16)

    def memory_grad(page, part):
        need("wkv")
        slot = part % 2
        need(("stage", slot))
        top = part * span
        height = min(slots - top, span)
        live = min(memory_rows - top, height)
        at = pl.ds(page * slots + top, height)

        def body(k, carry):
            col = pl.multiple_of(k * BLOCK, BLOCK)
            value = times_transposed(kv[at, :], w_b[pl.ds(col, BLOCK), :])
            for j in range(BLOCK // 128):
                stage[slot, pl.ds(k * (BLOCK // 128) + j, live, 8), :] = value[:live, j * 128 : j * 128 + 128]
            return carry

        lax.fori_loop(0, D // BLOCK, body, 0)
        fetch(
            ("stage", slot),
            stage.at[slot, pl.ds(0, live * 8)],
            memory_out.at[pl.ds((page * memory_rows + top) * 8, live * 8)],
            18 + slot,
        )

    span = -(-slots // 32) * 16
    memory_rows = memory_out.shape[0] // 8 // pages
    gain_sum[0] = gain_three[...]
    plan = Plan()
    for i in range(total):
        plan.add(i - 2, 0, stage0, i)
        plan.add(i, 1, stage1, i)
        plan.add(i + 1, 2, stage2, i)
        plan.add(i + 2, 3, stage3, i)
        plan.add(i + 3, 4, stage4, i)

    def cross_in_grad():
        need("wqo")
        context_grad(w_a, D)

    def self_in_grad():
        need("wo", "wq")
        context_grad(w_b, 0)

    plan.add(0, 9, round_branch)
    plan.add(0, 9, cross_in_grad)
    for page in range(pages):
        plan.add(1 + page, 9, cross_attention, page)
        plan.add(8 + page, 11, self_attention, page)
    plan.add(8, 9, second_norm)
    plan.add(8, 9, self_in_grad)
    plan.add(9 + pages, 9, first_norm)
    for page in range(pages):
        for part in range(2):
            plan.add(12 + 2 * part, 9, memory_grad, page, part)
    for h in range(len(moves)):
        plan.add(total - 4 + h, 5, gain_step, h)
    plan.run()
    for i in range(total):
        if i >= total - SPARE:
            copies[i, 0][0].wait_send()
        if i >= total - RING:
            for stage in (1, 2, 3):
                for copy in copies[i, stage]:
                    copy.wait_send()
    for h in range(len(moves)):
        for copy in copies["gain", h]:
            copy.wait_send()
    need(*list(loads))


def backward(big, small, shapes):
    dp, fsdp = lax.axis_size("dp"), lax.axis_size("fsdp")
    n = dp // CORES
    depth = fsdp // n
    devices = dp * fsdp
    rows = WIDTH // devices
    pages, length, slots, live = shapes
    tokens = pages * length
    D = WIDTH
    t = sum(k * m for k, m in ((big[0].shape[1], D), (D, big[1].shape[1]), (D, 8 * D))) // (D * D)
    dma = pltpu.SemaphoreType.DMA
    hops = 2 * n + depth - 2
    outs = [(big[0].shape[1], D), (D, big[1].shape[1]), (D, D), (D, D), (D, 2 * D), (D, D), (D, 3 * D)]
    f32 = jnp.float32

    def scratch(*lead):
        return pltpu.VMEM(lead + (rows, WIDTH), jnp.bfloat16)

    def like(value):
        return pltpu.VMEM(value.shape, value.dtype)

    hbm = pl.BlockSpec(memory_space=pltpu.HBM)
    vmem = pl.BlockSpec(memory_space=pltpu.VMEM)
    smem = pl.BlockSpec(memory_space=pltpu.SMEM)
    return pl.pallas_call(
        functools.partial(back_kernel, (pages, length, slots)),
        out_shape=[jax.ShapeDtypeStruct((k // devices, m), f32) for k, m in outs]
        + [
            jax.ShapeDtypeStruct((8, D), f32),
            jax.ShapeDtypeStruct((tokens, D), f32),
            jax.ShapeDtypeStruct((pages * live * D // 128, 128), f32),
        ],
        in_specs=[hbm] * len(big) + [smem, smem] + [vmem] * 4,
        out_specs=[vmem] * (len(outs) + 2) + [hbm],
        scratch_shapes=[like(v) for v in big[:15]]
        + [pltpu.VMEM((D, 2 * D), jnp.bfloat16)] * 2
        + [pltpu.VMEM((tokens, D), jnp.bfloat16)] * 2
        + [
            pltpu.VMEM((2, -(-slots // 32) * 16 * 8, 128), f32),
            pltpu.VMEM((tokens, D), f32),
            scratch(SPARE, n, depth, n),
            scratch(RING, n, depth, n),
            scratch(RING, n, n, depth),
            scratch(t, n - 1, n, depth),
            scratch(RING, n, depth),
            scratch(t, n - 1, depth),
            scratch(RING, depth),
            scratch(t, depth - 1),
            pltpu.VMEM((4, 8, D), f32),
            pltpu.VMEM((hops, 8, D), f32),
            dma((20,)),
            dma((SPARE,)),
            dma((RING,)),
            dma((RING, n - 1)),
            dma((t, n - 1)),
            dma((RING, n - 1)),
            dma((t, n - 1)),
            dma((RING, depth - 1)),
            dma((t, depth - 1)),
            dma((hops,)),
            dma((hops,)),
            pltpu.SemaphoreType.REGULAR,
        ],
        compiler_params=pltpu.CompilerParams(
            collective_id=1, has_side_effects=True, vmem_limit_bytes=67043328
        ),
    )(*big, *small)


def per_device(
    hidden_in,
    memory,
    cotangent,
    lengths,
    memory_count,
    causal_gain,
    causal_query,
    causal_key,
    causal_value,
    causal_output,
    source_gain,
    source_query,
    source_key,
    source_value,
    source_output,
    dense_gain,
    dense_expand,
    dense_reduce,
):
    pages, _, rows, width = hidden_in.shape
    slots = memory.shape[2]
    pad = -slots % 16
    source = jnp.pad(memory[:, 0], ((0, 0), (0, pad), (0, 0)))

    def flat(value):
        return value.reshape(pages * value.shape[1], value.shape[2])

    gains = jnp.stack([causal_gain, source_gain, dense_gain], axis=1)
    gains = jnp.pad(gains, ((0, 0), (0, 125)))
    sources = [
        causal_query,
        causal_key,
        causal_value,
        causal_output,
        source_key,
        source_value,
        source_query,
        source_output,
        dense_expand,
        dense_reduce,
        gains,
    ]
    pieces = [(10, 0, 128, 5, 0, False)]
    pieces += [(k, 0, width, 0, k * width, False) for k in range(4)]
    pieces += [(4 + k, 0, width, 1, k * width, False) for k in range(2)]
    pieces += [(6 + k, 0, width, 2, k * width, False) for k in range(2)]
    pieces += [(8, k * width, width, 3, k * width, k < 3) for k in range(4)]
    pieces += [(9, k * BLOCK, BLOCK, 4, k * BLOCK, False) for k in range(4)]
    tokens = flat(hidden_in[:, 0])
    branch = flat(cotangent[:, 0])
    memory_rows = flat(source)
    page_length, page_count = lengths[:, 0], memory_count[:, 0]
    weights, saved, small = front(
        sources,
        pieces,
        [tokens, branch, memory_rows, page_count, page_length],
        (pages, rows, slots + pad),
    )
    self_weight, kv_weight, qo_weight, _, _, _ = weights
    result, hidden, pre, third, cross_grad, cctx, second, cq, kv, after_self, ctx, first, qkv = saved
    gain_rows, gain_three, lse_cross, lse_self = small
    big = [
        hidden,
        pre,
        third,
        branch,
        cross_grad,
        cctx,
        second,
        cq,
        kv,
        memory_rows,
        after_self,
        ctx,
        first,
        qkv,
        tokens,
        qo_weight,
        kv_weight,
        self_weight,
    ]
    small = [page_count, page_length, gain_rows, gain_three, lse_cross, lse_self]
    (
        grad_reduce,
        grad_expand,
        grad_source_output,
        grad_source_query,
        grad_source_both,
        grad_causal_output,
        grad_causal,
        grad_gains,
        grad_inputs,
        grad_memory,
    ) = backward(big, small, (pages, rows, slots + pad, slots))
    entries = causal_gain.shape[0]
    me = lax.axis_index("dp") * lax.axis_size("fsdp") + lax.axis_index("fsdp")
    grad_gains = lax.dynamic_slice_in_dim(grad_gains, me * entries, entries, axis=1)
    return (
        result.reshape(hidden_in.shape),
        grad_inputs.reshape(pages, 1, rows, width),
        grad_memory.reshape(memory.shape),
        grad_gains[0],
        grad_causal[:, :width],
        grad_causal[:, width : 2 * width],
        grad_causal[:, 2 * width :],
        grad_causal_output,
        grad_gains[1],
        grad_source_query,
        grad_source_both[:, :width],
        grad_source_both[:, width:],
        grad_source_output,
        grad_gains[2],
        grad_expand,
        grad_reduce,
    )


def solution(mesh):
    pages = P(None, AXES, None, None)
    counts = P(None, AXES)
    gain = P(AXES)
    weight = P(AXES, None)
    return jax.shard_map(
        per_device,
        mesh=mesh,
        in_specs=(pages, pages, pages, counts, counts)
        + (gain, weight, weight, weight, weight)
        + (gain, weight, weight, weight, weight)
        + (gain, weight, weight),
        out_specs=(pages, pages, pages)
        + (gain, weight, weight, weight, weight)
        + (gain, weight, weight, weight, weight)
        + (gain, weight, weight),
        check_vma=False,
    )
```

```python
import functools

import jax
import jax.numpy as jnp
from jax import lax
from jax.experimental import pallas as pl
from jax.experimental.pallas import tpu as pltpu
from jax.sharding import PartitionSpec as P

HD = 64
EPS = 1e-05
AXES = ("dp", "fsdp")
CORES = 2
WIDTH = 1024
BLOCK = 256
MESH = pl.DeviceIdType.MESH


class Grid:
    def __init__(self):
        dp, fsdp = lax.axis_size("dp"), lax.axis_size("fsdp")
        self.n = dp // CORES
        self.depth = fsdp // self.n
        self.devices = dp * fsdp
        d, f = lax.axis_index("dp"), lax.axis_index("fsdp")
        self.at = (d // CORES, d % CORES, f // self.n, f % self.n)

    def device(self, y, c, z, x):
        return (y * CORES + c, z * self.n + x)

    def step_z(self, k):
        y, c, z, x = self.at
        return self.device(y, c, lax.rem(z + k, self.depth), x)

    def step_plane(self, k, swap):
        y, c, z, x = self.at
        odd = lax.rem(c + swap, 2)
        return self.device(
            lax.rem(y + k * odd, self.n), c, z, lax.rem(x + k * (1 - odd), self.n)
        )

    def partner(self):
        y, c, z, x = self.at
        return self.device(y, 1 - c, z, x)

    def place(self, a, b):
        y, c, z, x = self.at
        ky = a * c + b * (1 - c)
        kx = a * (1 - c) + b * c
        return lax.rem(y + ky, self.n), lax.rem(x + kx, self.n)

    def peers(self):
        line = [self.step_z(k) for k in range(1, self.depth)]
        plane = [self.step_plane(k, s) for s in (0, 1) for k in range(1, self.n)]
        return line + plane + [self.partner()]

    def meet(self):
        barrier = pltpu.get_barrier_semaphore()
        peers = self.peers()
        for peer in peers:
            pl.semaphore_signal(barrier, inc=1, device_id=peer, device_id_type=MESH)
        pl.semaphore_wait(barrier, len(peers))


def remote(src, dst, send_sem, recv_sem, device):
    return pltpu.make_async_remote_copy(
        src_ref=src,
        dst_ref=dst,
        send_sem=send_sem,
        recv_sem=recv_sem,
        device_id=device,
        device_id_type=MESH,
    )


def started(*copy):
    made = remote(*copy)
    made.start()
    return made


class Plan:
    def __init__(self):
        self.calls = {}

    def add(self, tick, rank, call, *args):
        self.calls.setdefault((tick, rank), []).append((call, args))

    def run(self):
        for key in sorted(self.calls):
            for call, args in self.calls[key]:
                call(*args)


def times(left, right):
    return jnp.dot(left, right, preferred_element_type=jnp.float32)


def times_transposed(left, right):
    return lax.dot_general(left, right, (((1,), (1,)), ((), ())), preferred_element_type=jnp.float32)


def transposed_times(left, right):
    return lax.dot_general(left, right, (((0,), (0,)), ((), ())), preferred_element_type=jnp.float32)


def standardize(value):
    centred = value - jnp.mean(value, axis=-1, keepdims=True)
    spread = jnp.mean(centred * centred, axis=-1, keepdims=True)
    row_scale = lax.rsqrt(spread + EPS)
    return centred * row_scale, row_scale


def standardize_back(grad, unit, row_scale, gain):
    grad_unit = grad * gain
    inner = jnp.mean(grad_unit * unit, axis=-1, keepdims=True)
    return row_scale * (grad_unit - jnp.mean(grad_unit, axis=-1, keepdims=True) - unit * inner)


def lane_window(col, pair):
    return pl.ds(pl.multiple_of(col + pair * 2 * HD, 2 * HD), 2 * HD)


def both_heads(lane, value):
    zero = jnp.zeros_like(value)
    return jnp.concatenate(
        [jnp.where(lane < HD, value, zero), jnp.where(lane < HD, zero, value)], axis=0
    )


def causal(length, live):
    key = lax.broadcasted_iota(jnp.int32, (length, 2 * length), 0)
    query = lax.rem(lax.broadcasted_iota(jnp.int32, (length, 2 * length), 1), length)
    return (key <= query) & (key < live)


STRIP = 32


def strips(count, body, carry=None):
    def one(k, carry):
        return body(pl.ds(pl.multiple_of(k * STRIP, STRIP), STRIP), carry)

    return lax.fori_loop(0, count // STRIP, one, carry)


FLAT_AHEAD = 2
TALL_GAP = 2


def front_kernel(dims, chunks, names_, n_src, *refs):
    pages, length, slots = dims
    n_out = len(names_)
    it = iter(refs)

    def take(k):
        return [next(it) for _ in range(k)]

    shards = take(n_src)
    x_in, cot_in, memory_in, counts, lengths = take(5)
    outs = take(n_out)
    saved_out = take(13)
    gains, lse_cross, lse_self = take(3)
    saved = take(13)
    (result, hidden, pre, third, after_cross, cctx, second, cq, kv, after_self, ctx, first, qkv) = saved
    x_bf, cot, memory, w_a, w_b, w_d, w_gain, total_out, g_hidden = take(9)
    local, zs, zr, ps, pr, qs, qr, cs, cr, us, ur, ds, dr, loads_sem, stores_sem = take(15)
    f32, bf16 = jnp.float32, jnp.bfloat16
    grid = Grid()
    n, depth = grid.n, grid.depth
    y, c, z, x = grid.at
    tokens, D = x_bf.shape
    loads = {}

    def fetch(name, src, dst, slot):
        loads[name] = pltpu.make_async_copy(src, dst, loads_sem.at[slot])
        loads[name].start()

    def need(*names):
        for name in names:
            copy = loads.pop(name, None)
            if copy is not None:
                copy.wait()

    fetch("x", x_in, x_bf, 0)
    fetch("cot", cot_in, cot, 1)
    fetch("memory", memory_in, memory, 2)
    grid.meet()
    pending = []

    def send(*copy):
        made = started(*copy)
        pending.append(made)
        return made

    def window(i):
        _, r0, nr, c0, nc, _, o0, _ = chunks[i]
        return pl.ds(r0, nr), pl.ds(o0, nc)

    def out(i):
        return outs[chunks[i][5]]

    def shard(i):
        m, r0, nr, c0, nc, _, _, _ = chunks[i]
        return shards[m].at[pl.ds(r0, nr), pl.ds(c0, nc)]

    def block(i, yy, zz, xx):
        return out(i).at[(yy, c, zz, xx) + window(i)]

    def back(a, b):
        return grid.place((n - a) % n, (n - b) % n)

    def column(i, a, b):
        yy, xx = back(a, b)
        return out(i).at[(yy, c, slice(None), xx) + window(i)]

    def share(i, a, b):
        piece = column(i, a, b)
        slot = a * n + b
        return send(piece, piece, cs.at[i, slot], cr.at[i, slot], grid.partner())

    zc, pc, qc, cc, lc = {}, {}, {}, {}, {}

    def keep_own(i):
        lc[i] = pltpu.make_async_copy(shard(i), block(i, y, z, x), local.at[i])
        lc[i].start()

    def stage_z(i):
        zc[i] = [
            send(shard(i), block(i, y, z, x), zs.at[i, k - 1], zr.at[i, k - 1], grid.step_z(k))
            for k in range(1, depth)
        ]
        keep_own(i)

    def stage_p(i):
        for copy in zc[i]:
            copy.wait_recv()
        lc[i].wait()
        piece = column(i, 0, 0)
        pc[i] = [
            send(piece, piece, ps.at[i, a - 1], pr.at[i, a - 1], grid.step_plane(a, 0))
            for a in range(1, n)
        ]
        qc[i] = [
            send(piece, piece, qs.at[i, b - 1], qr.at[i, b - 1], grid.step_plane(b, 1))
            for b in range(1, n)
        ]
        cc[i] = [share(i, 0, 0)]

    def stage_q(i):
        for a in range(1, n):
            pc[i][a - 1].wait_recv()
            piece = column(i, a, 0)
            for b in range(1, n):
                j = a * (n - 1) + b - 1
                qc[i].append(
                    send(piece, piece, qs.at[i, j], qr.at[i, j], grid.step_plane(b, 1))
                )
            cc[i].append(share(i, a, 0))

    def stage_c(i):
        j = 0
        for a in range(n):
            for b in range(1, n):
                qc[i][j].wait_recv()
                j += 1
                cc[i].append(share(i, a, b))

    def tall_p(i):
        keep_own(i)
        pc[i] = [
            send(shard(i), block(i, y, z, x), ps.at[i, a - 1], pr.at[i, a - 1], grid.step_plane(a, 0))
            for a in range(1, n)
        ]

    def tall_q(i):
        lc[i].wait()
        qc[i] = []
        for a in range(n):
            if a:
                pc[i][a - 1].wait_recv()
            yy, xx = back(a, 0)
            piece = block(i, yy, z, xx)
            for b in range(1, n):
                j = a * (n - 1) + b - 1
                qc[i].append(
                    send(piece, piece, qs.at[i, j], qr.at[i, j], grid.step_plane(b, 1))
                )

    def layer(i, k, j):
        zz = lax.rem(z + (depth - j if k == 0 else j), depth)
        return out(i).at[(slice(None), c, zz, slice(None)) + window(i)]

    def hop(i, k, j):
        piece = layer(i, k, j)
        send_sem, recv_sem = ((us, ur), (ds, dr))[k]
        to = grid.device(y, c, lax.rem(z + (1 if k == 0 else depth - 1), depth), x)
        return remote(piece, piece, send_sem.at[i, j], recv_sem.at[i, j], to)

    def share_layer(i, k, j):
        piece = layer(i, k, j)
        slot = k * (depth - 1) + j
        return remote(piece, piece, cs.at[i, slot], cr.at[i, slot], grid.partner())

    def level(k):
        return z if k == 0 else depth - 1 - z

    def climb(i, j):
        if j == 0:
            for copy in qc[i]:
                copy.wait_recv()
            share_layer(i, 0, 0).start()
        for k in (0, 1):
            if j:

                @pl.when(level(k) >= j)
                def _():
                    hop(i, k, j - 1).wait_recv()
                    share_layer(i, k, j).start()

            if j < depth - 1:

                @pl.when((level(k) >= j) & (level(k) < depth - 1))
                def _():
                    hop(i, k, j).start()

    def each_layer(i, call, hops):
        call(share_layer(i, 0, 0))
        for k in (0, 1):
            for j in range(depth - 1):
                if hops:

                    @pl.when((level(k) >= j) & (level(k) < depth - 1))
                    def _():
                        call(hop(i, k, j))

                @pl.when(level(k) >= j + 1)
                def _():
                    call(share_layer(i, k, j + 1))

    there = set()

    def arrive(*ids):
        for i in ids:
            if i in there:
                continue
            there.add(i)
            if chunks[i][7]:
                each_layer(i, lambda copy: copy.wait_recv(), False)
            else:
                for copy in cc[i]:
                    copy.wait_recv()

    def pull(name, k, dst, slot):
        ids = held[name][k]
        arrive(*ids)
        fetch((name, k), out(ids[0]), dst, slot)

    def store(name, slot):
        src = saved[name]
        made = pltpu.make_async_copy(src, saved_out[name], stores_sem.at[slot])
        made.start()
        stores.append(made)

    stores = []
    lane = lax.broadcasted_iota(jnp.int32, (length, 2 * HD), 1)

    def attention(page, pair, q_ref, k_ref, k_row, k_rows, k_col, v_col, allowed, to, lse):
        q_at, k_at = pl.ds(page * length, length), pl.ds(k_row, k_rows)
        q = both_heads(lane, q_ref[q_at, lane_window(0, pair)])
        keys = k_ref[k_at, lane_window(k_col, pair)]
        values = k_ref[k_at, lane_window(v_col, pair)]
        scores = times_transposed(keys, q) * HD ** (-0.5)
        scores = jnp.where(allowed, scores, -1000000000.0)
        top = jnp.max(scores, axis=0, keepdims=True)
        expos = jnp.exp(scores - top)
        sum_ = jnp.sum(expos, axis=0, keepdims=True)
        probs = (expos * (1.0 / sum_)).astype(bf16)
        lse[pl.ds(page * (D // HD // 2) + pair, 1), :] = top + jnp.log(sum_)
        found = transposed_times(probs, values)
        to[q_at, lane_window(0, pair)] = jnp.where(lane < HD, found[:length], found[length:]).astype(bf16)

    def read_gains():
        arrive(*held["gain"][0])
        copy = pltpu.make_async_copy(out(held["gain"][0][0]), w_gain, loads_sem.at[3])
        copy.start()
        copy.wait()
        columns = w_gain.reshape(D, 128)[...].astype(f32)
        gains[...] = columns.T[:8]

    def project(left, weight, col, count, to, to_col):
        to[:, pl.ds(to_col, count)] = times(left[...], weight[:, pl.ds(col, count)]).astype(to.dtype)

    def first_norm():
        need("x")
        gain = gains[pl.ds(0, 1), :]

        def body(at, carry):
            unit, _ = standardize(x_bf[at].astype(f32))
            first[at] = (unit * gain).astype(bf16)
            return carry

        strips(tokens, body, 0)

    def self_project(k):
        need(("self", k))
        project(first, flat_b, k * D, D, qkv, k * D)

    def self_attention(page):
        allowed = causal(length, lengths[page])

        def body(pair, carry):
            attention(page, pair, qkv, qkv, page * length, length, D, 2 * D, allowed, ctx, lse_self)
            return carry

        lax.fori_loop(0, D // (2 * HD), body, 0, unroll=2)

    def residual(left, weight, col, base, to):
        to[...] = base[...].astype(f32) + times(left[...], weight[:, pl.ds(col, D)])

    def self_out():
        need(("self", 3))
        residual(ctx, flat_b, 3 * D, x_bf, after_self)
        gain = gains[pl.ds(1, 1), :]

        def body(at, carry):
            unit, _ = standardize(after_self[at])
            second[at] = (unit * gain).astype(bf16)
            return carry

        strips(tokens, body, 0)

    def memory_project(page, part):
        need("memory", ("kv", 0), ("kv", 1))
        span = -(-slots // 32) * 16
        at = pl.ds(page * slots + part * span, min(span, slots - part * span))

        def body(k, carry):
            col = pl.ds(pl.multiple_of(k * D, D), D)
            kv[at, col] = times(memory[at, :], flat_a[:, col]).astype(bf16)
            return carry

        lax.fori_loop(0, 2, body, 0)

    def cross_query():
        need(("qo", 0))
        project(second, flat_a, 0, D, cq, 0)

    def cross_attention(page, part):
        allowed = lax.broadcasted_iota(jnp.int32, (slots, 2 * length), 0) < counts[page]
        pairs = D // (2 * HD) // 2

        def body(k, carry):
            pair = part * pairs + k
            attention(page, pair, cq, kv, page * slots, slots, 0, D, allowed, cctx, lse_cross)
            return carry

        lax.fori_loop(0, pairs, body, 0, unroll=2)

    def cross_out():
        need(("qo", 1))
        residual(cctx, flat_a, D, after_self, after_cross)
        gain = gains[pl.ds(2, 1), :]

        def body(at, carry):
            unit, _ = standardize(after_cross[at])
            third[at] = (unit * gain).astype(bf16)
            return carry

        strips(tokens, body, 0)

    def hidden_grad(k):
        need("cot", ("reduce", 0))
        g_hidden[:, pl.ds(k * D, D)] = times_transposed(cot[...], flat_d[pl.ds(k * D, D), :])

    def expand(k):
        need(("expand", k))

        def body(j, carry):
            at = pl.ds(pl.multiple_of(k * D + j * 2 * BLOCK, BLOCK), 2 * BLOCK)
            value = times(third[...], flat_b[:, at])
            below = 0.5 + 0.5 * lax.erf(value * 0.5**0.5)
            hidden[:, at] = (value * below).astype(bf16)
            density = jnp.exp(-0.5 * value * value) * 0.3989422804014327
            pre[:, at] = (g_hidden[:, at] * (below + value * density)).astype(bf16)
            return carry

        lax.fori_loop(0, D // (2 * BLOCK), body, 0)

    def reduce_out(k):
        at = pl.ds(k * D, D)
        value = after_cross[...] if k == 0 else total_out[...]
        value = value + times(hidden[:, at], flat_d[at, :])
        if k < 3:
            total_out[...] = value
        else:
            result[...] = value.astype(bf16)

    flat_a, flat_b, flat_d = w_a.reshape(D, 2 * D), w_b.reshape(D, 4 * D), w_d.reshape(4 * D, D)

    held = {}
    for i, chunk in enumerate(chunks):
        name, k = names_[chunk[5]]
        held.setdefault(name, {}).setdefault(k, []).append(i)

    plan = Plan()
    flat = [i for i, chunk in enumerate(chunks) if not chunk[7]]
    tall = [i for i, chunk in enumerate(chunks) if chunk[7]]
    tick = {}
    for t, i in enumerate(flat):
        plan.add(t - FLAT_AHEAD, 0, stage_z, i)
        plan.add(t, 2, stage_p, i)
        plan.add(t + 1, 4, stage_q, i)
        plan.add(t + 2, 6, stage_c, i)
        tick[i] = t + 3
    for t, i in enumerate(tall):
        t = TALL_GAP * t - 1
        plan.add(t, 1, tall_p, i)
        plan.add(t + 2, 3, tall_q, i)
        for h in range(depth):
            plan.add(t + 4 + 2 * h, 5, climb, i, h)
        tick[i] = t + 4 + 2 * (depth - 1) + 1

    def ready(name, k):
        return max(tick[i] for i in held[name][k])

    def part(buffer, k, width):
        return buffer.at[:, :, :, :, :, pl.ds(k * width, width)]

    clock = [0]

    def then(when, call, *args):
        clock[0] = max(clock[0] + 1, 3 * when)
        plan.add(clock[0] // 3, 3 + 2 * (clock[0] % 3), call, *args)
        return clock[0] // 3

    def keep(*names):
        for name in names:
            store(name, name)

    plan.add(ready("gain", 0), 8, read_gains)
    plan.add(ready("gain", 0), 8, first_norm)
    for k in range(2):
        plan.add(ready("kv", k), 8, pull, "kv", k, part(w_a, k, D), 8 + k)
    for k in range(4):
        plan.add(ready("self", k), 8, pull, "self", k, part(w_b, k, D), 4 + k)
    for page in range(pages):
        for half in range(2):
            kv_done = then(ready("kv", 1) + 1, memory_project, page, half)
    for k in range(3):
        then(ready("self", k) + 1, self_project, k)
    for page in range(pages):
        then(0, self_attention, page)
    self_done = then(ready("self", 3) + 1, self_out)
    plan.add(self_done, 9, keep, 8, 10, 11, 12, 9, 6)
    for k in range(2):
        plan.add(max(ready("qo", k), kv_done + 1), 8, pull, "qo", k, part(w_a, k, D), 10 + k)
    for k in range(4):
        plan.add(
            max(ready("expand", k), self_done + 1), 8, pull, "expand", k, part(w_b, k, D), 12 + k
        )
    plan.add(ready("reduce", 0), 8, pull, "reduce", 0, w_d, 16)
    then(max(ready("qo", 0), kv_done + 1) + 1, cross_query)
    for page in range(pages):
        for half in range(2):
            then(0, cross_attention, page, half)
    cross_done = then(max(ready("qo", 1), kv_done + 1) + 1, cross_out)
    plan.add(cross_done, 9, keep, 3, 4, 5, 7)
    for k in range(4):
        then(ready("reduce", 0) + 1, hidden_grad, k)
    for k in range(4):
        then(max(ready("expand", k), self_done + 1) + 1, expand, k)
        last = then(0, reduce_out, k)
    plan.add(last, 10, keep, 1, 2, 0)
    plan.run()
    for i in flat:
        arrive(i)
    for i in tall:
        arrive(i)
        each_layer(i, lambda copy: copy.wait_send(), True)
    for copy in pending:
        copy.wait_send()
    for copy in stores:
        copy.wait()


def front(sources, pieces, names, tokens_in, shapes):
    dp, fsdp = lax.axis_size("dp"), lax.axis_size("fsdp")
    n = dp // CORES
    depth = fsdp // n
    rows = sources[0].shape[0]
    pages, length, slots = shapes
    tokens, D = pages * length, WIDTH
    groups = [(4 * rows if name == "reduce" else rows, 128 if name == "gain" else D) for name, _ in names]
    chunks = [(m, r0, rows, c0, groups[o][1], o, 0, tall) for m, r0, c0, o, tall in pieces]
    t = len(chunks)
    slot_count = max(n * n, 2 * depth - 1)
    shapes_ = (depth - 1, depth - 1, n - 1, n - 1, n * (n - 1), n * (n - 1), slot_count, slot_count)
    shapes_ += (depth - 1,) * 4
    dma = pltpu.SemaphoreType.DMA
    f32, bf16 = jnp.float32, jnp.bfloat16
    lead = (n, CORES, depth, n)
    saved = [
        ((tokens, D), bf16),
        ((tokens, 4 * D), bf16),
        ((tokens, 4 * D), bf16),
        ((tokens, D), bf16),
        ((tokens, D), f32),
        ((tokens, D), bf16),
        ((tokens, D), bf16),
        ((tokens, D), bf16),
        ((pages * slots, 2 * D), bf16),
        ((tokens, D), f32),
        ((tokens, D), bf16),
        ((tokens, D), bf16),
        ((tokens, 3 * D), bf16),
    ]
    small = [((8, D), f32)] + [((pages * D // HD // 2, 2 * length), f32)] * 2
    hbm = pl.BlockSpec(memory_space=pltpu.HBM)
    vmem = pl.BlockSpec(memory_space=pltpu.VMEM)
    smem = pl.BlockSpec(memory_space=pltpu.SMEM)
    found = pl.pallas_call(
        functools.partial(front_kernel, shapes, chunks, names, len(sources)),
        out_shape=[jax.ShapeDtypeStruct(lead + g, bf16) for g in groups]
        + [jax.ShapeDtypeStruct(*s) for s in saved + small],
        in_specs=[vmem] * len(sources) + [hbm] * 3 + [smem] * 2,
        out_specs=[hbm] * (len(groups) + len(saved)) + [vmem] * 3,
        scratch_shapes=[pltpu.VMEM(*s) for s in saved]
        + [
            pltpu.VMEM((tokens, D), bf16),
            pltpu.VMEM((tokens, D), bf16),
            pltpu.VMEM((pages * slots, D), bf16),
            pltpu.VMEM(lead + (rows, 2 * D), bf16),
            pltpu.VMEM(lead + (rows, 4 * D), bf16),
            pltpu.VMEM(lead + (4 * rows, D), bf16),
            pltpu.VMEM(lead + (rows, 128), bf16),
            pltpu.VMEM((tokens, D), f32),
            pltpu.VMEM((tokens, 4 * D), f32),
            dma((t,)),
        ]
        + [dma((t, k)) for k in shapes_]
        + [dma((20,)), dma((13,))],
        compiler_params=pltpu.CompilerParams(
            collective_id=0, has_side_effects=True, vmem_limit_bytes=67043328
        ),
    )(*sources, *tokens_in)
    weights = [
        w.reshape(dp * fsdp * g[0], g[1]) for w, g in zip(found[: len(groups)], groups)
    ]
    return weights, found[len(groups) : len(groups) + len(saved)], found[len(groups) + len(saved) :]


RING = 4
KEPT = (("self", 4), ("kv", 2), ("qo", 2), ("expand", 4))
SPARE = 2


def back_kernel(dims, *refs):
    pages, length, slots = dims
    it = iter(refs)

    def take(k):
        return [next(it) for _ in range(k)]

    (hidden_in, pre_in, third_in, out_in, cross_in, cctx_in, second_in, cq_in, kv_in, memory_in,
     self_in, ctx_in, first_in, qkv_in, x_in) = take(15)
    kept = {name: take(count) for name, count in KEPT}
    counts, lengths, gains, lse_cross, lse_self = take(5)
    grad_outs = take(7)
    gain_out, input_out, memory_out = take(3)
    (hidden, pre, third, out_grad, cross, cctx, second, cq, kv, memory, after_self, ctx, first, qkv, x_bf,
     w_a, w_b, branch, g_ctx, stage, g_norm) = take(21)
    send0, got0, parts, got1, halves, got2, line, got3, gain_sum, gain_got = take(10)
    local, s0, r0, s1, r1, s2, r2, s3, r3, gs, gr, free = take(12)

    grid = Grid()
    n, depth = grid.n, grid.depth
    y, c, z, x = grid.at
    rows, width = send0.shape[-2:]
    f32, bf16 = jnp.float32, jnp.bfloat16
    copies, loads = {}, {}

    def fetch(name, src, dst, slot):
        loads[name] = pltpu.make_async_copy(src, dst, local.at[slot])
        loads[name].start()

    def need(*names):
        for name in names:
            copy = loads.pop(name, None)
            if copy is not None:
                copy.wait()

    D = x_bf.shape[1]
    fetch("hidden", hidden_in, hidden, 0)
    fetch("out", out_in, out_grad, 1)
    fetch("pre", pre_in, pre, 2)
    fetch("third", third_in, third, 3)

    def weights(label, *moves):
        for name, k, buffer, half in moves:
            slot = 15 + half + (0 if buffer is w_a else 2)
            fetch((label, slot), kept[name][k], buffer.at[:, pl.ds(half * D, D)], slot)

    def need_all(label):
        need(*[key for key in list(loads) if key[0] == label])

    weights("expand", *[("expand", k, (w_a, w_b)[k // 2], k % 2) for k in range(4)])
    fetch("cross", cross_in, cross, 4)
    grid.meet()
    fetch("cctx", cctx_in, cctx, 5)
    fetch("cq", cq_in, cq, 7)
    fetch("kv", kv_in, kv, 8)
    fetch("second", second_in, second, 6)
    fetch("memory", memory_in, memory, 9)
    fetch("self", self_in, after_self, 10)
    fetch("ctx", ctx_in, ctx, 11)
    fetch("first", first_in, first, 12)
    fetch("qkv", qkv_in, qkv, 13)
    fetch("x", x_in, x_bf, 14)

    chunks = []
    wide = hidden.shape[1] // grid.devices
    for col in range(0, D, width * rows // wide):
        chunks.append((0, hidden, out_grad, col, ("hidden", "out")))
    for col in range(0, pre.shape[1], width):
        chunks.append((1, third, pre, col, ("third", "pre")))
    chunks.append((2, cctx, branch, 0, ("cctx",)))
    chunks.append((3, second, cq, 0, ("second",)))
    chunks.append((4, memory, kv, 0, ("memory",)))
    chunks.append((4, memory, kv, D, ()))
    chunks.append((5, ctx, branch, 0, ("ctx",)))
    for col in range(0, 3 * D, width):
        chunks.append((6, first, qkv, col, ("first",)))
    total = len(chunks)

    def products(i, core, emit):
        _, left, right, col, names = chunks[i]
        need(*names)
        own = left.shape[1] // grid.devices
        span = left.shape[1] // (n * CORES)
        lanes = width * rows // own

        def body(yy, carry):
            at = pl.multiple_of((yy * CORES + core) * span, min(span, BLOCK))
            value = lax.dot_general(
                left[:, pl.ds(at, span)],
                right[:, pl.ds(col, lanes)],
                (((0,), (0,)), ((), ())),
                preferred_element_type=f32,
            )
            for k in range(depth * n):
                for part in range(own // rows):
                    top = k * own + part * rows
                    emit(yy, k // n, k % n, part * lanes, lanes, value[top : top + rows])
            return carry

        lax.fori_loop(0, n, body, 0)

    def reuse(i, stage, ring):
        if i >= ring:
            for copy in copies[i - ring, stage]:
                copy.wait_send()

    def stage0(i):
        s = i % SPARE
        reuse(i, 0, SPARE)

        def emit(yy, zz, xx, lane, lanes, value):
            send0[s, yy, zz, xx, :, pl.ds(lane, lanes)] = value.astype(bf16)

        products(i, 1 - c, emit)
        if i >= RING:
            pl.semaphore_wait(free, 1)
        copies[i, 0] = [started(send0.at[s], got0.at[i % RING], s0.at[s], r0.at[i % RING], grid.partner())]

    def stage1(i):
        s = i % RING
        reuse(i, 1, RING)
        copies[i, 0][0].wait_recv()

        def emit(yy, zz, xx, lane, lanes, value):
            value = value + got0[s, yy, zz, xx, :, pl.ds(lane, lanes)].astype(f32)
            to_y = lax.rem(yy - y + n, n)
            to_x = lax.rem(xx - x + n, n)
            a = to_x * (1 - c) + to_y * c
            b = to_y * (1 - c) + to_x * c
            parts[s, a, b, zz, :, pl.ds(lane, lanes)] = value.astype(bf16)

        products(i, c, emit)
        if i + RING < total:
            pl.semaphore_signal(free, inc=1, device_id=grid.partner(), device_id_type=MESH)
        copies[i, 1] = [
            started(
                parts.at[s, a],
                got1.at[i, a - 1],
                s1.at[s, a - 1],
                r1.at[i, a - 1],
                grid.step_plane(a, 0),
            )
            for a in range(1, n)
        ]

    def stage2(i):
        s = i % RING
        reuse(i, 2, RING)
        for copy in copies[i, 1]:
            copy.wait_recv()
        copies[i, 2] = []
        for b in list(range(1, n)) + [0]:

            def body(zz, carry):
                value = parts[s, 0, b, zz].astype(f32)
                for a in range(1, n):
                    value = value + got1[i, a - 1, b, zz].astype(f32)
                halves[s, b, zz] = value.astype(bf16)
                return carry

            lax.fori_loop(0, depth, body, 0)
            if b:
                copies[i, 2].append(
                    started(
                        halves.at[s, b],
                        got2.at[i, b - 1],
                        s2.at[s, b - 1],
                        r2.at[i, b - 1],
                        grid.step_plane(b, 1),
                    )
                )

    def stage3(i):
        s = i % RING
        reuse(i, 3, RING)
        for copy in copies[i, 2]:
            copy.wait_recv()

        def body(zz, carry):
            value = halves[s, 0, zz].astype(f32)
            for b in range(1, n):
                value = value + got2[i, b - 1, zz].astype(f32)
            line[s, zz] = value.astype(bf16)
            return carry

        lax.fori_loop(0, depth, body, 0)
        copies[i, 3] = [
            started(
                line.at[s, lax.rem(z + k, depth)],
                got3.at[i, k - 1],
                s3.at[s, k - 1],
                r3.at[i, k - 1],
                grid.step_z(k),
            )
            for k in range(1, depth)
        ]

    def stage4(i):
        m, left, _, col, _ = chunks[i]
        for copy in copies[i, 3]:
            copy.wait_recv()
        value = line[i % RING, z].astype(f32)
        for k in range(1, depth):
            value = value + got3[i, k - 1].astype(f32)
        own = left.shape[1] // grid.devices
        if own == rows:
            grad_outs[m][:, pl.ds(col, width)] = value
        else:
            for part in range(own // rows):
                grad_outs[m][pl.ds(part * rows, rows), pl.ds(col, BLOCK)] = value[
                    :, part * BLOCK : (part + 1) * BLOCK
                ]

    moves = [
        [grid.partner()],
        [grid.step_plane(a, 0) for a in range(1, n)],
        [grid.step_plane(a, 1) for a in range(1, n)],
        [grid.step_z(k) for k in range(1, depth)],
        [],
    ]
    start = [0, 1, n, 2 * n - 1, 2 * n + depth - 2]

    def gain_step(h):
        value = gain_sum[min(h, 3)]
        if h:
            for j, copy in enumerate(copies["gain", h - 1]):
                copy.wait_recv()
                value = value + gain_got[start[h - 1] + j]
        if h == len(moves) - 1:
            gain_out[...] = value
        elif h:
            gain_sum[h] = value
        if h < len(moves) - 2:
            gain_sum[h + 1] = value
        copies["gain", h] = [
            started(
                gain_sum.at[h],
                gain_got.at[start[h] + j],
                gs.at[start[h] + j],
                gr.at[start[h] + j],
                device,
            )
            for j, device in enumerate(moves[h])
        ]

    def context_grad(weight, col):
        g_ctx[...] = times_transposed(branch[...], weight[:, pl.ds(col, D)]).astype(bf16)

    lane = lax.broadcasted_iota(jnp.int32, (length, 2 * HD), 1)
    scale = HD ** (-0.5)

    def attention(page, pair, q_ref, q_col, k_ref, k_row, k_rows, k_col, v_col, lse, allowed):
        q_at = pl.ds(page * length, length)
        k_at = pl.ds(k_row, k_rows)
        q = both_heads(lane, q_ref[q_at, lane_window(q_col, pair)])
        g = both_heads(lane, g_ctx[q_at, lane_window(0, pair)])
        keys, values = k_ref[k_at, lane_window(k_col, pair)], k_ref[k_at, lane_window(v_col, pair)]
        scores = times_transposed(keys, q) * scale
        scores = jnp.where(allowed, scores, -1000000000.0)
        probs = jnp.exp(scores - lse[pl.ds(page * (D // HD // 2) + pair, 1), :])
        g_probs = times_transposed(values, g)
        inner = jnp.sum(probs * g_probs, axis=0, keepdims=True)
        g_scores = (probs * (g_probs - inner)).astype(bf16)
        g_values = times(probs.astype(bf16), g)
        g_keys = times(g_scores, q) * scale
        g_q = transposed_times(g_scores, keys)
        g_q = jnp.where(lane < HD, g_q[:length], g_q[length:]) * scale
        q_ref[q_at, lane_window(q_col, pair)] = g_q.astype(bf16)
        k_ref[k_at, lane_window(k_col, pair)] = g_keys.astype(bf16)
        k_ref[k_at, lane_window(v_col, pair)] = g_values.astype(bf16)

    def cross_attention(page):
        need("cq", "kv")
        place = lax.broadcasted_iota(jnp.int32, (slots, 2 * length), 0)
        allowed = place < counts[page]

        def body(pair, carry):
            attention(page, pair, cq, 0, kv, page * slots, slots, 0, D, lse_cross, allowed)
            return carry

        lax.fori_loop(0, D // (2 * HD), body, 0, unroll=2)

    def self_attention(page):
        need("qkv")
        allowed = causal(length, lengths[page])

        def body(pair, carry):
            attention(page, pair, qkv, 0, qkv, page * length, length, D, 2 * D, lse_self, allowed)
            return carry

        lax.fori_loop(0, D // (2 * HD), body, 0, unroll=2)

    def norm_back(value_ref, gain_row, put):
        gain = gains[pl.ds(gain_row, 1), :]

        def body(k, total_):
            at = pl.ds(k * 32, 32)
            value = value_ref[at].astype(f32)
            centred = value - jnp.mean(value, axis=-1, keepdims=True)
            spread = jnp.mean(centred * centred, axis=-1, keepdims=True)
            row_scale = lax.rsqrt(spread + EPS)
            unit = centred * row_scale
            grad = g_norm[at]
            grad_unit = grad * gain
            inner = jnp.mean(grad_unit * unit, axis=-1, keepdims=True)
            put(at, row_scale * (grad_unit - jnp.mean(grad_unit, axis=-1, keepdims=True) - unit * inner))
            return total_ + jnp.sum(grad * unit, axis=0, keepdims=True)

        summed = lax.fori_loop(0, value_ref.shape[0] // 32, body, jnp.zeros((1, D), f32))
        gain_sum[0, pl.ds(gain_row, 1), :] = summed

    def spread(terms):
        def body(k, carry):
            at = pl.ds(pl.multiple_of(k * 2 * BLOCK, BLOCK), 2 * BLOCK)
            value = None
            for left, left_col, right, right_col in terms:
                term = times_transposed(
                    left[:, pl.ds(left_col, D)], right[at, pl.ds(right_col, D)]
                )
                value = term if value is None else value + term
            g_norm[:, at] = value
            return carry

        lax.fori_loop(0, D // (2 * BLOCK), body, 0)

    def third_norm():
        need("pre", "out", "cross")
        need_all("expand")
        spread([(pre, 0, w_a, 0), (pre, D, w_a, D), (pre, 2 * D, w_b, 0), (pre, 3 * D, w_b, D)])

        def put(at, value):
            value = out_grad[at].astype(f32) + value
            cross[at] = value
            branch[at] = value.astype(bf16)

        norm_back(cross, 2, put)
        weights("qo", ("qo", 1, w_a, 1), ("qo", 0, w_a, 0))
        weights("self", ("self", 3, w_b, 0), ("self", 0, w_b, 1))

    def second_norm():
        need("self")
        spread([(cq, 0, w_a, 0)])

        def put(at, value):
            value = cross[at] + value
            cross[at] = value
            branch[at] = value.astype(bf16)

        norm_back(after_self, 1, put)
        weights("pair", ("self", 1, w_a, 0), ("self", 2, w_a, 1))

    def first_norm():
        need("x")
        need_all("pair")
        spread([(qkv, 0, w_b, D), (qkv, D, w_a, 0), (qkv, 2 * D, w_a, D)])

        def put(at, value):
            input_out[at] = cross[at] + value

        norm_back(x_bf, 0, put)
        weights("kv", ("kv", 0, w_b, 0), ("kv", 1, w_b, 1))

    def memory_grad(page, part):
        need_all("kv")
        slot = part % 2
        need(("stage", slot))
        top = part * span
        height = min(slots - top, span)
        live = min(memory_rows - top, height)
        at = pl.ds(page * slots + top, height)

        def body(k, carry):
            col = pl.multiple_of(k * BLOCK, BLOCK)
            value = times_transposed(kv[at, :], w_b[pl.ds(col, BLOCK), :])
            for j in range(BLOCK // 128):
                stage[slot, pl.ds(k * (BLOCK // 128) + j, live, 8), :] = value[:live, j * 128 : j * 128 + 128]
            return carry

        lax.fori_loop(0, D // BLOCK, body, 0)
        fetch(
            ("stage", slot),
            stage.at[slot, pl.ds(0, live * 8)],
            memory_out.at[pl.ds((page * memory_rows + top) * 8, live * 8)],
            19 + slot,
        )

    span = -(-slots // 32) * 16
    memory_rows = memory_out.shape[0] // 8 // pages
    gain_sum[0] = jnp.zeros(gain_sum.shape[1:], f32)
    plan = Plan()
    for i in range(total):
        plan.add(i - 2, 0, stage0, i)
        plan.add(i, 1, stage1, i)
        plan.add(i + 1, 2, stage2, i)
        plan.add(i + 2, 3, stage3, i)
        plan.add(i + 3, 4, stage4, i)

    def cross_in_grad():
        need_all("qo")
        context_grad(w_a, D)

    def self_in_grad():
        need_all("self")
        context_grad(w_b, 0)

    plan.add(0, 9, third_norm)
    plan.add(1, 9, cross_in_grad)
    for page in range(pages):
        plan.add(1 + page, 10, cross_attention, page)
        plan.add(8 + page, 11, self_attention, page)
    plan.add(8, 9, second_norm)
    plan.add(8, 9, self_in_grad)
    plan.add(9 + pages, 9, first_norm)
    for page in range(pages):
        for part in range(2):
            plan.add(12 + 2 * part, 9, memory_grad, page, part)
    for h in range(len(moves)):
        plan.add(total - 4 + h, 5, gain_step, h)
    plan.run()
    for i in range(total):
        if i >= total - SPARE:
            copies[i, 0][0].wait_send()
        if i >= total - RING:
            for stage in (1, 2, 3):
                for copy in copies[i, stage]:
                    copy.wait_send()
    for h in range(len(moves)):
        for copy in copies["gain", h]:
            copy.wait_send()
    need(*list(loads))


def backward(big, small, shapes):
    dp, fsdp = lax.axis_size("dp"), lax.axis_size("fsdp")
    n = dp // CORES
    depth = fsdp // n
    devices = dp * fsdp
    rows = WIDTH // devices
    pages, length, slots, live = shapes
    tokens = pages * length
    D = WIDTH
    t = sum(k * m for k, m in ((big[0].shape[1], D), (D, big[1].shape[1]), (D, 8 * D))) // (D * D)
    dma = pltpu.SemaphoreType.DMA
    hops = 2 * n + depth - 2
    outs = [(big[0].shape[1], D), (D, big[1].shape[1]), (D, D), (D, D), (D, 2 * D), (D, D), (D, 3 * D)]
    f32 = jnp.float32

    def scratch(*lead):
        return pltpu.VMEM(lead + (rows, WIDTH), jnp.bfloat16)

    def like(value):
        return pltpu.VMEM(value.shape, value.dtype)

    hbm = pl.BlockSpec(memory_space=pltpu.HBM)
    vmem = pl.BlockSpec(memory_space=pltpu.VMEM)
    smem = pl.BlockSpec(memory_space=pltpu.SMEM)
    return pl.pallas_call(
        functools.partial(back_kernel, (pages, length, slots)),
        out_shape=[jax.ShapeDtypeStruct((k // devices, m), f32) for k, m in outs]
        + [
            jax.ShapeDtypeStruct((8, D), f32),
            jax.ShapeDtypeStruct((tokens, D), f32),
            jax.ShapeDtypeStruct((pages * live * D // 128, 128), f32),
        ],
        in_specs=[hbm] * len(big) + [smem, smem] + [vmem] * 3,
        out_specs=[vmem] * (len(outs) + 2) + [hbm],
        scratch_shapes=[like(v) for v in big[:15]]
        + [pltpu.VMEM((D, 2 * D), jnp.bfloat16)] * 2
        + [pltpu.VMEM((tokens, D), jnp.bfloat16)] * 2
        + [
            pltpu.VMEM((2, -(-slots // 32) * 16 * 8, 128), f32),
            pltpu.VMEM((tokens, D), f32),
            scratch(SPARE, n, depth, n),
            scratch(RING, n, depth, n),
            scratch(RING, n, n, depth),
            scratch(t, n - 1, n, depth),
            scratch(RING, n, depth),
            scratch(t, n - 1, depth),
            scratch(RING, depth),
            scratch(t, depth - 1),
            pltpu.VMEM((4, 8, D), f32),
            pltpu.VMEM((hops, 8, D), f32),
            dma((21,)),
            dma((SPARE,)),
            dma((RING,)),
            dma((RING, n - 1)),
            dma((t, n - 1)),
            dma((RING, n - 1)),
            dma((t, n - 1)),
            dma((RING, depth - 1)),
            dma((t, depth - 1)),
            dma((hops,)),
            dma((hops,)),
            pltpu.SemaphoreType.REGULAR,
        ],
        compiler_params=pltpu.CompilerParams(
            collective_id=1, has_side_effects=True, vmem_limit_bytes=67043328
        ),
    )(*big, *small)


def hand_kernel(slabs, count, *refs):
    ins, gains = refs[:count], refs[count]
    outs, gain_outs = refs[count + 1 : 2 * count + 1], refs[2 * count + 1 : 2 * count + 4]
    buffers = refs[2 * count + 4 : 3 * count + 4]
    loaded, stored = refs[3 * count + 4 :]
    copies = []
    for k, (m, first, rows) in enumerate(slabs):
        at = pl.ds(first, rows)
        load = pltpu.make_async_copy(ins[m].at[at], buffers[m].at[at], loaded.at[k])
        load.start()
        copies.append((load, pltpu.make_async_copy(buffers[m].at[at], outs[m].at[at], stored.at[k])))
    entries = gain_outs[0].shape[-1]
    me = lax.axis_index("dp") * lax.axis_size("fsdp") + lax.axis_index("fsdp")
    turned = pltpu.roll(gains[...], lax.rem(gains.shape[1] - me * entries, gains.shape[1]), 1)
    for k, gain_out in enumerate(gain_outs):
        gain_out[...] = turned[k : k + 1, :entries]
    for load, store in copies:
        load.wait()
        store.start()
    for _, store in copies:
        store.wait()


def hand_over(arrays, gains):
    devices = lax.axis_size("dp") * lax.axis_size("fsdp")
    entries = gains.shape[1] // devices
    slabs = []
    for m, value in enumerate(arrays):
        parts = 4 if value.shape[0] % 64 == 0 and value.size >= 1 << 20 else 1
        rows = value.shape[0] // parts
        slabs += [(m, k * rows, rows) for k in range(parts)]
    hbm = pl.BlockSpec(memory_space=pltpu.HBM)
    vmem = pl.BlockSpec(memory_space=pltpu.VMEM)
    dma = pltpu.SemaphoreType.DMA
    found = pl.pallas_call(
        functools.partial(hand_kernel, slabs, len(arrays)),
        out_shape=[jax.ShapeDtypeStruct(v.shape, v.dtype) for v in arrays]
        + [jax.ShapeDtypeStruct((1, entries), gains.dtype)] * 3,
        in_specs=[hbm] * len(arrays) + [vmem],
        out_specs=[hbm] * len(arrays) + [vmem] * 3,
        scratch_shapes=[pltpu.VMEM(v.shape, v.dtype) for v in arrays]
        + [dma((len(slabs),)), dma((len(slabs),))],
        compiler_params=pltpu.CompilerParams(vmem_limit_bytes=67043328),
    )(*arrays, gains)
    return found[:-3], [v.reshape(-1) for v in found[-3:]]


def per_device(
    hidden_in,
    memory,
    cotangent,
    lengths,
    memory_count,
    causal_gain,
    causal_query,
    causal_key,
    causal_value,
    causal_output,
    source_gain,
    source_query,
    source_key,
    source_value,
    source_output,
    dense_gain,
    dense_expand,
    dense_reduce,
):
    pages, _, rows, width = hidden_in.shape
    slots = memory.shape[2]
    pad = -slots % 16
    source = jnp.pad(memory[:, 0], ((0, 0), (0, pad), (0, 0)))

    def flat(value):
        return value.reshape(pages * value.shape[1], value.shape[2])

    gains = jnp.stack([causal_gain, source_gain, dense_gain], axis=1)
    gains = jnp.pad(gains, ((0, 0), (0, 125)))
    sources = [
        causal_query,
        causal_key,
        causal_value,
        causal_output,
        source_key,
        source_value,
        source_query,
        source_output,
        dense_expand,
        dense_reduce,
        gains,
    ]
    names = [("gain", 0)]
    pieces = [(10, 0, 0, 0, False)]
    for first, count, name in ((4, 2, "kv"), (0, 4, "self"), (6, 2, "qo")):
        for k in range(count):
            pieces.append((first + k, 0, 0, len(names), False))
            names.append((name, k))
    for k in range(4):
        pieces.append((9, k * causal_query.shape[0], 0, len(names), k < 3))
    names.append(("reduce", 0))
    for k in range(4):
        pieces.append((8, 0, k * width, len(names), False))
        names.append(("expand", k))
    tokens = flat(hidden_in[:, 0])
    branch = flat(cotangent[:, 0])
    memory_rows = flat(source)
    page_length, page_count = lengths[:, 0], memory_count[:, 0]
    weights, saved, small = front(
        sources,
        pieces,
        names,
        [tokens, branch, memory_rows, page_count, page_length],
        (pages, rows, slots + pad),
    )
    result, hidden, pre, third, after_cross, cctx, second, cq, kv, after_self, ctx, first, qkv = saved
    gain_rows, lse_cross, lse_self = small
    big = [
        hidden,
        pre,
        third,
        branch,
        after_cross,
        cctx,
        second,
        cq,
        kv,
        memory_rows,
        after_self,
        ctx,
        first,
        qkv,
        tokens,
    ]
    place = {name: weight for name, weight in zip(names, weights)}
    big += [place[name, k] for name, count in KEPT for k in range(count)]
    small = [page_count, page_length, gain_rows, lse_cross, lse_self]
    (
        grad_reduce,
        grad_expand,
        grad_source_output,
        grad_source_query,
        grad_source_both,
        grad_causal_output,
        grad_causal,
        grad_gains,
        grad_inputs,
        grad_memory,
    ) = backward(big, small, (pages, rows, slots + pad, slots))
    (
        result,
        grad_inputs,
        grad_memory,
        grad_reduce,
        grad_expand,
        grad_source_output,
        grad_source_query,
        grad_source_both,
        grad_causal_output,
        grad_causal,
    ), grad_gains = hand_over(
        [
            result,
            grad_inputs,
            grad_memory,
            grad_reduce,
            grad_expand,
            grad_source_output,
            grad_source_query,
            grad_source_both,
            grad_causal_output,
            grad_causal,
        ],
        grad_gains,
    )
    return (
        result.reshape(hidden_in.shape),
        grad_inputs.reshape(pages, 1, rows, width),
        grad_memory.reshape(memory.shape),
        grad_gains[0],
        grad_causal[:, :width],
        grad_causal[:, width : 2 * width],
        grad_causal[:, 2 * width :],
        grad_causal_output,
        grad_gains[1],
        grad_source_query,
        grad_source_both[:, :width],
        grad_source_both[:, width:],
        grad_source_output,
        grad_gains[2],
        grad_expand,
        grad_reduce,
    )


def solution(mesh):
    pages = P(None, AXES, None, None)
    counts = P(None, AXES)
    gain = P(AXES)
    weight = P(AXES, None)
    return jax.shard_map(
        per_device,
        mesh=mesh,
        in_specs=(pages, pages, pages, counts, counts)
        + (gain, weight, weight, weight, weight)
        + (gain, weight, weight, weight, weight)
        + (gain, weight, weight),
        out_specs=(pages, pages, pages)
        + (gain, weight, weight, weight, weight)
        + (gain, weight, weight, weight, weight)
        + (gain, weight, weight),
        check_vma=False,
    )
```

```python
import functools

import jax
import jax.numpy as jnp
from jax import lax
from jax.experimental import pallas as pl
from jax.experimental.pallas import tpu as pltpu
from jax.sharding import PartitionSpec as P

HD = 64
EPS = 1e-05
AXES = ("dp", "fsdp")
CORES = 2
WIDTH = 1024
BLOCK = 256
MESH = pl.DeviceIdType.MESH


class Grid:
    def __init__(self):
        dp, fsdp = lax.axis_size("dp"), lax.axis_size("fsdp")
        self.n = dp // CORES
        self.depth = fsdp // self.n
        self.devices = dp * fsdp
        d, f = lax.axis_index("dp"), lax.axis_index("fsdp")
        self.at = (d // CORES, d % CORES, f // self.n, f % self.n)

    def device(self, y, c, z, x):
        return (y * CORES + c, z * self.n + x)

    def step_z(self, k):
        y, c, z, x = self.at
        return self.device(y, c, lax.rem(z + k, self.depth), x)

    def step_plane(self, k, swap):
        y, c, z, x = self.at
        odd = lax.rem(c + swap, 2)
        return self.device(
            lax.rem(y + k * odd, self.n), c, z, lax.rem(x + k * (1 - odd), self.n)
        )

    def partner(self):
        y, c, z, x = self.at
        return self.device(y, 1 - c, z, x)

    def place(self, a, b):
        y, c, z, x = self.at
        ky = a * c + b * (1 - c)
        kx = a * (1 - c) + b * c
        return lax.rem(y + ky, self.n), lax.rem(x + kx, self.n)

    def peers(self):
        line = [self.step_z(k) for k in range(1, self.depth)]
        plane = [self.step_plane(k, s) for s in (0, 1) for k in range(1, self.n)]
        return line + plane + [self.partner()]

    def meet(self):
        barrier = pltpu.get_barrier_semaphore()
        peers = self.peers()
        for peer in peers:
            pl.semaphore_signal(barrier, inc=1, device_id=peer, device_id_type=MESH)
        pl.semaphore_wait(barrier, len(peers))


def remote(src, dst, send_sem, recv_sem, device):
    return pltpu.make_async_remote_copy(
        src_ref=src,
        dst_ref=dst,
        send_sem=send_sem,
        recv_sem=recv_sem,
        device_id=device,
        device_id_type=MESH,
    )


def started(*copy):
    made = remote(*copy)
    made.start()
    return made


class Plan:
    def __init__(self):
        self.calls = {}

    def add(self, tick, rank, call, *args):
        self.calls.setdefault((tick, rank), []).append((call, args))

    def run(self):
        for key in sorted(self.calls):
            for call, args in self.calls[key]:
                call(*args)


def times(left, right):
    return jnp.dot(left, right, preferred_element_type=jnp.float32)


def times_transposed(left, right):
    return lax.dot_general(left, right, (((1,), (1,)), ((), ())), preferred_element_type=jnp.float32)


def transposed_times(left, right):
    return lax.dot_general(left, right, (((0,), (0,)), ((), ())), preferred_element_type=jnp.float32)


def standardize(value):
    centred = value - jnp.mean(value, axis=-1, keepdims=True)
    spread = jnp.mean(centred * centred, axis=-1, keepdims=True)
    row_scale = lax.rsqrt(spread + EPS)
    return centred * row_scale, row_scale


def standardize_back(grad, unit, row_scale, gain):
    grad_unit = grad * gain
    inner = jnp.mean(grad_unit * unit, axis=-1, keepdims=True)
    return row_scale * (grad_unit - jnp.mean(grad_unit, axis=-1, keepdims=True) - unit * inner)


def lane_window(col, pair):
    return pl.ds(pl.multiple_of(col + pair * 2 * HD, 2 * HD), 2 * HD)


def both_heads(lane, value):
    zero = jnp.zeros_like(value)
    return jnp.concatenate(
        [jnp.where(lane < HD, value, zero), jnp.where(lane < HD, zero, value)], axis=0
    )


def causal(length, live):
    key = lax.broadcasted_iota(jnp.int32, (length, 2 * length), 0)
    query = lax.rem(lax.broadcasted_iota(jnp.int32, (length, 2 * length), 1), length)
    return (key <= query) & (key < live)


STRIP = 32


def strips(count, body, carry=None):
    def one(k, carry):
        return body(pl.ds(pl.multiple_of(k * STRIP, STRIP), STRIP), carry)

    return lax.fori_loop(0, count // STRIP, one, carry)


def bands(count, body):
    def one(k, carry):
        body(pl.multiple_of(k * 2 * BLOCK, BLOCK))
        return carry

    lax.fori_loop(0, count // (2 * BLOCK), one, 0)


FLAT_AHEAD = 2
TALL_GAP = 1


def front_kernel(dims, chunks, names_, n_src, *refs):
    pages, length, slots = dims
    n_out = len(names_)
    it = iter(refs)

    def take(k):
        return [next(it) for _ in range(k)]

    shards = take(n_src)
    x_in, cot_in, memory_in, counts, lengths = take(5)
    outs = take(n_out)
    saved_out = take(13)
    gains, lse_cross, lse_self = take(3)
    saved = take(13)
    (result, hidden, pre, third, after_cross, cctx, second, cq, kv, after_self, ctx, first, qkv) = saved
    x_bf, cot, memory, w_a, w_b, w_d, w_gain, total_out, g_hidden = take(9)
    local, zs, zr, ps, pr, qs, qr, cs, cr, us, ur, ds, dr, loads_sem, stores_sem = take(15)
    f32, bf16 = jnp.float32, jnp.bfloat16
    grid = Grid()
    n, depth = grid.n, grid.depth
    y, c, z, x = grid.at
    tokens, D = x_bf.shape
    loads = {}

    def fetch(name, src, dst, slot):
        loads[name] = pltpu.make_async_copy(src, dst, loads_sem.at[slot])
        loads[name].start()

    def need(*names):
        for name in names:
            copy = loads.pop(name, None)
            if copy is not None:
                copy.wait()

    fetch("x", x_in, x_bf, 0)
    fetch("cot", cot_in, cot, 1)
    fetch("memory", memory_in, memory, 2)
    grid.meet()
    pending = []

    def send(*copy):
        made = started(*copy)
        pending.append(made)
        return made

    def window(i):
        _, r0, nr, c0, nc, _, o0, _ = chunks[i]
        return pl.ds(r0, nr), pl.ds(o0, nc)

    def out(i):
        return outs[chunks[i][5]]

    def shard(i):
        m, r0, nr, c0, nc, _, _, _ = chunks[i]
        return shards[m].at[pl.ds(r0, nr), pl.ds(c0, nc)]

    def block(i, yy, zz, xx):
        return out(i).at[(yy, c, zz, xx) + window(i)]

    def back(a, b):
        return grid.place((n - a) % n, (n - b) % n)

    def column(i, a, b):
        yy, xx = back(a, b)
        return out(i).at[(yy, c, slice(None), xx) + window(i)]

    def share(i, a, b):
        piece = column(i, a, b)
        slot = a * n + b
        return send(piece, piece, cs.at[i, slot], cr.at[i, slot], grid.partner())

    zc, pc, qc, cc, lc = {}, {}, {}, {}, {}

    def keep_own(i):
        lc[i] = pltpu.make_async_copy(shard(i), block(i, y, z, x), local.at[i])
        lc[i].start()

    def stage_z(i):
        zc[i] = [
            send(shard(i), block(i, y, z, x), zs.at[i, k - 1], zr.at[i, k - 1], grid.step_z(k))
            for k in range(1, depth)
        ]
        keep_own(i)

    def stage_p(i):
        for copy in zc[i]:
            copy.wait_recv()
        lc[i].wait()
        piece = column(i, 0, 0)
        pc[i] = [
            send(piece, piece, ps.at[i, a - 1], pr.at[i, a - 1], grid.step_plane(a, 0))
            for a in range(1, n)
        ]
        qc[i] = [
            send(piece, piece, qs.at[i, b - 1], qr.at[i, b - 1], grid.step_plane(b, 1))
            for b in range(1, n)
        ]
        cc[i] = [share(i, 0, 0)]

    def stage_q(i):
        for a in range(1, n):
            pc[i][a - 1].wait_recv()
            piece = column(i, a, 0)
            for b in range(1, n):
                j = a * (n - 1) + b - 1
                qc[i].append(
                    send(piece, piece, qs.at[i, j], qr.at[i, j], grid.step_plane(b, 1))
                )
            cc[i].append(share(i, a, 0))

    def stage_c(i):
        j = 0
        for a in range(n):
            for b in range(1, n):
                qc[i][j].wait_recv()
                j += 1
                cc[i].append(share(i, a, b))

    def tall_p(i):
        keep_own(i)
        pc[i] = [
            send(shard(i), block(i, y, z, x), ps.at[i, a - 1], pr.at[i, a - 1], grid.step_plane(a, 0))
            for a in range(1, n)
        ]

    def tall_q(i):
        lc[i].wait()
        qc[i] = []
        for a in range(n):
            if a:
                pc[i][a - 1].wait_recv()
            yy, xx = back(a, 0)
            piece = block(i, yy, z, xx)
            for b in range(1, n):
                j = a * (n - 1) + b - 1
                qc[i].append(
                    send(piece, piece, qs.at[i, j], qr.at[i, j], grid.step_plane(b, 1))
                )

    def layer(i, k, j):
        zz = lax.rem(z + (depth - j if k == 0 else j), depth)
        return out(i).at[(slice(None), c, zz, slice(None)) + window(i)]

    def hop(i, k, j):
        piece = layer(i, k, j)
        send_sem, recv_sem = ((us, ur), (ds, dr))[k]
        to = grid.device(y, c, lax.rem(z + (1 if k == 0 else depth - 1), depth), x)
        return remote(piece, piece, send_sem.at[i, j], recv_sem.at[i, j], to)

    def share_layer(i, k, j):
        piece = layer(i, k, j)
        slot = k * (depth - 1) + j
        return remote(piece, piece, cs.at[i, slot], cr.at[i, slot], grid.partner())

    def level(k):
        return z if k == 0 else depth - 1 - z

    def climb(i, j):
        if j == 0:
            for copy in qc[i]:
                copy.wait_recv()
            share_layer(i, 0, 0).start()
        for k in (0, 1):
            if j:

                @pl.when(level(k) >= j)
                def _():
                    hop(i, k, j - 1).wait_recv()
                    share_layer(i, k, j).start()

            if j < depth - 1:

                @pl.when((level(k) >= j) & (level(k) < depth - 1))
                def _():
                    hop(i, k, j).start()

    def each_layer(i, call, hops):
        call(share_layer(i, 0, 0))
        for k in (0, 1):
            for j in range(depth - 1):
                if hops:

                    @pl.when((level(k) >= j) & (level(k) < depth - 1))
                    def _():
                        call(hop(i, k, j))

                @pl.when(level(k) >= j + 1)
                def _():
                    call(share_layer(i, k, j + 1))

    there = set()

    def arrive(*ids):
        for i in ids:
            if i in there:
                continue
            there.add(i)
            if chunks[i][7]:
                each_layer(i, lambda copy: copy.wait_recv(), False)
            else:
                for copy in cc[i]:
                    copy.wait_recv()

    def pull(name, k, dst, slot):
        ids = held[name][k]
        arrive(*ids)
        fetch((name, k), out(ids[0]), dst, slot)

    def store(name, slot):
        src = saved[name]
        made = pltpu.make_async_copy(src, saved_out[name], stores_sem.at[slot])
        made.start()
        stores.append(made)

    stores = []
    lane = lax.broadcasted_iota(jnp.int32, (length, 2 * HD), 1)

    def attention(page, pair, q_ref, k_ref, k_row, k_rows, k_col, v_col, allowed, to, lse):
        q_at, k_at = pl.ds(page * length, length), pl.ds(k_row, k_rows)
        q = both_heads(lane, q_ref[q_at, lane_window(0, pair)])
        keys = k_ref[k_at, lane_window(k_col, pair)]
        values = k_ref[k_at, lane_window(v_col, pair)]
        scores = times_transposed(keys, q) * HD ** (-0.5)
        scores = jnp.where(allowed, scores, -1000000000.0)
        top = jnp.max(scores, axis=0, keepdims=True)
        expos = jnp.exp(scores - top)
        sum_ = jnp.sum(expos, axis=0, keepdims=True)
        probs = (expos * (1.0 / sum_)).astype(bf16)
        lse[pl.ds(page * (D // HD // 2) + pair, 1), :] = top + jnp.log(sum_)
        found = transposed_times(probs, values)
        to[q_at, lane_window(0, pair)] = jnp.where(lane < HD, found[:length], found[length:]).astype(bf16)

    def read_gains():
        arrive(*held["gain"][0])
        copy = pltpu.make_async_copy(out(held["gain"][0][0]), w_gain, loads_sem.at[3])
        copy.start()
        copy.wait()
        columns = w_gain.reshape(D, 128)[...].astype(f32)
        gains[...] = columns.T[:8]

    def project(left, weight, col, count, to, to_col):
        def body(at):
            w_at = pl.ds(pl.multiple_of(col + at, BLOCK), 2 * BLOCK)
            to_at = pl.ds(pl.multiple_of(to_col + at, BLOCK), 2 * BLOCK)
            to[:, to_at] = times(left[...], weight[:, w_at]).astype(to.dtype)

        bands(count, body)

    def first_norm():
        need("x")
        gain = gains[pl.ds(0, 1), :]

        def body(at, carry):
            unit, _ = standardize(x_bf[at].astype(f32))
            first[at] = (unit * gain).astype(bf16)
            return carry

        strips(tokens, body, 0)

    def self_project(k):
        need(("self", k))
        project(first, flat_b, k * D, D, qkv, k * D)

    def self_attention(page):
        allowed = causal(length, lengths[page])

        def body(pair, carry):
            attention(page, pair, qkv, qkv, page * length, length, D, 2 * D, allowed, ctx, lse_self)
            return carry

        lax.fori_loop(0, D // (2 * HD), body, 0)

    def residual(left, weight, col, base, to):
        def body(at):
            here = pl.ds(at, 2 * BLOCK)
            w_at = pl.ds(pl.multiple_of(col + at, BLOCK), 2 * BLOCK)
            to[:, here] = base[:, here].astype(f32) + times(left[...], weight[:, w_at])

        bands(D, body)

    def self_out():
        need(("self", 3))
        residual(ctx, flat_b, 3 * D, x_bf, after_self)
        gain = gains[pl.ds(1, 1), :]

        def body(at, carry):
            unit, _ = standardize(after_self[at])
            second[at] = (unit * gain).astype(bf16)
            return carry

        strips(tokens, body, 0)

    def memory_project(page, part):
        need("memory", ("kv", 0), ("kv", 1))
        span = -(-slots // 32) * 16
        at = pl.ds(page * slots + part * span, min(span, slots - part * span))

        def body(col):
            here = pl.ds(col, 2 * BLOCK)
            kv[at, here] = times(memory[at, :], flat_a[:, here]).astype(bf16)

        bands(2 * D, body)

    def cross_query():
        need(("qo", 0))
        project(second, flat_a, 0, D, cq, 0)

    def cross_attention(page, part):
        allowed = lax.broadcasted_iota(jnp.int32, (slots, 2 * length), 0) < counts[page]
        pairs = D // (2 * HD) // 2

        def body(k, carry):
            pair = part * pairs + k
            attention(page, pair, cq, kv, page * slots, slots, 0, D, allowed, cctx, lse_cross)
            return carry

        lax.fori_loop(0, pairs, body, 0, unroll=2)

    def cross_out():
        need(("qo", 1))
        residual(cctx, flat_a, D, after_self, after_cross)
        gain = gains[pl.ds(2, 1), :]

        def body(at, carry):
            unit, _ = standardize(after_cross[at])
            third[at] = (unit * gain).astype(bf16)
            return carry

        strips(tokens, body, 0)

    def hidden_grad(k):
        need("cot", ("reduce", 0))

        def body(at):
            here = pl.ds(pl.multiple_of(k * D + at, BLOCK), 2 * BLOCK)
            g_hidden[:, here] = times_transposed(cot[...], flat_d[here, :])

        bands(D, body)

    def expand(k):
        need(("expand", k))

        def body(j, carry):
            at = pl.ds(pl.multiple_of(k * D + j * 2 * BLOCK, BLOCK), 2 * BLOCK)
            value = times(third[...], flat_b[:, at])
            below = 0.5 + 0.5 * lax.erf(value * 0.5**0.5)
            hidden[:, at] = (value * below).astype(bf16)
            density = jnp.exp(-0.5 * value * value) * 0.3989422804014327
            pre[:, at] = (g_hidden[:, at] * (below + value * density)).astype(bf16)
            return carry

        lax.fori_loop(0, D // (2 * BLOCK), body, 0)

    def reduce_out(k):
        at = pl.ds(k * D, D)

        def body(col):
            here = pl.ds(col, 2 * BLOCK)
            value = after_cross[:, here] if k == 0 else total_out[:, here]
            value = value + times(hidden[:, at], flat_d[at, here])
            if k < 3:
                total_out[:, here] = value
            else:
                result[:, here] = value.astype(bf16)

        bands(D, body)

    flat_a, flat_b, flat_d = w_a.reshape(D, 2 * D), w_b.reshape(D, 4 * D), w_d.reshape(4 * D, D)

    held = {}
    for i, chunk in enumerate(chunks):
        name, k = names_[chunk[5]]
        held.setdefault(name, {}).setdefault(k, []).append(i)

    plan = Plan()
    flat = [i for i, chunk in enumerate(chunks) if not chunk[7]]
    tall = [i for i, chunk in enumerate(chunks) if chunk[7]]
    tick = {}
    for t, i in enumerate(flat):
        plan.add(t - FLAT_AHEAD, 0, stage_z, i)
        plan.add(t, 2, stage_p, i)
        plan.add(t + 1, 4, stage_q, i)
        plan.add(t + 2, 6, stage_c, i)
        tick[i] = t + 3
    for t, i in enumerate(tall):
        t = TALL_GAP * t - 1
        plan.add(t, 1, tall_p, i)
        plan.add(t + 2, 3, tall_q, i)
        for h in range(depth):
            plan.add(t + 4 + 2 * h, 5, climb, i, h)
        tick[i] = t + 4 + 2 * (depth - 1) + 1

    def ready(name, k):
        return max(tick[i] for i in held[name][k])

    def part(buffer, k, width):
        return buffer.at[:, :, :, :, :, pl.ds(k * width, width)]

    clock = [0]

    def then(when, call, *args):
        clock[0] = max(clock[0] + 1, 3 * when)
        plan.add(clock[0] // 3, 3 + 2 * (clock[0] % 3), call, *args)
        return clock[0] // 3

    def keep(*names):
        for name in names:
            store(name, name)

    plan.add(ready("gain", 0), 8, read_gains)
    plan.add(ready("gain", 0), 8, first_norm)
    for k in range(2):
        plan.add(ready("kv", k), 8, pull, "kv", k, part(w_a, k, D), 8 + k)
    for k in range(4):
        plan.add(ready("self", k), 8, pull, "self", k, part(w_b, k, D), 4 + k)
    for page in range(pages):
        for half in range(2):
            kv_done = then(ready("kv", 1) + 1, memory_project, page, half)
    for k in range(3):
        then(ready("self", k) + 1, self_project, k)
    for page in range(pages):
        then(0, self_attention, page)
    self_done = then(ready("self", 3) + 1, self_out)
    plan.add(self_done, 9, keep, 8, 10, 11, 12, 9, 6)
    for k in range(2):
        plan.add(max(ready("qo", k), kv_done + 1), 8, pull, "qo", k, part(w_a, k, D), 10 + k)
    for k in range(4):
        plan.add(
            max(ready("expand", k), self_done + 1), 8, pull, "expand", k, part(w_b, k, D), 12 + k
        )
    plan.add(ready("reduce", 0), 8, pull, "reduce", 0, w_d, 16)
    then(max(ready("qo", 0), kv_done + 1) + 1, cross_query)
    for page in range(pages):
        for half in range(2):
            then(0, cross_attention, page, half)
    cross_done = then(max(ready("qo", 1), kv_done + 1) + 1, cross_out)
    plan.add(cross_done, 9, keep, 3, 4, 5, 7)
    for k in range(4):
        plan.add(ready("reduce", 0) + 1 + k // 2, 9, hidden_grad, k)
    for k in range(4):
        then(max(ready("expand", k), self_done + 1) + 1, expand, k)
        last = then(0, reduce_out, k)
    plan.add(last, 10, keep, 1, 2, 0)
    plan.run()
    for i in flat:
        arrive(i)
    for i in tall:
        arrive(i)
        each_layer(i, lambda copy: copy.wait_send(), True)
    for copy in pending:
        copy.wait_send()
    for copy in stores:
        copy.wait()


def front(sources, pieces, names, tokens_in, shapes):
    dp, fsdp = lax.axis_size("dp"), lax.axis_size("fsdp")
    n = dp // CORES
    depth = fsdp // n
    rows = sources[0].shape[0]
    pages, length, slots = shapes
    tokens, D = pages * length, WIDTH
    groups = [(4 * rows if name == "reduce" else rows, 128 if name == "gain" else D) for name, _ in names]
    chunks = [(m, r0, rows, c0, groups[o][1], o, 0, tall) for m, r0, c0, o, tall in pieces]
    t = len(chunks)
    slot_count = max(n * n, 2 * depth - 1)
    shapes_ = (depth - 1, depth - 1, n - 1, n - 1, n * (n - 1), n * (n - 1), slot_count, slot_count)
    shapes_ += (depth - 1,) * 4
    dma = pltpu.SemaphoreType.DMA
    f32, bf16 = jnp.float32, jnp.bfloat16
    lead = (n, CORES, depth, n)
    saved = [
        ((tokens, D), bf16),
        ((tokens, 4 * D), bf16),
        ((tokens, 4 * D), bf16),
        ((tokens, D), bf16),
        ((tokens, D), f32),
        ((tokens, D), bf16),
        ((tokens, D), bf16),
        ((tokens, D), bf16),
        ((pages * slots, 2 * D), bf16),
        ((tokens, D), f32),
        ((tokens, D), bf16),
        ((tokens, D), bf16),
        ((tokens, 3 * D), bf16),
    ]
    small = [((8, D), f32)] + [((pages * D // HD // 2, 2 * length), f32)] * 2
    hbm = pl.BlockSpec(memory_space=pltpu.HBM)
    vmem = pl.BlockSpec(memory_space=pltpu.VMEM)
    smem = pl.BlockSpec(memory_space=pltpu.SMEM)
    found = pl.pallas_call(
        functools.partial(front_kernel, shapes, chunks, names, len(sources)),
        out_shape=[jax.ShapeDtypeStruct(lead + g, bf16) for g in groups]
        + [jax.ShapeDtypeStruct(*s) for s in saved + small],
        in_specs=[vmem] * len(sources) + [hbm] * 3 + [smem] * 2,
        out_specs=[hbm] * (len(groups) + len(saved)) + [vmem] * 3,
        scratch_shapes=[pltpu.VMEM(*s) for s in saved]
        + [
            pltpu.VMEM((tokens, D), bf16),
            pltpu.VMEM((tokens, D), bf16),
            pltpu.VMEM((pages * slots, D), bf16),
            pltpu.VMEM(lead + (rows, 2 * D), bf16),
            pltpu.VMEM(lead + (rows, 4 * D), bf16),
            pltpu.VMEM(lead + (4 * rows, D), bf16),
            pltpu.VMEM(lead + (rows, 128), bf16),
            pltpu.VMEM((tokens, D), f32),
            pltpu.VMEM((tokens, 4 * D), f32),
            dma((t,)),
        ]
        + [dma((t, k)) for k in shapes_]
        + [dma((20,)), dma((13,))],
        compiler_params=pltpu.CompilerParams(
            collective_id=0, has_side_effects=True, vmem_limit_bytes=67043328
        ),
    )(*sources, *tokens_in)
    weights = [
        w.reshape(dp * fsdp * g[0], g[1]) for w, g in zip(found[: len(groups)], groups)
    ]
    return weights, found[len(groups) : len(groups) + len(saved)], found[len(groups) + len(saved) :]


RING = 4
KEPT = (("self", 4), ("kv", 2), ("qo", 2), ("expand", 4))
SPARE = 2
BACK_TALL = (1, 5, 9)
TALL_STEP = 2


def back_kernel(dims, *refs):
    pages, length, slots = dims
    it = iter(refs)

    def take(k):
        return [next(it) for _ in range(k)]

    (hidden_in, pre_in, third_in, out_in, cross_in, cctx_in, second_in, cq_in, kv_in, memory_in,
     self_in, ctx_in, first_in, qkv_in, x_in) = take(15)
    kept = {name: take(count) for name, count in KEPT}
    counts, lengths, gains, lse_cross, lse_self = take(5)
    grad_outs = take(7)
    gain_out, input_out, memory_out = take(3)
    (hidden, pre, third, out_grad, cross, cctx, second, cq, kv, memory, after_self, ctx, first, qkv,
     w_a, w_b, branch, g_ctx, stage, g_norm) = take(20)
    send0, got0, parts, got1, halves, got2, line, got3, gain_sum, gain_got = take(10)
    tower, tower_got, tower_got1, tower_half, tower_got2 = take(5)
    local, s0, r0, s1, r1, s2, r2, s3, r3, gs, gr, free, free1 = take(13)
    sz, rz, sa, ra, sb, rb = take(6)

    grid = Grid()
    n, depth = grid.n, grid.depth
    y, c, z, x = grid.at
    rows, width = send0.shape[-2:]
    f32, bf16 = jnp.float32, jnp.bfloat16
    copies, loads = {}, {}

    def fetch(name, src, dst, slot):
        loads[name] = pltpu.make_async_copy(src, dst, local.at[slot])
        loads[name].start()

    def need(*names):
        for name in names:
            copy = loads.pop(name, None)
            if copy is not None:
                copy.wait()

    D = third.shape[1]
    fetch("hidden", hidden_in, hidden, 0)
    fetch("out", out_in, out_grad, 1)
    fetch("pre", pre_in, pre, 2)
    fetch("third", third_in, third, 3)

    def weights(label, *moves):
        for name, k, buffer, half in moves:
            slot = 15 + half + (0 if buffer is w_a else 2)
            fetch((label, slot), kept[name][k], buffer.at[:, pl.ds(half * D, D)], slot)

    def need_all(label):
        need(*[key for key in list(loads) if key[0] == label])

    weights("expand", *[("expand", k, (w_a, w_b)[k // 2], k % 2) for k in range(4)])
    fetch("cross", cross_in, cross, 4)
    grid.meet()
    fetch("cctx", cctx_in, cctx, 5)
    fetch("cq", cq_in, cq, 7)
    fetch("kv", kv_in, kv, 8)
    fetch("second", second_in, second, 6)
    fetch("memory", memory_in, memory, 9)
    fetch("self", self_in, after_self, 10)
    fetch("ctx", ctx_in, ctx, 11)
    fetch("first", first_in, first, 12)
    fetch("qkv", qkv_in, qkv, 13)

    chunks = []
    wide = hidden.shape[1] // grid.devices
    for col in range(0, D, width * rows // wide):
        chunks.append((0, hidden, out_grad, col, ("hidden", "out")))
    for col in range(0, pre.shape[1], width):
        chunks.append((1, third, pre, col, ("third", "pre")))
    OUT_CHUNK = len(chunks)
    chunks.append((2, cctx, branch, 0, ("cctx",)))
    chunks.append((3, second, cq, 0, ("second",)))
    chunks.append((4, memory, kv, 0, ("memory",)))
    chunks.append((4, memory, kv, D, ()))
    chunks.append((5, ctx, branch, 0, ("ctx",)))
    for col in range(0, 3 * D, width):
        chunks.append((6, first, qkv, col, ("first",)))
    total = len(chunks)
    tall = {i: k for k, i in enumerate(BACK_TALL)}
    flat = {}
    ticks = []
    for i in range(total):
        if i in tall:
            ticks.append(len(flat) - 1)
        else:
            ticks.append(len(flat))
            flat[i] = len(flat)
    by_flat = {f: i for i, f in flat.items()}

    def products(i, core, emit):
        _, left, right, col, names = chunks[i]
        need(*names)
        own = left.shape[1] // grid.devices
        span = left.shape[1] // (n * CORES)
        lanes = width * rows // own

        band = min(lanes, 2 * BLOCK)

        def body(step, carry):
            yy, j = step // (lanes // band), step % (lanes // band)
            at = pl.multiple_of((yy * CORES + core) * span, min(span, BLOCK))
            value = transposed_times(
                left[:, pl.ds(at, span)],
                right[:, pl.ds(pl.multiple_of(col + j * band, BLOCK), band)],
            )
            for k in range(depth * n):
                for part in range(own // rows):
                    top = k * own + part * rows
                    lane = pl.multiple_of(part * lanes + j * band, BLOCK)
                    emit(yy, k // n, k % n, lane, band, value[top : top + rows])
            return carry

        lax.fori_loop(0, n * (lanes // band), body, 0)

    def reuse(i, stage, ring):
        before = i - ring if stage == 0 else by_flat.get(flat[i] - ring, -1)
        if before >= 0:
            for copy in copies[before, stage]:
                copy.wait_send()

    def credit(i):
        if i + RING < total:
            pl.semaphore_signal(free, inc=1, device_id=grid.partner(), device_id_type=MESH)

    def stage0(i):
        s = i % SPARE
        reuse(i, 0, SPARE)

        def emit(yy, zz, xx, lane, lanes, value):
            send0[s, yy, zz, xx, :, pl.ds(lane, lanes)] = value.astype(bf16)

        products(i, 1 - c, emit)
        if i >= RING:
            pl.semaphore_wait(free, 1)
        copies[i, 0] = [started(send0.at[s], got0.at[i % RING], s0.at[s], r0.at[i % RING], grid.partner())]

    def relative(yy, xx):
        to_y = lax.rem(yy - y + n, n)
        to_x = lax.rem(xx - x + n, n)
        return to_x * (1 - c) + to_y * c, to_y * (1 - c) + to_x * c

    def stage1(i):
        s, g = flat[i] % RING, i % RING
        reuse(i, 1, RING)
        copies[i, 0][0].wait_recv()

        def emit(yy, zz, xx, lane, lanes, value):
            value = value + got0[g, yy, zz, xx, :, pl.ds(lane, lanes)].astype(f32)
            a, b = relative(yy, xx)
            parts[s, a, b, zz, :, pl.ds(lane, lanes)] = value.astype(bf16)

        products(i, c, emit)
        credit(i)
        copies[i, 1] = []
        for a in range(1, n):
            if flat[i] >= RING:
                pl.semaphore_wait(free1.at[a - 1], 1)
            copies[i, 1].append(
                started(
                    parts.at[s, a],
                    got1.at[s, a - 1],
                    s1.at[s, a - 1],
                    r1.at[s, a - 1],
                    grid.step_plane(a, 0),
                )
            )

    def stage2(i):
        s, f = flat[i] % RING, flat[i]
        reuse(i, 2, RING)
        for copy in copies[i, 1]:
            copy.wait_recv()
        copies[i, 2] = []
        for b in list(range(1, n)) + [0]:

            def body(zz, carry):
                value = parts[s, 0, b, zz].astype(f32)
                for a in range(1, n):
                    value = value + got1[s, a - 1, b, zz].astype(f32)
                halves[s, b, zz] = value.astype(bf16)
                return carry

            lax.fori_loop(0, depth, body, 0)
            if b:
                copies[i, 2].append(
                    started(
                        halves.at[s, b],
                        got2.at[f, b - 1],
                        s2.at[s, b - 1],
                        r2.at[f, b - 1],
                        grid.step_plane(b, 1),
                    )
                )
        if f + RING < len(flat):
            for a in range(1, n):
                pl.semaphore_signal(
                    free1.at[a - 1], inc=1, device_id=grid.step_plane(n - a, 0), device_id_type=MESH
                )

    def stage3(i):
        s, f = flat[i] % RING, flat[i]
        reuse(i, 3, RING)
        for copy in copies[i, 2]:
            copy.wait_recv()

        def body(zz, carry):
            value = halves[s, 0, zz].astype(f32)
            for b in range(1, n):
                value = value + got2[f, b - 1, zz].astype(f32)
            line[s, zz] = value.astype(bf16)
            return carry

        lax.fori_loop(0, depth, body, 0)
        copies[i, 3] = [
            started(
                line.at[s, lax.rem(z + k, depth)],
                got3.at[f, k - 1],
                s3.at[s, k - 1],
                r3.at[f, k - 1],
                grid.step_z(k),
            )
            for k in range(1, depth)
        ]

    def tall1(i):
        k, g = tall[i], i % RING
        copies[i, 0][0].wait_recv()

        def emit(yy, zz, xx, lane, lanes, value):
            value = value + got0[g, yy, zz, xx, :, pl.ds(lane, lanes)].astype(f32)
            tower[k, zz, yy, xx, :, pl.ds(lane, lanes)] = value.astype(bf16)

        products(i, c, emit)
        credit(i)

    def level(up):
        return z if up else depth - 1 - z

    def pass_on(i, up, d):
        k = tall[i]
        target = lax.rem(z + (d if up else depth - d), depth)
        slot = target if up or d > 1 else depth
        to = grid.device(y, c, lax.rem(z + (1 if up else depth - 1), depth), x)
        return remote(
            tower.at[k, target], tower_got.at[k, slot], sz.at[k, target], rz.at[k, slot], to
        )

    def absorb(i, target, slot):
        k = tall[i]
        remote(
            tower.at[k, target], tower_got.at[k, slot], sz.at[k, target], rz.at[k, slot], grid.partner()
        ).wait_recv()

        def body(j, carry):
            yy, xx = j // n, j % n
            value = tower[k, target, yy, xx].astype(f32) + tower_got[k, slot, yy, xx].astype(f32)
            tower[k, target, yy, xx] = value.astype(bf16)
            return carry

        lax.fori_loop(0, n * n, body, 0)

    def tall_z(i, d):
        for up in (True, False):

            @pl.when(level(up) + d < depth)
            def _():
                target = lax.rem(z + (d if up else depth - d), depth)

                @pl.when(level(up) > 0)
                def _():
                    absorb(i, target, target)

                pass_on(i, up, d).start()

    def tall_plane(i):
        k = tall[i]

        @pl.when(z > 0)
        def _():
            absorb(i, z, z)

        @pl.when(z < depth - 1)
        def _():
            absorb(i, z, depth)

        copies[i, 1] = []
        for a in range(1, n):
            for b in range(n):
                yy, xx = grid.place(a, b)
                j = (a - 1) * n + b
                copies[i, 1].append(
                    started(
                        tower.at[k, z, yy, xx],
                        tower_got1.at[k, j],
                        sa.at[k, j],
                        ra.at[k, j],
                        grid.step_plane(a, 0),
                    )
                )

    def tall_half(i):
        k = tall[i]
        for copy in copies[i, 1]:
            copy.wait_recv()
        copies[i, 2] = []
        for b in list(range(1, n)) + [0]:
            yy, xx = grid.place(0, b)
            value = tower[k, z, yy, xx].astype(f32)
            for a in range(1, n):
                value = value + tower_got1[k, (a - 1) * n + b].astype(f32)
            tower_half[k, b] = value.astype(bf16)
            if b:
                copies[i, 2].append(
                    started(
                        tower_half.at[k, b],
                        tower_got2.at[k, b - 1],
                        sb.at[k, b - 1],
                        rb.at[k, b - 1],
                        grid.step_plane(b, 1),
                    )
                )

    def tall_out(i):
        k = tall[i]
        for copy in copies[i, 2]:
            copy.wait_recv()
        value = tower_half[k, 0].astype(f32)
        for b in range(1, n):
            value = value + tower_got2[k, b - 1].astype(f32)
        put_out(i, value)

    def put_out(i, value):
        m, left, _, col, _ = chunks[i]
        own = left.shape[1] // grid.devices
        if own == rows:
            grad_outs[m][:, pl.ds(col, width)] = value
        else:
            for part in range(own // rows):
                grad_outs[m][pl.ds(part * rows, rows), pl.ds(col, BLOCK)] = value[
                    :, part * BLOCK : (part + 1) * BLOCK
                ]

    def stage4(i):
        for copy in copies[i, 3]:
            copy.wait_recv()
        value = line[flat[i] % RING, z].astype(f32)
        for k in range(1, depth):
            value = value + got3[flat[i], k - 1].astype(f32)
        put_out(i, value)

    moves = [
        [grid.partner()],
        [grid.step_plane(a, 0) for a in range(1, n)],
        [grid.step_plane(a, 1) for a in range(1, n)],
        [grid.step_z(k) for k in range(1, depth)],
        [],
    ]
    start = [0, 1, n, 2 * n - 1, 2 * n + depth - 2]

    def gain_step(h):
        value = gain_sum[min(h, 3)]
        if h:
            for j, copy in enumerate(copies["gain", h - 1]):
                copy.wait_recv()
                value = value + gain_got[start[h - 1] + j]
        if h == len(moves) - 1:
            gain_out[...] = value
        elif h:
            gain_sum[h] = value
        if h < len(moves) - 2:
            gain_sum[h + 1] = value
        copies["gain", h] = [
            started(
                gain_sum.at[h],
                gain_got.at[start[h] + j],
                gs.at[start[h] + j],
                gr.at[start[h] + j],
                device,
            )
            for j, device in enumerate(moves[h])
        ]

    def context_grad(weight, col):
        g_ctx[...] = times_transposed(branch[...], weight[:, pl.ds(col, D)]).astype(bf16)

    lane = lax.broadcasted_iota(jnp.int32, (length, 2 * HD), 1)
    scale = HD ** (-0.5)

    def attention(page, pair, q_ref, q_col, k_ref, k_row, k_rows, k_col, v_col, lse, allowed):
        q_at = pl.ds(page * length, length)
        k_at = pl.ds(k_row, k_rows)
        q = both_heads(lane, q_ref[q_at, lane_window(q_col, pair)])
        g = both_heads(lane, g_ctx[q_at, lane_window(0, pair)])
        keys, values = k_ref[k_at, lane_window(k_col, pair)], k_ref[k_at, lane_window(v_col, pair)]
        scores = times_transposed(keys, q) * scale
        scores = jnp.where(allowed, scores, -1000000000.0)
        probs = jnp.exp(scores - lse[pl.ds(page * (D // HD // 2) + pair, 1), :])
        g_probs = times_transposed(values, g)
        inner = jnp.sum(probs * g_probs, axis=0, keepdims=True)
        g_scores = (probs * (g_probs - inner)).astype(bf16)
        g_values = times(probs.astype(bf16), g)
        g_keys = times(g_scores, q) * scale
        g_q = transposed_times(g_scores, keys)
        g_q = jnp.where(lane < HD, g_q[:length], g_q[length:]) * scale
        q_ref[q_at, lane_window(q_col, pair)] = g_q.astype(bf16)
        k_ref[k_at, lane_window(k_col, pair)] = g_keys.astype(bf16)
        k_ref[k_at, lane_window(v_col, pair)] = g_values.astype(bf16)

    def cross_attention(page):
        need("cq", "kv")
        place = lax.broadcasted_iota(jnp.int32, (slots, 2 * length), 0)
        allowed = place < counts[page]

        def body(pair, carry):
            attention(page, pair, cq, 0, kv, page * slots, slots, 0, D, lse_cross, allowed)
            return carry

        lax.fori_loop(0, D // (2 * HD), body, 0, unroll=2)

    def self_attention(page):
        need("qkv")
        allowed = causal(length, lengths[page])

        def body(pair, carry):
            attention(page, pair, qkv, 0, qkv, page * length, length, D, 2 * D, lse_self, allowed)
            return carry

        lax.fori_loop(0, D // (2 * HD), body, 0)

    def norm_back(value_ref, gain_row, put):
        gain = gains[pl.ds(gain_row, 1), :]

        def body(k, total_):
            at = pl.ds(k * 32, 32)
            value = value_ref[at].astype(f32)
            centred = value - jnp.mean(value, axis=-1, keepdims=True)
            spread = jnp.mean(centred * centred, axis=-1, keepdims=True)
            row_scale = lax.rsqrt(spread + EPS)
            unit = centred * row_scale
            grad = g_norm[at]
            grad_unit = grad * gain
            inner = jnp.mean(grad_unit * unit, axis=-1, keepdims=True)
            put(at, row_scale * (grad_unit - jnp.mean(grad_unit, axis=-1, keepdims=True) - unit * inner))
            return total_ + jnp.sum(grad * unit, axis=0, keepdims=True)

        summed = lax.fori_loop(0, value_ref.shape[0] // 32, body, jnp.zeros((1, D), f32))
        gain_sum[0, pl.ds(gain_row, 1), :] = summed

    def spread(terms):
        def body(k, carry):
            at = pl.ds(pl.multiple_of(k * 2 * BLOCK, BLOCK), 2 * BLOCK)
            value = None
            for left, left_col, right, right_col in terms:
                term = times_transposed(
                    left[:, pl.ds(left_col, D)], right[at, pl.ds(right_col, D)]
                )
                value = term if value is None else value + term
            g_norm[:, at] = value
            return carry

        lax.fori_loop(0, D // (2 * BLOCK), body, 0)

    def third_norm():
        need("pre", "out", "cross")
        need_all("expand")
        spread([(pre, 0, w_a, 0), (pre, D, w_a, D), (pre, 2 * D, w_b, 0), (pre, 3 * D, w_b, D)])

        def put(at, value):
            value = out_grad[at].astype(f32) + value
            cross[at] = value
            branch[at] = value.astype(bf16)

        norm_back(cross, 2, put)
        weights("qo", ("qo", 1, w_a, 1), ("qo", 0, w_a, 0))
        weights("self", ("self", 3, w_b, 0), ("self", 0, w_b, 1))

    def second_norm():
        need("self")
        fetch("x", x_in, third, 14)
        spread([(cq, 0, w_a, 0)])

        def put(at, value):
            value = cross[at] + value
            cross[at] = value
            branch[at] = value.astype(bf16)

        norm_back(after_self, 1, put)
        weights("pair", ("self", 1, w_a, 0), ("self", 2, w_a, 1))

    def first_norm():
        need("x")
        need_all("pair")
        spread([(qkv, 0, w_b, D), (qkv, D, w_a, 0), (qkv, 2 * D, w_a, D)])

        def put(at, value):
            input_out[at] = cross[at] + value

        norm_back(third, 0, put)
        weights("kv", ("kv", 0, w_b, 0), ("kv", 1, w_b, 1))

    def memory_grad(page, part):
        need_all("kv")
        slot = part % 2
        need(("stage", slot))
        top = part * span
        height = min(slots - top, span)
        live = min(memory_rows - top, height)
        at = pl.ds(page * slots + top, height)

        def body(k, carry):
            col = pl.multiple_of(k * BLOCK, BLOCK)
            value = times_transposed(kv[at, :], w_b[pl.ds(col, BLOCK), :])
            for j in range(BLOCK // 128):
                stage[slot, pl.ds(k * (BLOCK // 128) + j, live, 8), :] = value[:live, j * 128 : j * 128 + 128]
            return carry

        lax.fori_loop(0, D // BLOCK, body, 0)
        fetch(
            ("stage", slot),
            stage.at[slot, pl.ds(0, live * 8)],
            memory_out.at[pl.ds((page * memory_rows + top) * 8, live * 8)],
            19 + slot,
        )

    span = -(-slots // 32) * 16
    memory_rows = memory_out.shape[0] // 8 // pages
    gain_sum[0] = jnp.zeros(gain_sum.shape[1:], f32)
    plan = Plan()
    for i in range(total):
        t = ticks[i]
        plan.add(t - 2, 0, stage0, i)
        if i in tall:
            plan.add(t, 1, tall1, i)
            for d in range(depth - 1, 0, -1):
                plan.add(t + TALL_STEP * (depth - 1 - d), 5, tall_z, i, d)
            t += TALL_STEP * (depth - 1)
            plan.add(t, 5, tall_plane, i)
            plan.add(t + 1, 5, tall_half, i)
            plan.add(t + 2, 5, tall_out, i)
        else:
            plan.add(t, 1, stage1, i)
            plan.add(t + 1, 2, stage2, i)
            plan.add(t + 2, 3, stage3, i)
            plan.add(t + 3, 4, stage4, i)

    def cross_in_grad():
        need_all("qo")
        context_grad(w_a, D)

    def self_in_grad():
        need_all("self")
        context_grad(w_b, 0)

    plan.add(0, 9, third_norm)
    plan.add(1, 9, cross_in_grad)
    for page in range(pages):
        plan.add(1 + page, 10, cross_attention, page)
    turn = ticks[OUT_CHUNK]
    plan.add(turn, 8, second_norm)
    plan.add(turn, 9, self_in_grad)
    for page in range(pages):
        plan.add(turn + page, 11, self_attention, page)
    plan.add(turn + pages, 9, first_norm)
    for page in range(pages):
        for part in range(2):
            plan.add(turn + pages + 1 + 2 * part, 9, memory_grad, page, part)
    for h in range(len(moves)):
        plan.add(len(flat) - 4 + h, 7, gain_step, h)
    plan.run()
    for i in range(total):
        if i >= total - SPARE:
            copies[i, 0][0].wait_send()
        if i in tall:
            for copy in copies[i, 1] + copies[i, 2]:
                copy.wait_send()
            for up in (True, False):
                for d in range(1, depth):

                    @pl.when(level(up) + d < depth)
                    def _():
                        pass_on(i, up, d).wait_send()

        elif flat[i] >= len(flat) - RING:
            for stage in (1, 2, 3):
                for copy in copies[i, stage]:
                    copy.wait_send()
    for h in range(len(moves)):
        for copy in copies["gain", h]:
            copy.wait_send()
    need(*list(loads))


def backward(big, small, shapes):
    dp, fsdp = lax.axis_size("dp"), lax.axis_size("fsdp")
    n = dp // CORES
    depth = fsdp // n
    devices = dp * fsdp
    rows = WIDTH // devices
    pages, length, slots, live = shapes
    tokens = pages * length
    D = WIDTH
    high = len(BACK_TALL)
    t = sum(k * m for k, m in ((big[0].shape[1], D), (D, big[1].shape[1]), (D, 8 * D))) // (D * D) - high
    dma = pltpu.SemaphoreType.DMA
    hops = 2 * n + depth - 2
    outs = [(big[0].shape[1], D), (D, big[1].shape[1]), (D, D), (D, D), (D, 2 * D), (D, D), (D, 3 * D)]
    f32 = jnp.float32

    def scratch(*lead):
        return pltpu.VMEM(lead + (rows, WIDTH), jnp.bfloat16)

    def like(value):
        return pltpu.VMEM(value.shape, value.dtype)

    hbm = pl.BlockSpec(memory_space=pltpu.HBM)
    vmem = pl.BlockSpec(memory_space=pltpu.VMEM)
    smem = pl.BlockSpec(memory_space=pltpu.SMEM)
    return pl.pallas_call(
        functools.partial(back_kernel, (pages, length, slots)),
        out_shape=[jax.ShapeDtypeStruct((k // devices, m), f32) for k, m in outs]
        + [
            jax.ShapeDtypeStruct((8, D), f32),
            jax.ShapeDtypeStruct((tokens, D), f32),
            jax.ShapeDtypeStruct((pages * live * D // 128, 128), f32),
        ],
        in_specs=[hbm] * len(big) + [smem, smem] + [vmem] * 3,
        out_specs=[vmem] * (len(outs) + 2) + [hbm],
        scratch_shapes=[like(v) for v in big[:14]]
        + [pltpu.VMEM((D, 2 * D), jnp.bfloat16)] * 2
        + [pltpu.VMEM((tokens, D), jnp.bfloat16)] * 2
        + [
            pltpu.VMEM((2, -(-slots // 32) * 16 * 8, 128), f32),
            pltpu.VMEM((tokens, D), f32),
            scratch(SPARE, n, depth, n),
            scratch(RING, n, depth, n),
            scratch(RING, n, n, depth),
            scratch(RING, n - 1, n, depth),
            scratch(RING, n, depth),
            scratch(t, n - 1, depth),
            scratch(RING, depth),
            scratch(t, depth - 1),
            pltpu.VMEM((4, 8, D), f32),
            pltpu.VMEM((hops, 8, D), f32),
            scratch(high, depth, n, n),
            scratch(high, depth + 1, n, n),
            scratch(high, (n - 1) * n),
            scratch(high, n),
            scratch(high, n - 1),
            dma((21,)),
            dma((SPARE,)),
            dma((RING,)),
            dma((RING, n - 1)),
            dma((RING, n - 1)),
            dma((RING, n - 1)),
            dma((t, n - 1)),
            dma((RING, depth - 1)),
            dma((t, depth - 1)),
            dma((hops,)),
            dma((hops,)),
            pltpu.SemaphoreType.REGULAR,
            pltpu.SemaphoreType.REGULAR((n - 1,)),
            dma((high, depth)),
            dma((high, depth + 1)),
            dma((high, (n - 1) * n)),
            dma((high, (n - 1) * n)),
            dma((high, n - 1)),
            dma((high, n - 1)),
        ],
        compiler_params=pltpu.CompilerParams(
            collective_id=1, has_side_effects=True, vmem_limit_bytes=67043328
        ),
    )(*big, *small)


def hand_kernel(slabs, count, *refs):
    ins, gains = refs[:count], refs[count]
    outs, gain_outs = refs[count + 1 : 2 * count + 1], refs[2 * count + 1 : 2 * count + 4]
    buffers = refs[2 * count + 4 : 3 * count + 4]
    loaded, stored = refs[3 * count + 4 :]
    copies = []
    for k, (m, first, rows) in enumerate(slabs):
        at = pl.ds(first, rows)
        load = pltpu.make_async_copy(ins[m].at[at], buffers[m].at[at], loaded.at[k])
        load.start()
        copies.append((load, pltpu.make_async_copy(buffers[m].at[at], outs[m].at[at], stored.at[k])))
    entries = gain_outs[0].shape[-1]
    me = lax.axis_index("dp") * lax.axis_size("fsdp") + lax.axis_index("fsdp")
    turned = pltpu.roll(gains[...], lax.rem(gains.shape[1] - me * entries, gains.shape[1]), 1)
    for k, gain_out in enumerate(gain_outs):
        gain_out[...] = turned[k : k + 1, :entries]
    for load, store in copies:
        load.wait()
        store.start()
    for _, store in copies:
        store.wait()


def hand_over(arrays, gains):
    devices = lax.axis_size("dp") * lax.axis_size("fsdp")
    entries = gains.shape[1] // devices
    slabs = []
    for m, value in enumerate(arrays):
        parts = 4 if value.shape[0] % 64 == 0 and value.size >= 1 << 20 else 1
        rows = value.shape[0] // parts
        slabs += [(m, k * rows, rows) for k in range(parts)]
    hbm = pl.BlockSpec(memory_space=pltpu.HBM)
    vmem = pl.BlockSpec(memory_space=pltpu.VMEM)
    dma = pltpu.SemaphoreType.DMA
    found = pl.pallas_call(
        functools.partial(hand_kernel, slabs, len(arrays)),
        out_shape=[jax.ShapeDtypeStruct(v.shape, v.dtype) for v in arrays]
        + [jax.ShapeDtypeStruct((1, entries), gains.dtype)] * 3,
        in_specs=[hbm] * len(arrays) + [vmem],
        out_specs=[hbm] * len(arrays) + [vmem] * 3,
        scratch_shapes=[pltpu.VMEM(v.shape, v.dtype) for v in arrays]
        + [dma((len(slabs),)), dma((len(slabs),))],
        compiler_params=pltpu.CompilerParams(vmem_limit_bytes=67043328),
    )(*arrays, gains)
    return found[:-3], [v.reshape(-1) for v in found[-3:]]


def per_device(
    hidden_in,
    memory,
    cotangent,
    lengths,
    memory_count,
    causal_gain,
    causal_query,
    causal_key,
    causal_value,
    causal_output,
    source_gain,
    source_query,
    source_key,
    source_value,
    source_output,
    dense_gain,
    dense_expand,
    dense_reduce,
):
    pages, _, rows, width = hidden_in.shape
    slots = memory.shape[2]
    pad = -slots % 16
    source = jnp.pad(memory[:, 0], ((0, 0), (0, pad), (0, 0)))

    def flat(value):
        return value.reshape(pages * value.shape[1], value.shape[2])

    gains = jnp.stack([causal_gain, source_gain, dense_gain], axis=1)
    gains = jnp.pad(gains, ((0, 0), (0, 125)))
    sources = [
        causal_query,
        causal_key,
        causal_value,
        causal_output,
        source_key,
        source_value,
        source_query,
        source_output,
        dense_expand,
        dense_reduce,
        gains,
    ]
    names = [("gain", 0)]
    pieces = [(10, 0, 0, 0, False)]
    for first, count, name in ((4, 2, "kv"), (0, 4, "self"), (6, 2, "qo")):
        for k in range(count):
            pieces.append((first + k, 0, 0, len(names), False))
            names.append((name, k))
    for k in range(4):
        pieces.append((9, k * causal_query.shape[0], 0, len(names), k < 3))
    names.append(("reduce", 0))
    for k in range(4):
        pieces.append((8, 0, k * width, len(names), False))
        names.append(("expand", k))
    tokens = flat(hidden_in[:, 0])
    branch = flat(cotangent[:, 0])
    memory_rows = flat(source)
    page_length, page_count = lengths[:, 0], memory_count[:, 0]
    weights, saved, small = front(
        sources,
        pieces,
        names,
        [tokens, branch, memory_rows, page_count, page_length],
        (pages, rows, slots + pad),
    )
    result, hidden, pre, third, after_cross, cctx, second, cq, kv, after_self, ctx, first, qkv = saved
    gain_rows, lse_cross, lse_self = small
    big = [
        hidden,
        pre,
        third,
        branch,
        after_cross,
        cctx,
        second,
        cq,
        kv,
        memory_rows,
        after_self,
        ctx,
        first,
        qkv,
        tokens,
    ]
    place = {name: weight for name, weight in zip(names, weights)}
    big += [place[name, k] for name, count in KEPT for k in range(count)]
    small = [page_count, page_length, gain_rows, lse_cross, lse_self]
    (
        grad_reduce,
        grad_expand,
        grad_source_output,
        grad_source_query,
        grad_source_both,
        grad_causal_output,
        grad_causal,
        grad_gains,
        grad_inputs,
        grad_memory,
    ) = backward(big, small, (pages, rows, slots + pad, slots))
    (
        result,
        grad_inputs,
        grad_memory,
        grad_reduce,
        grad_expand,
        grad_source_output,
        grad_source_query,
        grad_source_both,
        grad_causal_output,
        grad_causal,
    ), grad_gains = hand_over(
        [
            result,
            grad_inputs,
            grad_memory,
            grad_reduce,
            grad_expand,
            grad_source_output,
            grad_source_query,
            grad_source_both,
            grad_causal_output,
            grad_causal,
        ],
        grad_gains,
    )
    return (
        result.reshape(hidden_in.shape),
        grad_inputs.reshape(pages, 1, rows, width),
        grad_memory.reshape(memory.shape),
        grad_gains[0],
        grad_causal[:, :width],
        grad_causal[:, width : 2 * width],
        grad_causal[:, 2 * width :],
        grad_causal_output,
        grad_gains[1],
        grad_source_query,
        grad_source_both[:, :width],
        grad_source_both[:, width:],
        grad_source_output,
        grad_gains[2],
        grad_expand,
        grad_reduce,
    )


def solution(mesh):
    pages = P(None, AXES, None, None)
    counts = P(None, AXES)
    gain = P(AXES)
    weight = P(AXES, None)
    return jax.shard_map(
        per_device,
        mesh=mesh,
        in_specs=(pages, pages, pages, counts, counts)
        + (gain, weight, weight, weight, weight)
        + (gain, weight, weight, weight, weight)
        + (gain, weight, weight),
        out_specs=(pages, pages, pages)
        + (gain, weight, weight, weight, weight)
        + (gain, weight, weight, weight, weight)
        + (gain, weight, weight),
        check_vma=False,
    )
```

```python
import functools

import jax
import jax.numpy as jnp
from jax import lax
from jax.experimental import pallas as pl
from jax.experimental.pallas import tpu as pltpu
from jax.sharding import PartitionSpec as P

HD = 64
EPS = 1e-05
AXES = ("dp", "fsdp")
CORES = 2
WIDTH = 1024
BLOCK = 256
MESH = pl.DeviceIdType.MESH


class Grid:
    def __init__(self):
        dp, fsdp = lax.axis_size("dp"), lax.axis_size("fsdp")
        self.n = dp // CORES
        self.depth = fsdp // self.n
        self.devices = dp * fsdp
        d, f = lax.axis_index("dp"), lax.axis_index("fsdp")
        self.at = (d // CORES, d % CORES, f // self.n, f % self.n)

    def device(self, y, c, z, x):
        return (y * CORES + c, z * self.n + x)

    def step_z(self, k):
        y, c, z, x = self.at
        return self.device(y, c, lax.rem(z + k, self.depth), x)

    def step_plane(self, k, swap):
        y, c, z, x = self.at
        odd = lax.rem(c + swap, 2)
        return self.device(
            lax.rem(y + k * odd, self.n), c, z, lax.rem(x + k * (1 - odd), self.n)
        )

    def partner(self):
        y, c, z, x = self.at
        return self.device(y, 1 - c, z, x)

    def place(self, a, b):
        y, c, z, x = self.at
        ky = a * c + b * (1 - c)
        kx = a * (1 - c) + b * c
        return lax.rem(y + ky, self.n), lax.rem(x + kx, self.n)

    def peers(self):
        line = [self.step_z(k) for k in range(1, self.depth)]
        plane = [self.step_plane(k, s) for s in (0, 1) for k in range(1, self.n)]
        return line + plane + [self.partner()]

    def meet(self):
        barrier = pltpu.get_barrier_semaphore()
        peers = self.peers()
        for peer in peers:
            pl.semaphore_signal(barrier, inc=1, device_id=peer, device_id_type=MESH)
        pl.semaphore_wait(barrier, len(peers))


def remote(src, dst, send_sem, recv_sem, device):
    return pltpu.make_async_remote_copy(
        src_ref=src,
        dst_ref=dst,
        send_sem=send_sem,
        recv_sem=recv_sem,
        device_id=device,
        device_id_type=MESH,
    )


def started(*copy):
    made = remote(*copy)
    made.start()
    return made


class Plan:
    def __init__(self):
        self.calls = {}

    def add(self, tick, rank, call, *args):
        self.calls.setdefault((tick, rank), []).append((call, args))

    def run(self):
        for key in sorted(self.calls):
            for call, args in self.calls[key]:
                call(*args)


def times(left, right):
    return jnp.dot(left, right, preferred_element_type=jnp.float32)


def times_transposed(left, right):
    return lax.dot_general(left, right, (((1,), (1,)), ((), ())), preferred_element_type=jnp.float32)


def transposed_times(left, right):
    return lax.dot_general(left, right, (((0,), (0,)), ((), ())), preferred_element_type=jnp.float32)


def standardize(value):
    centred = value - jnp.mean(value, axis=-1, keepdims=True)
    spread = jnp.mean(centred * centred, axis=-1, keepdims=True)
    row_scale = lax.rsqrt(spread + EPS)
    return centred * row_scale, row_scale


def standardize_back(grad, unit, row_scale, gain):
    grad_unit = grad * gain
    inner = jnp.mean(grad_unit * unit, axis=-1, keepdims=True)
    return row_scale * (grad_unit - jnp.mean(grad_unit, axis=-1, keepdims=True) - unit * inner)


def lane_window(col, pair):
    return pl.ds(pl.multiple_of(col + pair * 2 * HD, 2 * HD), 2 * HD)


def both_heads(lane, value):
    zero = jnp.zeros_like(value)
    return jnp.concatenate(
        [jnp.where(lane < HD, value, zero), jnp.where(lane < HD, zero, value)], axis=0
    )


def causal(length, live):
    key = lax.broadcasted_iota(jnp.int32, (length, 2 * length), 0)
    query = lax.rem(lax.broadcasted_iota(jnp.int32, (length, 2 * length), 1), length)
    return (key <= query) & (key < live)


STRIP = 32


def strips(count, body, carry=None):
    def one(k, carry):
        return body(pl.ds(pl.multiple_of(k * STRIP, STRIP), STRIP), carry)

    return lax.fori_loop(0, count // STRIP, one, carry)


def bands(count, body):
    def one(k, carry):
        body(pl.multiple_of(k * 2 * BLOCK, BLOCK))
        return carry

    lax.fori_loop(0, count // (2 * BLOCK), one, 0)


FLAT_AHEAD = 2
TALL_GAP = 3


def front_kernel(dims, chunks, names_, n_src, *refs):
    pages, length, slots = dims
    n_out = len(names_)
    it = iter(refs)

    def take(k):
        return [next(it) for _ in range(k)]

    shards = take(n_src)
    x_in, cot_in, memory_in, counts, lengths = take(5)
    outs = take(n_out)
    saved_out = take(13)
    gains, lse_cross, lse_self = take(3)
    saved = take(13)
    (result, hidden, pre, third, after_cross, cctx, second, cq, kv, after_self, ctx, first, qkv) = saved
    x_bf, cot, memory, w_a, w_b, w_d, w_gain, total_out, g_hidden = take(9)
    local, zs, zr, ps, pr, qs, qr, cs, cr, us, ur, ds, dr, loads_sem, stores_sem = take(15)
    f32, bf16 = jnp.float32, jnp.bfloat16
    grid = Grid()
    n, depth = grid.n, grid.depth
    y, c, z, x = grid.at
    tokens, D = x_bf.shape
    loads = {}

    def fetch(name, src, dst, slot):
        loads[name] = pltpu.make_async_copy(src, dst, loads_sem.at[slot])
        loads[name].start()

    def need(*names):
        for name in names:
            copy = loads.pop(name, None)
            if copy is not None:
                copy.wait()

    fetch("x", x_in, x_bf, 0)
    fetch("cot", cot_in, cot, 1)
    fetch("memory", memory_in, memory, 2)
    grid.meet()
    pending = []

    def send(*copy):
        made = started(*copy)
        pending.append(made)
        return made

    def window(i):
        _, r0, nr, c0, nc, _, o0, _ = chunks[i]
        return pl.ds(r0, nr), pl.ds(o0, nc)

    def out(i):
        return outs[chunks[i][5]]

    def shard(i):
        m, r0, nr, c0, nc, _, _, _ = chunks[i]
        return shards[m].at[pl.ds(r0, nr), pl.ds(c0, nc)]

    def block(i, yy, zz, xx):
        return out(i).at[(yy, c, zz, xx) + window(i)]

    def back(a, b):
        return grid.place((n - a) % n, (n - b) % n)

    def column(i, a, b):
        yy, xx = back(a, b)
        return out(i).at[(yy, c, slice(None), xx) + window(i)]

    def share(i, a, b):
        piece = column(i, a, b)
        slot = a * n + b
        return send(piece, piece, cs.at[i, slot], cr.at[i, slot], grid.partner())

    zc, pc, qc, cc, lc = {}, {}, {}, {}, {}

    def keep_own(i):
        lc[i] = pltpu.make_async_copy(shard(i), block(i, y, z, x), local.at[i])
        lc[i].start()

    def stage_z(i):
        zc[i] = [
            send(shard(i), block(i, y, z, x), zs.at[i, k - 1], zr.at[i, k - 1], grid.step_z(k))
            for k in range(1, depth)
        ]
        keep_own(i)

    def stage_p(i):
        for copy in zc[i]:
            copy.wait_recv()
        lc[i].wait()
        piece = column(i, 0, 0)
        pc[i] = [
            send(piece, piece, ps.at[i, a - 1], pr.at[i, a - 1], grid.step_plane(a, 0))
            for a in range(1, n)
        ]
        qc[i] = [
            send(piece, piece, qs.at[i, b - 1], qr.at[i, b - 1], grid.step_plane(b, 1))
            for b in range(1, n)
        ]
        cc[i] = [share(i, 0, 0)]

    def stage_q(i):
        for a in range(1, n):
            pc[i][a - 1].wait_recv()
            piece = column(i, a, 0)
            for b in range(1, n):
                j = a * (n - 1) + b - 1
                qc[i].append(
                    send(piece, piece, qs.at[i, j], qr.at[i, j], grid.step_plane(b, 1))
                )
            cc[i].append(share(i, a, 0))

    def stage_c(i):
        j = 0
        for a in range(n):
            for b in range(1, n):
                qc[i][j].wait_recv()
                j += 1
                cc[i].append(share(i, a, b))

    def tall_p(i):
        keep_own(i)
        pc[i] = [
            send(shard(i), block(i, y, z, x), ps.at[i, a - 1], pr.at[i, a - 1], grid.step_plane(a, 0))
            for a in range(1, n)
        ]

    def tall_q(i):
        lc[i].wait()
        qc[i] = []
        for a in range(n):
            if a:
                pc[i][a - 1].wait_recv()
            yy, xx = back(a, 0)
            piece = block(i, yy, z, xx)
            for b in range(1, n):
                j = a * (n - 1) + b - 1
                qc[i].append(
                    send(piece, piece, qs.at[i, j], qr.at[i, j], grid.step_plane(b, 1))
                )

    def layer(i, k, j):
        zz = lax.rem(z + (depth - j if k == 0 else j), depth)
        return out(i).at[(slice(None), c, zz, slice(None)) + window(i)]

    def hop(i, k, j):
        piece = layer(i, k, j)
        send_sem, recv_sem = ((us, ur), (ds, dr))[k]
        to = grid.device(y, c, lax.rem(z + (1 if k == 0 else depth - 1), depth), x)
        return remote(piece, piece, send_sem.at[i, j], recv_sem.at[i, j], to)

    def share_layer(i, k, j):
        piece = layer(i, k, j)
        slot = k * (depth - 1) + j
        return remote(piece, piece, cs.at[i, slot], cr.at[i, slot], grid.partner())

    def level(k):
        return z if k == 0 else depth - 1 - z

    def climb(i, j):
        if j == 0:
            for copy in qc[i]:
                copy.wait_recv()
            share_layer(i, 0, 0).start()
        for k in (0, 1):
            if j:

                @pl.when(level(k) >= j)
                def _():
                    hop(i, k, j - 1).wait_recv()
                    share_layer(i, k, j).start()

            if j < depth - 1:

                @pl.when((level(k) >= j) & (level(k) < depth - 1))
                def _():
                    hop(i, k, j).start()

    def each_layer(i, call, hops):
        call(share_layer(i, 0, 0))
        for k in (0, 1):
            for j in range(depth - 1):
                if hops:

                    @pl.when((level(k) >= j) & (level(k) < depth - 1))
                    def _():
                        call(hop(i, k, j))

                @pl.when(level(k) >= j + 1)
                def _():
                    call(share_layer(i, k, j + 1))

    there = set()

    def arrive(*ids):
        for i in ids:
            if i in there:
                continue
            there.add(i)
            if chunks[i][7]:
                each_layer(i, lambda copy: copy.wait_recv(), False)
            else:
                for copy in cc[i]:
                    copy.wait_recv()

    def pull(name, k, dst, slot):
        ids = held[name][k]
        arrive(*ids)
        fetch((name, k), out(ids[0]), dst, slot)

    def store(name, slot):
        src = saved[name]
        made = pltpu.make_async_copy(src, saved_out[name], stores_sem.at[slot])
        made.start()
        stores.append(made)

    stores = []
    lane = lax.broadcasted_iota(jnp.int32, (length, 2 * HD), 1)

    def attention(page, pair, q_ref, k_ref, k_row, k_rows, k_col, v_col, allowed, to, lse):
        q_at, k_at = pl.ds(page * length, length), pl.ds(k_row, k_rows)
        q = both_heads(lane, q_ref[q_at, lane_window(0, pair)])
        keys = k_ref[k_at, lane_window(k_col, pair)]
        values = k_ref[k_at, lane_window(v_col, pair)]
        scores = times_transposed(keys, q) * HD ** (-0.5)
        scores = jnp.where(allowed, scores, -1000000000.0)
        top = jnp.max(scores, axis=0, keepdims=True)
        expos = jnp.exp(scores - top)
        sum_ = jnp.sum(expos, axis=0, keepdims=True)
        probs = (expos * (1.0 / sum_)).astype(bf16)
        lse[pl.ds(page * (D // HD // 2) + pair, 1), :] = top + jnp.log(sum_)
        found = transposed_times(probs, values)
        to[q_at, lane_window(0, pair)] = jnp.where(lane < HD, found[:length], found[length:]).astype(bf16)

    def read_gains():
        arrive(*held["gain"][0])
        copy = pltpu.make_async_copy(out(held["gain"][0][0]), w_gain, loads_sem.at[3])
        copy.start()
        copy.wait()
        columns = w_gain.reshape(D, 128)[...].astype(f32)
        gains[...] = columns.T[:8]

    def project(left, weight, col, count, to, to_col):
        def body(at):
            w_at = pl.ds(pl.multiple_of(col + at, BLOCK), 2 * BLOCK)
            to_at = pl.ds(pl.multiple_of(to_col + at, BLOCK), 2 * BLOCK)
            to[:, to_at] = times(left[...], weight[:, w_at]).astype(to.dtype)

        bands(count, body)

    def first_norm():
        need("x")
        gain = gains[pl.ds(0, 1), :]

        def body(at, carry):
            unit, _ = standardize(x_bf[at].astype(f32))
            first[at] = (unit * gain).astype(bf16)
            return carry

        strips(tokens, body, 0)

    def self_project(k):
        need(("self", k))
        project(first, flat_b, k * D, D, qkv, k * D)

    def self_attention(page):
        allowed = causal(length, lengths[page])

        def body(pair, carry):
            attention(page, pair, qkv, qkv, page * length, length, D, 2 * D, allowed, ctx, lse_self)
            return carry

        lax.fori_loop(0, D // (2 * HD), body, 0)

    def residual(left, weight, col, base, to):
        def body(at):
            here = pl.ds(at, 2 * BLOCK)
            w_at = pl.ds(pl.multiple_of(col + at, BLOCK), 2 * BLOCK)
            to[:, here] = base[:, here].astype(f32) + times(left[...], weight[:, w_at])

        bands(D, body)

    def self_out():
        need(("self", 3))
        residual(ctx, flat_b, 3 * D, x_bf, after_self)
        gain = gains[pl.ds(1, 1), :]

        def body(at, carry):
            unit, _ = standardize(after_self[at])
            second[at] = (unit * gain).astype(bf16)
            return carry

        strips(tokens, body, 0)

    def memory_project(page, part):
        need("memory", ("kv", 0), ("kv", 1))
        span = -(-slots // 32) * 16
        at = pl.ds(page * slots + part * span, min(span, slots - part * span))

        def body(col):
            here = pl.ds(col, 2 * BLOCK)
            kv[at, here] = times(memory[at, :], flat_a[:, here]).astype(bf16)

        bands(2 * D, body)

    def cross_query():
        need(("qo", 0))
        project(second, flat_a, 0, D, cq, 0)

    def cross_attention(page, part):
        allowed = lax.broadcasted_iota(jnp.int32, (slots, 2 * length), 0) < counts[page]
        pairs = D // (2 * HD) // 2

        def body(k, carry):
            pair = part * pairs + k
            attention(page, pair, cq, kv, page * slots, slots, 0, D, allowed, cctx, lse_cross)
            return carry

        lax.fori_loop(0, pairs, body, 0, unroll=2)

    def cross_out():
        need(("qo", 1))
        residual(cctx, flat_a, D, after_self, after_cross)
        gain = gains[pl.ds(2, 1), :]

        def body(at, carry):
            unit, _ = standardize(after_cross[at])
            third[at] = (unit * gain).astype(bf16)
            return carry

        strips(tokens, body, 0)

    def hidden_grad(k):
        need("cot", ("reduce", 0))

        def body(at):
            here = pl.ds(pl.multiple_of(k * D + at, BLOCK), 2 * BLOCK)
            g_hidden[:, here] = times_transposed(cot[...], flat_d[here, :])

        bands(D, body)

    def expand(k):
        need(("expand", k))

        def body(j, carry):
            at = pl.ds(pl.multiple_of(k * D + j * 2 * BLOCK, BLOCK), 2 * BLOCK)
            value = times(third[...], flat_b[:, at])
            below = 0.5 + 0.5 * lax.erf(value * 0.5**0.5)
            hidden[:, at] = (value * below).astype(bf16)
            density = jnp.exp(-0.5 * value * value) * 0.3989422804014327
            pre[:, at] = (g_hidden[:, at] * (below + value * density)).astype(bf16)
            return carry

        lax.fori_loop(0, D // (2 * BLOCK), body, 0)

    def reduce_out(k):
        at = pl.ds(k * D, D)

        def body(col):
            here = pl.ds(col, 2 * BLOCK)
            value = after_cross[:, here] if k == 0 else total_out[:, here]
            value = value + times(hidden[:, at], flat_d[at, here])
            if k < 3:
                total_out[:, here] = value
            else:
                result[:, here] = value.astype(bf16)

        bands(D, body)

    flat_a, flat_b, flat_d = w_a.reshape(D, 2 * D), w_b.reshape(D, 4 * D), w_d.reshape(4 * D, D)

    held = {}
    for i, chunk in enumerate(chunks):
        name, k = names_[chunk[5]]
        held.setdefault(name, {}).setdefault(k, []).append(i)

    plan = Plan()
    flat = [i for i, chunk in enumerate(chunks) if not chunk[7]]
    tall = [i for i, chunk in enumerate(chunks) if chunk[7]]
    tick = {}
    for t, i in enumerate(flat):
        t = max(t - 1, 0)
        plan.add(t - FLAT_AHEAD, 0, stage_z, i)
        plan.add(t, 2, stage_p, i)
        plan.add(t + 1, 4, stage_q, i)
        plan.add(t + 3, 6, stage_c, i)
        tick[i] = t + 4
    for t, i in enumerate(tall):
        t = TALL_GAP * t - 1
        plan.add(t, 1, tall_p, i)
        plan.add(t + 2, 3, tall_q, i)
        for h in range(depth):
            plan.add(t + 4 + 2 * h, 5, climb, i, h)
        tick[i] = t + 4 + 2 * (depth - 1) + 1

    def ready(name, k):
        return max(tick[i] for i in held[name][k])

    def part(buffer, k, width):
        return buffer.at[:, :, :, :, :, pl.ds(k * width, width)]

    clock = [0]

    def then(when, call, *args):
        clock[0] = max(clock[0] + 1, 3 * when)
        plan.add(clock[0] // 3, 3 + 2 * (clock[0] % 3), call, *args)
        return clock[0] // 3

    def keep(*names):
        for name in names:
            store(name, name)

    plan.add(ready("gain", 0), 8, read_gains)
    plan.add(ready("gain", 0), 8, first_norm)
    for k in range(2):
        plan.add(ready("kv", k), 8, pull, "kv", k, part(w_a, k, D), 8 + k)
    for k in range(4):
        plan.add(ready("self", k), 8, pull, "self", k, part(w_b, k, D), 4 + k)
    for page in range(pages):
        for half in range(2):
            kv_done = then(ready("kv", 1) + 1, memory_project, page, half)
    for k in range(3):
        then(ready("self", k) + 1, self_project, k)
    for page in range(pages):
        then(0, self_attention, page)
    self_done = then(ready("self", 3) + 1, self_out)
    plan.add(self_done, 9, keep, 8, 10, 11, 12, 9, 6)
    for k in range(2):
        plan.add(max(ready("qo", k), kv_done + 1), 8, pull, "qo", k, part(w_a, k, D), 10 + k)
    for k in range(4):
        plan.add(
            max(ready("expand", k), self_done + 1), 8, pull, "expand", k, part(w_b, k, D), 12 + k
        )
    plan.add(ready("reduce", 0), 8, pull, "reduce", 0, w_d, 16)
    then(max(ready("qo", 0), kv_done + 1) + 1, cross_query)
    for page in range(pages):
        for half in range(2):
            then(0, cross_attention, page, half)
    cross_done = then(max(ready("qo", 1), kv_done + 1) + 1, cross_out)
    plan.add(cross_done, 9, keep, 3, 4, 5, 7)
    for k in range(4):
        plan.add(ready("reduce", 0) + 1 + k // 2, 9, hidden_grad, k)
    for k in range(4):
        then(max(ready("expand", k), self_done + 1) + 1, expand, k)
        last = then(0, reduce_out, k)
    plan.add(last, 10, keep, 1, 2, 0)
    plan.run()
    for i in flat:
        arrive(i)
    for i in tall:
        arrive(i)
        each_layer(i, lambda copy: copy.wait_send(), True)
    for copy in pending:
        copy.wait_send()
    for copy in stores:
        copy.wait()


def front(sources, pieces, names, tokens_in, shapes):
    dp, fsdp = lax.axis_size("dp"), lax.axis_size("fsdp")
    n = dp // CORES
    depth = fsdp // n
    rows = sources[0].shape[0]
    pages, length, slots = shapes
    tokens, D = pages * length, WIDTH
    groups = [(4 * rows if name == "reduce" else rows, 128 if name == "gain" else D) for name, _ in names]
    chunks = [(m, r0, rows, c0, groups[o][1], o, 0, tall) for m, r0, c0, o, tall in pieces]
    t = len(chunks)
    slot_count = max(n * n, 2 * depth - 1)
    shapes_ = (depth - 1, depth - 1, n - 1, n - 1, n * (n - 1), n * (n - 1), slot_count, slot_count)
    shapes_ += (depth - 1,) * 4
    dma = pltpu.SemaphoreType.DMA
    f32, bf16 = jnp.float32, jnp.bfloat16
    lead = (n, CORES, depth, n)
    saved = [
        ((tokens, D), bf16),
        ((tokens, 4 * D), bf16),
        ((tokens, 4 * D), bf16),
        ((tokens, D), bf16),
        ((tokens, D), f32),
        ((tokens, D), bf16),
        ((tokens, D), bf16),
        ((tokens, D), bf16),
        ((pages * slots, 2 * D), bf16),
        ((tokens, D), f32),
        ((tokens, D), bf16),
        ((tokens, D), bf16),
        ((tokens, 3 * D), bf16),
    ]
    small = [((8, D), f32)] + [((pages * D // HD // 2, 2 * length), f32)] * 2
    hbm = pl.BlockSpec(memory_space=pltpu.HBM)
    vmem = pl.BlockSpec(memory_space=pltpu.VMEM)
    smem = pl.BlockSpec(memory_space=pltpu.SMEM)
    found = pl.pallas_call(
        functools.partial(front_kernel, shapes, chunks, names, len(sources)),
        out_shape=[jax.ShapeDtypeStruct(lead + g, bf16) for g in groups]
        + [jax.ShapeDtypeStruct(*s) for s in saved + small],
        in_specs=[vmem] * len(sources) + [hbm] * 3 + [smem] * 2,
        out_specs=[hbm] * (len(groups) + len(saved)) + [vmem] * 3,
        scratch_shapes=[pltpu.VMEM(*s) for s in saved]
        + [
            pltpu.VMEM((tokens, D), bf16),
            pltpu.VMEM((tokens, D), bf16),
            pltpu.VMEM((pages * slots, D), bf16),
            pltpu.VMEM(lead + (rows, 2 * D), bf16),
            pltpu.VMEM(lead + (rows, 4 * D), bf16),
            pltpu.VMEM(lead + (4 * rows, D), bf16),
            pltpu.VMEM(lead + (rows, 128), bf16),
            pltpu.VMEM((tokens, D), f32),
            pltpu.VMEM((tokens, 4 * D), f32),
            dma((t,)),
        ]
        + [dma((t, k)) for k in shapes_]
        + [dma((20,)), dma((13,))],
        compiler_params=pltpu.CompilerParams(
            collective_id=0, has_side_effects=True, vmem_limit_bytes=67043328
        ),
    )(*sources, *tokens_in)
    weights = [
        w.reshape(dp * fsdp * g[0], g[1]) for w, g in zip(found[: len(groups)], groups)
    ]
    return weights, found[len(groups) : len(groups) + len(saved)], found[len(groups) + len(saved) :]


RING = 4
KEPT = (("self", 4), ("kv", 2), ("qo", 2), ("expand", 4))
SPARE = 2
BACK_TALL = (1, 5, 9)
TALL_STEP = 2


def back_kernel(dims, *refs):
    pages, length, slots = dims
    it = iter(refs)

    def take(k):
        return [next(it) for _ in range(k)]

    (hidden_in, pre_in, third_in, out_in, cross_in, cctx_in, second_in, cq_in, kv_in, memory_in,
     self_in, ctx_in, first_in, qkv_in, x_in) = take(15)
    kept = {name: take(count) for name, count in KEPT}
    counts, lengths, gains, lse_cross, lse_self = take(5)
    grad_outs = take(7)
    gain_out, input_out, memory_out = take(3)
    (hidden, pre, third, out_grad, cross, cctx, second, cq, kv, memory, after_self, ctx, first, qkv,
     w_a, w_b, branch, g_ctx, stage, g_norm) = take(20)
    send0, got0, parts, got1, halves, got2, line, got3, gain_sum, gain_got = take(10)
    tower, tower_got, tower_got1, tower_half, tower_got2 = take(5)
    local, s0, r0, s1, r1, s2, r2, s3, r3, gs, gr, free, free1 = take(13)
    sz, rz, sa, ra, sb, rb = take(6)

    grid = Grid()
    n, depth = grid.n, grid.depth
    y, c, z, x = grid.at
    rows, width = send0.shape[-2:]
    f32, bf16 = jnp.float32, jnp.bfloat16
    copies, loads = {}, {}

    def fetch(name, src, dst, slot):
        loads[name] = pltpu.make_async_copy(src, dst, local.at[slot])
        loads[name].start()

    def need(*names):
        for name in names:
            copy = loads.pop(name, None)
            if copy is not None:
                copy.wait()

    D = third.shape[1]
    fetch("hidden", hidden_in, hidden, 0)
    fetch("out", out_in, out_grad, 1)
    fetch("pre", pre_in, pre, 2)
    fetch("third", third_in, third, 3)

    def weights(label, *moves):
        for name, k, buffer, half in moves:
            slot = 15 + half + (0 if buffer is w_a else 2)
            fetch((label, slot), kept[name][k], buffer.at[:, pl.ds(half * D, D)], slot)

    def need_all(label):
        need(*[key for key in list(loads) if key[0] == label])

    weights("expand", *[("expand", k, (w_a, w_b)[k // 2], k % 2) for k in range(4)])
    fetch("cross", cross_in, cross, 4)
    grid.meet()
    fetch("cctx", cctx_in, cctx, 5)
    fetch("cq", cq_in, cq, 7)
    fetch("kv", kv_in, kv, 8)
    fetch("second", second_in, second, 6)
    fetch("memory", memory_in, memory, 9)
    fetch("self", self_in, after_self, 10)
    fetch("ctx", ctx_in, ctx, 11)
    fetch("first", first_in, first, 12)
    fetch("qkv", qkv_in, qkv, 13)

    chunks = []
    wide = hidden.shape[1] // grid.devices
    for col in range(0, D, width * rows // wide):
        chunks.append((0, hidden, out_grad, col, ("hidden", "out")))
    for col in range(0, pre.shape[1], width):
        chunks.append((1, third, pre, col, ("third", "pre")))
    OUT_CHUNK = len(chunks)
    chunks.append((2, cctx, branch, 0, ("cctx",)))
    chunks.append((3, second, cq, 0, ("second",)))
    chunks.append((4, memory, kv, 0, ("memory",)))
    chunks.append((4, memory, kv, D, ()))
    chunks.append((5, ctx, branch, 0, ("ctx",)))
    for col in range(0, 3 * D, width):
        chunks.append((6, first, qkv, col, ("first",)))
    total = len(chunks)
    tall = {i: k for k, i in enumerate(BACK_TALL)}
    flat = {}
    ticks = []
    for i in range(total):
        if i in tall:
            ticks.append(len(flat) - 1)
        else:
            ticks.append(len(flat))
            flat[i] = len(flat)
    by_flat = {f: i for i, f in flat.items()}

    def products(i, core, emit):
        _, left, right, col, names = chunks[i]
        need(*names)
        own = left.shape[1] // grid.devices
        span = left.shape[1] // (n * CORES)
        lanes = width * rows // own

        band = min(lanes, 2 * BLOCK)

        def body(step, carry):
            yy, j = step // (lanes // band), step % (lanes // band)
            at = pl.multiple_of((yy * CORES + core) * span, min(span, BLOCK))
            value = transposed_times(
                left[:, pl.ds(at, span)],
                right[:, pl.ds(pl.multiple_of(col + j * band, BLOCK), band)],
            )
            for k in range(depth * n):
                for part in range(own // rows):
                    top = k * own + part * rows
                    lane = pl.multiple_of(part * lanes + j * band, BLOCK)
                    emit(yy, k // n, k % n, lane, band, value[top : top + rows])
            return carry

        lax.fori_loop(0, n * (lanes // band), body, 0)

    def reuse(i, stage, ring):
        before = i - ring if stage == 0 else by_flat.get(flat[i] - ring, -1)
        if before >= 0:
            for copy in copies[before, stage]:
                copy.wait_send()

    def credit(i):
        if i + RING < total:
            pl.semaphore_signal(free, inc=1, device_id=grid.partner(), device_id_type=MESH)

    def stage0(i):
        s = i % SPARE
        reuse(i, 0, SPARE)

        def emit(yy, zz, xx, lane, lanes, value):
            send0[s, yy, zz, xx, :, pl.ds(lane, lanes)] = value.astype(bf16)

        products(i, 1 - c, emit)
        if i >= RING:
            pl.semaphore_wait(free, 1)
        copies[i, 0] = [started(send0.at[s], got0.at[i % RING], s0.at[s], r0.at[i % RING], grid.partner())]

    def relative(yy, xx):
        to_y = lax.rem(yy - y + n, n)
        to_x = lax.rem(xx - x + n, n)
        return to_x * (1 - c) + to_y * c, to_y * (1 - c) + to_x * c

    def stage1(i):
        s, g = flat[i] % RING, i % RING
        reuse(i, 1, RING)
        copies[i, 0][0].wait_recv()

        def emit(yy, zz, xx, lane, lanes, value):
            value = value + got0[g, yy, zz, xx, :, pl.ds(lane, lanes)].astype(f32)
            a, b = relative(yy, xx)
            parts[s, a, b, zz, :, pl.ds(lane, lanes)] = value.astype(bf16)

        products(i, c, emit)
        credit(i)
        copies[i, 1] = []
        for a in range(1, n):
            if flat[i] >= RING:
                pl.semaphore_wait(free1.at[a - 1], 1)
            copies[i, 1].append(
                started(
                    parts.at[s, a],
                    got1.at[s, a - 1],
                    s1.at[s, a - 1],
                    r1.at[s, a - 1],
                    grid.step_plane(a, 0),
                )
            )

    def stage2(i):
        s, f = flat[i] % RING, flat[i]
        reuse(i, 2, RING)
        for copy in copies[i, 1]:
            copy.wait_recv()
        copies[i, 2] = []
        for b in list(range(1, n)) + [0]:

            def body(zz, carry):
                value = parts[s, 0, b, zz].astype(f32)
                for a in range(1, n):
                    value = value + got1[s, a - 1, b, zz].astype(f32)
                halves[s, b, zz] = value.astype(bf16)
                return carry

            lax.fori_loop(0, depth, body, 0)
            if b:
                copies[i, 2].append(
                    started(
                        halves.at[s, b],
                        got2.at[f, b - 1],
                        s2.at[s, b - 1],
                        r2.at[f, b - 1],
                        grid.step_plane(b, 1),
                    )
                )
        if f + RING < len(flat):
            for a in range(1, n):
                pl.semaphore_signal(
                    free1.at[a - 1], inc=1, device_id=grid.step_plane(n - a, 0), device_id_type=MESH
                )

    def stage3(i):
        s, f = flat[i] % RING, flat[i]
        reuse(i, 3, RING)
        for copy in copies[i, 2]:
            copy.wait_recv()

        def body(zz, carry):
            value = halves[s, 0, zz].astype(f32)
            for b in range(1, n):
                value = value + got2[f, b - 1, zz].astype(f32)
            line[s, zz] = value.astype(bf16)
            return carry

        lax.fori_loop(0, depth, body, 0)
        copies[i, 3] = [
            started(
                line.at[s, lax.rem(z + k, depth)],
                got3.at[f, k - 1],
                s3.at[s, k - 1],
                r3.at[f, k - 1],
                grid.step_z(k),
            )
            for k in range(1, depth)
        ]

    def tall1(i):
        k, g = tall[i], i % RING
        copies[i, 0][0].wait_recv()

        def emit(yy, zz, xx, lane, lanes, value):
            value = value + got0[g, yy, zz, xx, :, pl.ds(lane, lanes)].astype(f32)
            tower[k, zz, yy, xx, :, pl.ds(lane, lanes)] = value.astype(bf16)

        products(i, c, emit)
        credit(i)

    def level(up):
        return z if up else depth - 1 - z

    def pass_on(i, up, d):
        k = tall[i]
        target = lax.rem(z + (d if up else depth - d), depth)
        slot = target if up or d > 1 else depth
        to = grid.device(y, c, lax.rem(z + (1 if up else depth - 1), depth), x)
        return remote(
            tower.at[k, target], tower_got.at[k, slot], sz.at[k, target], rz.at[k, slot], to
        )

    def absorb(i, target, slot):
        k = tall[i]
        remote(
            tower.at[k, target], tower_got.at[k, slot], sz.at[k, target], rz.at[k, slot], grid.partner()
        ).wait_recv()

        def body(j, carry):
            yy, xx = j // n, j % n
            value = tower[k, target, yy, xx].astype(f32) + tower_got[k, slot, yy, xx].astype(f32)
            tower[k, target, yy, xx] = value.astype(bf16)
            return carry

        lax.fori_loop(0, n * n, body, 0)

    def tall_z(i, d):
        for up in (True, False):

            @pl.when(level(up) + d < depth)
            def _():
                target = lax.rem(z + (d if up else depth - d), depth)

                @pl.when(level(up) > 0)
                def _():
                    absorb(i, target, target)

                pass_on(i, up, d).start()

    def tall_plane(i):
        k = tall[i]

        @pl.when(z > 0)
        def _():
            absorb(i, z, z)

        @pl.when(z < depth - 1)
        def _():
            absorb(i, z, depth)

        copies[i, 1] = []
        for a in range(1, n):
            for b in range(n):
                yy, xx = grid.place(a, b)
                j = (a - 1) * n + b
                copies[i, 1].append(
                    started(
                        tower.at[k, z, yy, xx],
                        tower_got1.at[k, j],
                        sa.at[k, j],
                        ra.at[k, j],
                        grid.step_plane(a, 0),
                    )
                )

    def tall_half(i):
        k = tall[i]
        for copy in copies[i, 1]:
            copy.wait_recv()
        copies[i, 2] = []
        for b in list(range(1, n)) + [0]:
            yy, xx = grid.place(0, b)
            value = tower[k, z, yy, xx].astype(f32)
            for a in range(1, n):
                value = value + tower_got1[k, (a - 1) * n + b].astype(f32)
            tower_half[k, b] = value.astype(bf16)
            if b:
                copies[i, 2].append(
                    started(
                        tower_half.at[k, b],
                        tower_got2.at[k, b - 1],
                        sb.at[k, b - 1],
                        rb.at[k, b - 1],
                        grid.step_plane(b, 1),
                    )
                )

    def tall_out(i):
        k = tall[i]
        for copy in copies[i, 2]:
            copy.wait_recv()
        value = tower_half[k, 0].astype(f32)
        for b in range(1, n):
            value = value + tower_got2[k, b - 1].astype(f32)
        put_out(i, value)

    def put_out(i, value):
        m, left, _, col, _ = chunks[i]
        own = left.shape[1] // grid.devices
        if own == rows:
            grad_outs[m][:, pl.ds(col, width)] = value
        else:
            for part in range(own // rows):
                grad_outs[m][pl.ds(part * rows, rows), pl.ds(col, BLOCK)] = value[
                    :, part * BLOCK : (part + 1) * BLOCK
                ]

    def stage4(i):
        for copy in copies[i, 3]:
            copy.wait_recv()
        value = line[flat[i] % RING, z].astype(f32)
        for k in range(1, depth):
            value = value + got3[flat[i], k - 1].astype(f32)
        put_out(i, value)

    moves = [
        [grid.partner()],
        [grid.step_plane(a, 0) for a in range(1, n)],
        [grid.step_plane(a, 1) for a in range(1, n)],
        [grid.step_z(k) for k in range(1, depth)],
        [],
    ]
    start = [0, 1, n, 2 * n - 1, 2 * n + depth - 2]

    def gain_step(h):
        value = gain_sum[min(h, 3)]
        if h:
            for j, copy in enumerate(copies["gain", h - 1]):
                copy.wait_recv()
                value = value + gain_got[start[h - 1] + j]
        if h == len(moves) - 1:
            gain_out[...] = value
        elif h:
            gain_sum[h] = value
        if h < len(moves) - 2:
            gain_sum[h + 1] = value
        copies["gain", h] = [
            started(
                gain_sum.at[h],
                gain_got.at[start[h] + j],
                gs.at[start[h] + j],
                gr.at[start[h] + j],
                device,
            )
            for j, device in enumerate(moves[h])
        ]

    def context_grad(weight, col):
        g_ctx[...] = times_transposed(branch[...], weight[:, pl.ds(col, D)]).astype(bf16)

    lane = lax.broadcasted_iota(jnp.int32, (length, 2 * HD), 1)
    scale = HD ** (-0.5)

    def attention(page, pair, q_ref, q_col, k_ref, k_row, k_rows, k_col, v_col, lse, allowed):
        q_at = pl.ds(page * length, length)
        k_at = pl.ds(k_row, k_rows)
        q = both_heads(lane, q_ref[q_at, lane_window(q_col, pair)])
        g = both_heads(lane, g_ctx[q_at, lane_window(0, pair)])
        keys, values = k_ref[k_at, lane_window(k_col, pair)], k_ref[k_at, lane_window(v_col, pair)]
        scores = times_transposed(keys, q) * scale
        scores = jnp.where(allowed, scores, -1000000000.0)
        probs = jnp.exp(scores - lse[pl.ds(page * (D // HD // 2) + pair, 1), :])
        g_probs = times_transposed(values, g)
        inner = jnp.sum(probs * g_probs, axis=0, keepdims=True)
        g_scores = (probs * (g_probs - inner)).astype(bf16)
        g_values = times(probs.astype(bf16), g)
        g_keys = times(g_scores, q) * scale
        g_q = transposed_times(g_scores, keys)
        g_q = jnp.where(lane < HD, g_q[:length], g_q[length:]) * scale
        q_ref[q_at, lane_window(q_col, pair)] = g_q.astype(bf16)
        k_ref[k_at, lane_window(k_col, pair)] = g_keys.astype(bf16)
        k_ref[k_at, lane_window(v_col, pair)] = g_values.astype(bf16)

    def cross_attention(page):
        need("cq", "kv")
        place = lax.broadcasted_iota(jnp.int32, (slots, 2 * length), 0)
        allowed = place < counts[page]

        def body(pair, carry):
            attention(page, pair, cq, 0, kv, page * slots, slots, 0, D, lse_cross, allowed)
            return carry

        lax.fori_loop(0, D // (2 * HD), body, 0, unroll=2)

    def self_attention(page):
        need("qkv")
        allowed = causal(length, lengths[page])

        def body(pair, carry):
            attention(page, pair, qkv, 0, qkv, page * length, length, D, 2 * D, lse_self, allowed)
            return carry

        lax.fori_loop(0, D // (2 * HD), body, 0)

    def norm_back(value_ref, gain_row, put):
        gain = gains[pl.ds(gain_row, 1), :]

        def body(k, total_):
            at = pl.ds(k * 32, 32)
            value = value_ref[at].astype(f32)
            centred = value - jnp.mean(value, axis=-1, keepdims=True)
            spread = jnp.mean(centred * centred, axis=-1, keepdims=True)
            row_scale = lax.rsqrt(spread + EPS)
            unit = centred * row_scale
            grad = g_norm[at]
            grad_unit = grad * gain
            inner = jnp.mean(grad_unit * unit, axis=-1, keepdims=True)
            put(at, row_scale * (grad_unit - jnp.mean(grad_unit, axis=-1, keepdims=True) - unit * inner))
            return total_ + jnp.sum(grad * unit, axis=0, keepdims=True)

        summed = lax.fori_loop(0, value_ref.shape[0] // 32, body, jnp.zeros((1, D), f32))
        gain_sum[0, pl.ds(gain_row, 1), :] = summed

    def spread(terms):
        def body(k, carry):
            at = pl.ds(pl.multiple_of(k * 2 * BLOCK, BLOCK), 2 * BLOCK)
            value = None
            for left, left_col, right, right_col in terms:
                term = times_transposed(
                    left[:, pl.ds(left_col, D)], right[at, pl.ds(right_col, D)]
                )
                value = term if value is None else value + term
            g_norm[:, at] = value
            return carry

        lax.fori_loop(0, D // (2 * BLOCK), body, 0)

    def third_norm():
        need("pre", "out", "cross")
        need_all("expand")
        spread([(pre, 0, w_a, 0), (pre, D, w_a, D), (pre, 2 * D, w_b, 0), (pre, 3 * D, w_b, D)])

        def put(at, value):
            value = out_grad[at].astype(f32) + value
            cross[at] = value
            branch[at] = value.astype(bf16)

        norm_back(cross, 2, put)
        weights("qo", ("qo", 1, w_a, 1), ("qo", 0, w_a, 0))
        weights("self", ("self", 3, w_b, 0), ("self", 0, w_b, 1))

    def second_norm():
        need("self")
        fetch("x", x_in, third, 14)
        spread([(cq, 0, w_a, 0)])

        def put(at, value):
            value = cross[at] + value
            cross[at] = value
            branch[at] = value.astype(bf16)

        norm_back(after_self, 1, put)
        weights("pair", ("self", 1, w_a, 0), ("self", 2, w_a, 1))

    def first_norm():
        need("x")
        need_all("pair")
        spread([(qkv, 0, w_b, D), (qkv, D, w_a, 0), (qkv, 2 * D, w_a, D)])

        def put(at, value):
            input_out[at] = cross[at] + value

        norm_back(third, 0, put)
        weights("kv", ("kv", 0, w_b, 0), ("kv", 1, w_b, 1))

    def memory_grad(page, part):
        need_all("kv")
        slot = part % 2
        need(("stage", slot))
        top = part * span
        height = min(slots - top, span)
        live = min(memory_rows - top, height)
        at = pl.ds(page * slots + top, height)

        def body(k, carry):
            col = pl.multiple_of(k * BLOCK, BLOCK)
            value = times_transposed(kv[at, :], w_b[pl.ds(col, BLOCK), :])
            for j in range(BLOCK // 128):
                stage[slot, pl.ds(k * (BLOCK // 128) + j, live, 8), :] = value[:live, j * 128 : j * 128 + 128]
            return carry

        lax.fori_loop(0, D // BLOCK, body, 0)
        fetch(
            ("stage", slot),
            stage.at[slot, pl.ds(0, live * 8)],
            memory_out.at[pl.ds((page * memory_rows + top) * 8, live * 8)],
            19 + slot,
        )

    span = -(-slots // 32) * 16
    memory_rows = memory_out.shape[0] // 8 // pages
    gain_sum[0] = jnp.zeros(gain_sum.shape[1:], f32)
    plan = Plan()
    for i in range(total):
        t = ticks[i]
        plan.add(t - 2, 0, stage0, i)
        if i in tall:
            plan.add(t, 1, tall1, i)
            for d in range(depth - 1, 0, -1):
                plan.add(t + TALL_STEP * (depth - 1 - d), 5, tall_z, i, d)
            t += TALL_STEP * (depth - 1)
            plan.add(t, 5, tall_plane, i)
            plan.add(t + 1, 5, tall_half, i)
            plan.add(t + 2, 5, tall_out, i)
        else:
            plan.add(t, 1, stage1, i)
            plan.add(t + 1, 2, stage2, i)
            plan.add(t + 2, 3, stage3, i)
            plan.add(t + 3, 4, stage4, i)

    def cross_in_grad():
        need_all("qo")
        context_grad(w_a, D)

    def self_in_grad():
        need_all("self")
        context_grad(w_b, 0)

    plan.add(0, 9, third_norm)
    plan.add(1, 9, cross_in_grad)
    for page in range(pages):
        plan.add(1 + page, 10, cross_attention, page)
    turn = ticks[OUT_CHUNK]
    plan.add(turn, 8, second_norm)
    plan.add(turn, 9, self_in_grad)
    for page in range(pages):
        plan.add(turn + page, 11, self_attention, page)
    plan.add(turn + pages, 9, first_norm)
    for page in range(pages):
        for part in range(2):
            plan.add(turn + pages + 1 + 2 * part, 9, memory_grad, page, part)
    for h in range(len(moves)):
        plan.add(len(flat) - 4 + h, 7, gain_step, h)
    plan.run()
    for i in range(total):
        if i >= total - SPARE:
            copies[i, 0][0].wait_send()
        if i in tall:
            for copy in copies[i, 1] + copies[i, 2]:
                copy.wait_send()
            for up in (True, False):
                for d in range(1, depth):

                    @pl.when(level(up) + d < depth)
                    def _():
                        pass_on(i, up, d).wait_send()

        elif flat[i] >= len(flat) - RING:
            for stage in (1, 2, 3):
                for copy in copies[i, stage]:
                    copy.wait_send()
    for h in range(len(moves)):
        for copy in copies["gain", h]:
            copy.wait_send()
    need(*list(loads))


def backward(big, small, shapes):
    dp, fsdp = lax.axis_size("dp"), lax.axis_size("fsdp")
    n = dp // CORES
    depth = fsdp // n
    devices = dp * fsdp
    rows = WIDTH // devices
    pages, length, slots, live = shapes
    tokens = pages * length
    D = WIDTH
    high = len(BACK_TALL)
    t = sum(k * m for k, m in ((big[0].shape[1], D), (D, big[1].shape[1]), (D, 8 * D))) // (D * D) - high
    dma = pltpu.SemaphoreType.DMA
    hops = 2 * n + depth - 2
    outs = [(big[0].shape[1], D), (D, big[1].shape[1]), (D, D), (D, D), (D, 2 * D), (D, D), (D, 3 * D)]
    f32 = jnp.float32

    def scratch(*lead):
        return pltpu.VMEM(lead + (rows, WIDTH), jnp.bfloat16)

    def like(value):
        return pltpu.VMEM(value.shape, value.dtype)

    hbm = pl.BlockSpec(memory_space=pltpu.HBM)
    vmem = pl.BlockSpec(memory_space=pltpu.VMEM)
    smem = pl.BlockSpec(memory_space=pltpu.SMEM)
    return pl.pallas_call(
        functools.partial(back_kernel, (pages, length, slots)),
        out_shape=[jax.ShapeDtypeStruct((k // devices, m), f32) for k, m in outs]
        + [
            jax.ShapeDtypeStruct((8, D), f32),
            jax.ShapeDtypeStruct((tokens, D), f32),
            jax.ShapeDtypeStruct((pages * live * D // 128, 128), f32),
        ],
        in_specs=[hbm] * len(big) + [smem, smem] + [vmem] * 3,
        out_specs=[vmem] * (len(outs) + 2) + [hbm],
        scratch_shapes=[like(v) for v in big[:14]]
        + [pltpu.VMEM((D, 2 * D), jnp.bfloat16)] * 2
        + [pltpu.VMEM((tokens, D), jnp.bfloat16)] * 2
        + [
            pltpu.VMEM((2, -(-slots // 32) * 16 * 8, 128), f32),
            pltpu.VMEM((tokens, D), f32),
            scratch(SPARE, n, depth, n),
            scratch(RING, n, depth, n),
            scratch(RING, n, n, depth),
            scratch(RING, n - 1, n, depth),
            scratch(RING, n, depth),
            scratch(t, n - 1, depth),
            scratch(RING, depth),
            scratch(t, depth - 1),
            pltpu.VMEM((4, 8, D), f32),
            pltpu.VMEM((hops, 8, D), f32),
            scratch(high, depth, n, n),
            scratch(high, depth + 1, n, n),
            scratch(high, (n - 1) * n),
            scratch(high, n),
            scratch(high, n - 1),
            dma((21,)),
            dma((SPARE,)),
            dma((RING,)),
            dma((RING, n - 1)),
            dma((RING, n - 1)),
            dma((RING, n - 1)),
            dma((t, n - 1)),
            dma((RING, depth - 1)),
            dma((t, depth - 1)),
            dma((hops,)),
            dma((hops,)),
            pltpu.SemaphoreType.REGULAR,
            pltpu.SemaphoreType.REGULAR((n - 1,)),
            dma((high, depth)),
            dma((high, depth + 1)),
            dma((high, (n - 1) * n)),
            dma((high, (n - 1) * n)),
            dma((high, n - 1)),
            dma((high, n - 1)),
        ],
        compiler_params=pltpu.CompilerParams(
            collective_id=1, has_side_effects=True, vmem_limit_bytes=67043328
        ),
    )(*big, *small)


def hand_kernel(slabs, count, made, *refs):
    ins, gains = refs[:count], refs[count]
    outs, gain_outs = refs[count + 1 : count + 1 + made], refs[count + 1 + made : count + 4 + made]
    buffers = refs[count + 4 + made : 2 * count + 4 + made]
    loaded, stored = refs[2 * count + 4 + made :]
    loads, stores = [], []
    for k, (m, rows, pieces) in enumerate(slabs):
        at = pl.ds(*rows)
        loads.append(pltpu.make_async_copy(ins[m].at[at], buffers[m].at[at], loaded.at[k]))
        loads[-1].start()
    entries = gain_outs[0].shape[-1]
    me = lax.axis_index("dp") * lax.axis_size("fsdp") + lax.axis_index("fsdp")
    turned = pltpu.roll(gains[...], lax.rem(gains.shape[1] - me * entries, gains.shape[1]), 1)
    for k, gain_out in enumerate(gain_outs):
        gain_out[...] = turned[k : k + 1, :entries]
    for load, (m, rows, pieces) in zip(loads, slabs):
        load.wait()
        at = pl.ds(*rows)
        for o, col in pieces:
            src = buffers[m].at[at, pl.ds(col, outs[o].shape[1])]
            stores.append(pltpu.make_async_copy(src, outs[o].at[at], stored.at[len(stores)]))
            stores[-1].start()
    for store in stores:
        store.wait()


def hand_over(arrays, gains):
    devices = lax.axis_size("dp") * lax.axis_size("fsdp")
    entries = gains.shape[1] // devices
    slabs, outs = [], []
    for m, (value, parts) in enumerate(arrays):
        cols = value.shape[1] // parts
        pieces = [(len(outs) + k, k * cols) for k in range(parts)]
        outs += [jax.ShapeDtypeStruct((value.shape[0], cols), value.dtype)] * parts
        cuts = 4 if value.shape[0] % 64 == 0 and value.size >= 1 << 20 else 1
        rows = value.shape[0] // cuts
        slabs += [(m, (k * rows, rows), pieces) for k in range(cuts)]
    hbm = pl.BlockSpec(memory_space=pltpu.HBM)
    vmem = pl.BlockSpec(memory_space=pltpu.VMEM)
    dma = pltpu.SemaphoreType.DMA
    found = pl.pallas_call(
        functools.partial(hand_kernel, slabs, len(arrays), len(outs)),
        out_shape=outs + [jax.ShapeDtypeStruct((1, entries), gains.dtype)] * 3,
        in_specs=[hbm] * len(arrays) + [vmem],
        out_specs=[hbm] * len(outs) + [vmem] * 3,
        scratch_shapes=[pltpu.VMEM(v.shape, v.dtype) for v, _ in arrays]
        + [dma((len(slabs),)), dma((sum(len(pieces) for _, _, pieces in slabs),))],
        compiler_params=pltpu.CompilerParams(vmem_limit_bytes=67043328),
    )(*[v for v, _ in arrays], gains)
    return found[:-3], [v.reshape(-1) for v in found[-3:]]


def per_device(
    hidden_in,
    memory,
    cotangent,
    lengths,
    memory_count,
    causal_gain,
    causal_query,
    causal_key,
    causal_value,
    causal_output,
    source_gain,
    source_query,
    source_key,
    source_value,
    source_output,
    dense_gain,
    dense_expand,
    dense_reduce,
):
    pages, _, rows, width = hidden_in.shape
    slots = memory.shape[2]
    pad = -slots % 16
    source = jnp.pad(memory[:, 0], ((0, 0), (0, pad), (0, 0)))

    def flat(value):
        return value.reshape(pages * value.shape[1], value.shape[2])

    gains = jnp.stack([causal_gain, source_gain, dense_gain], axis=1)
    gains = jnp.pad(gains, ((0, 0), (0, 125)))
    sources = [
        causal_query,
        causal_key,
        causal_value,
        causal_output,
        source_key,
        source_value,
        source_query,
        source_output,
        dense_expand,
        dense_reduce,
        gains,
    ]
    names = [("gain", 0)]
    pieces = [(10, 0, 0, 0, False)]
    for first, count, name in ((4, 2, "kv"), (0, 4, "self"), (6, 2, "qo")):
        for k in range(count):
            pieces.append((first + k, 0, 0, len(names), False))
            names.append((name, k))
    for k in range(4):
        pieces.append((9, k * causal_query.shape[0], 0, len(names), k < 2))
    names.append(("reduce", 0))
    for k in range(4):
        pieces.append((8, 0, k * width, len(names), k == 3))
        names.append(("expand", k))
    tokens = flat(hidden_in[:, 0])
    branch = flat(cotangent[:, 0])
    memory_rows = flat(source)
    page_length, page_count = lengths[:, 0], memory_count[:, 0]
    weights, saved, small = front(
        sources,
        pieces,
        names,
        [tokens, branch, memory_rows, page_count, page_length],
        (pages, rows, slots + pad),
    )
    result, hidden, pre, third, after_cross, cctx, second, cq, kv, after_self, ctx, first, qkv = saved
    gain_rows, lse_cross, lse_self = small
    big = [
        hidden,
        pre,
        third,
        branch,
        after_cross,
        cctx,
        second,
        cq,
        kv,
        memory_rows,
        after_self,
        ctx,
        first,
        qkv,
        tokens,
    ]
    place = {name: weight for name, weight in zip(names, weights)}
    big += [place[name, k] for name, count in KEPT for k in range(count)]
    small = [page_count, page_length, gain_rows, lse_cross, lse_self]
    (
        grad_reduce,
        grad_expand,
        grad_source_output,
        grad_source_query,
        grad_source_both,
        grad_causal_output,
        grad_causal,
        grad_gains,
        grad_inputs,
        grad_memory,
    ) = backward(big, small, (pages, rows, slots + pad, slots))
    (
        grad_memory,
        grad_inputs,
        result,
        grad_reduce,
        grad_expand,
        *grad_causal,
        grad_source_key,
        grad_source_value,
        grad_source_query,
        grad_source_output,
        grad_causal_output,
    ), grad_gains = hand_over(
        [
            (grad_memory, 1),
            (grad_inputs, 1),
            (result, 1),
            (grad_reduce, 1),
            (grad_expand, 1),
            (grad_causal, 3),
            (grad_source_both, 2),
            (grad_source_query, 1),
            (grad_source_output, 1),
            (grad_causal_output, 1),
        ],
        grad_gains,
    )
    return (
        result.reshape(hidden_in.shape),
        grad_inputs.reshape(hidden_in.shape),
        grad_memory.reshape(memory.shape),
        grad_gains[0],
        *grad_causal,
        grad_causal_output,
        grad_gains[1],
        grad_source_query,
        grad_source_key,
        grad_source_value,
        grad_source_output,
        grad_gains[2],
        grad_expand,
        grad_reduce,
    )


def solution(mesh):
    pages = P(None, AXES, None, None)
    counts = P(None, AXES)
    gain = P(AXES)
    weight = P(AXES, None)
    return jax.shard_map(
        per_device,
        mesh=mesh,
        in_specs=(pages, pages, pages, counts, counts)
        + (gain, weight, weight, weight, weight)
        + (gain, weight, weight, weight, weight)
        + (gain, weight, weight),
        out_specs=(pages, pages, pages)
        + (gain, weight, weight, weight, weight)
        + (gain, weight, weight, weight, weight)
        + (gain, weight, weight),
        check_vma=False,
    )
```
